32 devices in a mesh: dp: 4 (over y, x), fsdp: 8 (over z, core).
Axes of the slice: x: 2, y: 2, z: 4, core: 2. Of those that a mesh axis runs over, the one named last changes fastest.
Arguments:
- tokens: bfloat16 [32768, 768], P(('dp', 'fsdp')), may hold values from -6 to 6
- cotangent: bfloat16 [32768, 768], P(('dp', 'fsdp')), may hold values from -6 to 6
- tie_map: int32 [12], replicated, may hold values from 0 to 3, as said below
- first_length: int32 [32], P(('dp', 'fsdp')), may hold values from 512 to 1024, as said below
- gain_attend: bfloat16 [4, 768], P(None, ('dp', 'fsdp')), may hold values from 0.5 to 1.5
- shift_attend: bfloat16 [4, 768], P(None, ('dp', 'fsdp')), may hold values from -3 to 3
- heads_weight: bfloat16 [4, 768, 2304], P(None, ('dp', 'fsdp')), may hold values from -0.21875 to 0.21875
- query_bias: bfloat16 [4, 768], P(None, ('dp', 'fsdp')), may hold values from -3 to 3
- value_bias: bfloat16 [4, 768], P(None, ('dp', 'fsdp')), may hold values from -3 to 3
- mixing_weight: bfloat16 [4, 768, 768], P(None, ('dp', 'fsdp')), may hold values from -0.625 to 0.625
- mixing_bias: bfloat16 [4, 768], P(None, ('dp', 'fsdp')), may hold values from -3 to 3
- gain_feed: bfloat16 [4, 768], P(None, ('dp', 'fsdp')), may hold values from 0.5 to 1.5
- shift_feed: bfloat16 [4, 768], P(None, ('dp', 'fsdp')), may hold values from -3 to 3
- expand_weight: bfloat16 [4, 768, 3072], P(None, ('dp', 'fsdp')), may hold values from -0.21875 to 0.21875
- expand_bias: bfloat16 [4, 3072], P(None, ('dp', 'fsdp')), may hold values from -3 to 3
- shrink_weight: bfloat16 [4, 3072, 768], P(None, ('dp', 'fsdp')), may hold values from -0.109375 to 0.109375
- shrink_bias: bfloat16 [4, 768], P(None, ('dp', 'fsdp')), may hold values from -3 to 3
Outputs:
- block_output: bfloat16 [32768, 768], P(('dp', 'fsdp'))
- tokens_grad: bfloat16 [32768, 768], P(('dp', 'fsdp'))
- dgain_attend: float32 [4, 768], P(None, ('dp', 'fsdp'))
- dshift_attend: float32 [4, 768], P(None, ('dp', 'fsdp'))
- dheads_weight: float32 [4, 768, 2304], P(None, ('dp', 'fsdp'))
- dquery_bias: float32 [4, 768], P(None, ('dp', 'fsdp'))
- dvalue_bias: float32 [4, 768], P(None, ('dp', 'fsdp'))
- dmixing_weight: float32 [4, 768, 768], P(None, ('dp', 'fsdp'))
- dmixing_bias: float32 [4, 768], P(None, ('dp', 'fsdp'))
- dgain_feed: float32 [4, 768], P(None, ('dp', 'fsdp'))
- dshift_feed: float32 [4, 768], P(None, ('dp', 'fsdp'))
- dexpand_weight: float32 [4, 768, 3072], P(None, ('dp', 'fsdp'))
- dexpand_bias: float32 [4, 3072], P(None, ('dp', 'fsdp'))
- dshrink_weight: float32 [4, 3072, 768], P(None, ('dp', 'fsdp'))
- dshrink_bias: float32 [4, 768], P(None, ('dp', 'fsdp'))
The draws below stay inside these ranges and needn't reach their ends.
Inputs may be any that keep to these rules, and one draw needn't show every extreme that they name: `tie_map`: the first 2 entries name distinct sources; the others name sources too. `first_length`: each entry is 512 or 1024; both occur in every draw.
All inputs are finite; a program needn't handle non-finite values.
Results may differ from the reference program's by a relative error of at most 0.013.
Values may be sent and summed in bfloat16 or wider, within the bound.
A program may use at most 256 MiB of HBM per device.

```python
import jax
import jax.numpy as jnp
from jax import lax

D = 768
HEADS = 12
HD = 64
FF = 3072
LONG = 1024
LAYERS = 2
UNIQUE = 4
SLOTS = 12
ROWS = 32
TOKENS = 32768


def draw_tie_map(key, part):
    filler = jax.random.randint(key, (SLOTS,), 0, UNIQUE).astype(jnp.int32)
    leading = jax.random.permutation(jax.random.fold_in(key, 7), UNIQUE).astype(jnp.int32)
    return jnp.concatenate([leading[:LAYERS], filler[LAYERS:]]).astype(jnp.int32)


def draw_first_length(key, part):
    picks = jax.random.randint(key, (ROWS,), 0, 2).astype(jnp.int32)
    lengths = LONG // 2 + picks * (LONG - LONG // 2)
    return lengths.at[0].set(LONG).at[1].set(LONG // 2).astype(jnp.int32)


def steps_of(own_key, shape, cuts, smallest, largest):
    level = 1.0
    for axis_at, shards_of in cuts:
        steps = jax.random.uniform(jax.random.fold_in(jax.random.fold_in(own_key, 6), axis_at), (shards_of,), jnp.float32, smallest / len(cuts), largest / len(cuts))
        level = level * jnp.repeat(jnp.exp(steps), shape[axis_at] // shards_of).reshape((-1,) + (1,) * (len(shape) - 1 - axis_at))
    return level


def normal_values(stream_key, extent, width, bound, cuts=(), held_as=jnp.bfloat16):
    entries = width * jax.random.normal(stream_key, extent, jnp.float32)
    if cuts:
        entries = entries * steps_of(stream_key, extent, cuts, -0.22, 0.18)
    return jnp.clip(entries, -bound, bound).astype(held_as)


def setup_inputs(seed: int = 0) -> dict:
    arg_keys = jax.random.split(jax.random.key(seed), 18)
    return {
        "tokens": normal_values(arg_keys[0], (TOKENS, D), 1.0, 6.0, ((0, 32),)),
        "cotangent": normal_values(arg_keys[1], (TOKENS, D), 1.0, 6.0, ((0, 32),)),
        "tie_map": draw_tie_map(jax.random.fold_in(arg_keys[17], 71), 0),
        "first_length": draw_first_length(jax.random.fold_in(arg_keys[17], 71), 0),
        "gain_attend": jnp.clip(1.0 + 0.1 * jax.random.normal(arg_keys[4], (UNIQUE, D), jnp.float32), 0.5, 1.5).astype(jnp.bfloat16),
        "shift_attend": normal_values(arg_keys[5], (UNIQUE, D), 0.3, 3.0, ((1, 32),)),
        "heads_weight": normal_values(arg_keys[6], (UNIQUE, D, 3 * D), D ** -0.5, 0.21875, ((1, 32),)),
        "query_bias": normal_values(arg_keys[7], (UNIQUE, D), 0.3, 3.0, ((1, 32),)),
        "value_bias": normal_values(arg_keys[8], (UNIQUE, D), 0.5, 3.0, ((1, 32),)),
        "mixing_weight": normal_values(arg_keys[9], (UNIQUE, D, D), (D // 8) ** -0.5, 0.625, ((1, 32),)),
        "mixing_bias": normal_values(arg_keys[10], (UNIQUE, D), 0.3, 3.0, ((1, 32),)),
        "gain_feed": jnp.clip(1.0 + 0.1 * jax.random.normal(arg_keys[11], (UNIQUE, D), jnp.float32), 0.5, 1.5).astype(jnp.bfloat16),
        "shift_feed": normal_values(arg_keys[12], (UNIQUE, D), 0.3, 3.0, ((1, 32),)),
        "expand_weight": normal_values(arg_keys[13], (UNIQUE, D, FF), D ** -0.5, 0.21875, ((1, 32),)),
        "expand_bias": normal_values(arg_keys[14], (UNIQUE, FF), 0.5, 3.0, ((1, 32),)),
        "shrink_weight": normal_values(arg_keys[15], (UNIQUE, FF, D), FF ** -0.5, 0.109375, ((1, 32),)),
        "shrink_bias": normal_values(arg_keys[16], (UNIQUE, D), 0.3, 3.0, ((1, 32),)),
    }


@jax.custom_vjp
def low(v):
    return lax.optimization_barrier(v.astype(jnp.bfloat16)).astype(jnp.float32)

@jax.custom_vjp
def low_back(v):
    return v

def low_keep(v):
    return (low(v), None)

def low_pass(kept, grad):
    return (grad,)

def back_keep(v):
    return (v, None)

def back_low(kept, grad):
    return (low(grad),)
low.defvjp(low_keep, low_pass)
low_back.defvjp(back_keep, back_low)

def layer_norm(values, gain, shift):
    centre = values - lax.optimization_barrier(jnp.mean(values, axis=-1, keepdims=True))
    spread = lax.optimization_barrier(jnp.mean(centre * centre, axis=-1, keepdims=True))
    return centre * lax.rsqrt(spread + 1e-05) * gain + shift

def attend_row(packed):
    shaped, first_len = packed
    length = shaped.shape[0]
    queries = shaped[:, 0]
    keys = shaped[:, 1]
    values = shaped[:, 2]
    scores = jnp.einsum('qhd,khd->hqk', queries, keys, precision=lax.Precision.HIGHEST) * HD ** (-0.5)
    scores = low_back(scores)
    place = lax.iota(jnp.int32, length)
    second = place >= first_len
    allowed = (place[None, :] <= place[:, None]) & (second[None, :] == second[:, None])
    scores = jnp.where(allowed[None], scores, -1000000000.0)
    probs = low(jax.nn.softmax(scores, axis=-1))
    mixed = jnp.einsum('hqk,khd->qhd', probs, values, precision=lax.Precision.HIGHEST)
    return mixed.reshape(length, HEADS * HD)

def one_use(hidden, params, first_length):
    gain_a, shift_a, heads_w, query_b, value_b, mix_w, mix_b, gain_f, shift_f, expand_w, expand_b, shrink_w, shrink_b = params
    normed = low(layer_norm(hidden, gain_a, shift_a))
    bias = jnp.concatenate([query_b, jnp.zeros_like(query_b), value_b])
    projected = low(low_back(jnp.dot(normed, heads_w, precision=lax.Precision.HIGHEST) + bias))
    row_count = first_length.shape[0]
    length = hidden.shape[0] // row_count
    shaped = projected.reshape(row_count, length, 3, HEADS, HD)
    attended = lax.map(jax.checkpoint(attend_row), (shaped, first_length))
    attended = low(low_back(attended.reshape(-1, HEADS * HD)))
    middle = hidden + low_back(jnp.dot(attended, mix_w, precision=lax.Precision.HIGHEST) + mix_b)
    normed_two = low(layer_norm(middle, gain_f, shift_f))
    expanded = low_back(jnp.dot(normed_two, expand_w, precision=lax.Precision.HIGHEST) + expand_b)
    activated = low(jax.nn.gelu(expanded, approximate=True))
    return middle + low_back(jnp.dot(activated, shrink_w, precision=lax.Precision.HIGHEST) + shrink_b)

def reference(tokens, cotangent, tie_map, first_length, gain_attend, shift_attend, heads_weight, query_bias, value_bias, mixing_weight, mixing_bias, gain_feed, shift_feed, expand_weight, expand_bias, shrink_weight, shrink_bias):
    stacks = tuple((item.astype(jnp.float32) for item in (gain_attend, shift_attend, heads_weight, query_bias, value_bias, mixing_weight, mixing_bias, gain_feed, shift_feed, expand_weight, expand_bias, shrink_weight, shrink_bias)))

    def forward(inputs, weights):
        hidden = inputs
        for layer_index in range(LAYERS):
            source = tie_map[layer_index]
            params = tuple((stack[source] for stack in weights))
            hidden = one_use(hidden, params, first_length)
        return hidden
    result, pullback = jax.vjp(forward, tokens.astype(jnp.float32), stacks)
    input_grad, grads = pullback(cotangent.astype(jnp.float32))
    return (result.astype(jnp.bfloat16), input_grad.astype(jnp.bfloat16), grads[0], grads[1], grads[2], grads[3], grads[4], grads[5], grads[6], grads[7], grads[8], grads[9], grads[10], grads[11], grads[12])
```

```python
import functools

import jax
import jax.numpy as jnp
from jax import lax
from jax.experimental import pallas as pl
from jax.experimental.pallas import tpu as pltpu
from jax.sharding import PartitionSpec as P

LAYERS = 2
UNIQUE = 4
F32 = jnp.float32
BF = jnp.bfloat16
AX = ("dp", "fsdp")
LANES = 128
EPS = 1e-05

NEG=-1e9
def nt(a,b): return lax.dot_general(a,b,(((1,),(1,)),((),())),preferred_element_type=F32)
def nn(a,b): return lax.dot_general(a,b,(((1,),(0,)),((),())),preferred_element_type=F32)
def halves(x):
    lane=lax.broadcasted_iota(jnp.int32,x.shape,1)
    z=jnp.zeros_like(x)
    return jnp.where(lane<64,x,z), jnp.where(lane<64,z,x)

def fwd_kernel(fl_ref,q_ref,k_ref,v_ref,o_ref,lse_ref,*,bq):
    L=q_ref.shape[0]; half=L//2
    second=fl_ref[pl.program_id(0)]<L
    shut=jnp.where(second,F32(1e9),F32(0.))
    q=q_ref[...]*BF(0.125); k=k_ref[...]; vT=v_ref[...].T
    sub=lax.broadcasted_iota(jnp.int32,vT.shape,0)
    zero=jnp.zeros_like(vT)
    vTs=(jnp.where(sub<64,vT,zero),jnp.where(sub<64,zero,vT))
    qs=halves(q)
    tri=lax.broadcasted_iota(jnp.int32,(bq,bq),0)<=lax.broadcasted_iota(jnp.int32,(bq,bq),1)
    for j in range(L//bq):
        lo=j*bq; hi=lo+bq
        acc=jnp.zeros((128,bq),F32)
        for h in range(2):
            qh=qs[h][lo:hi]
            s=nt(k[:hi],qh)
            parts=[]
            if lo>0 : parts.append((0,min(lo,half),s[:min(lo,half)]))
            if lo>half: parts.append((half,lo,s[half:lo]))
            diag=jnp.where(tri,s[lo:],NEG)
            m=jnp.max(diag,axis=0,keepdims=True)
            for a,b,t in parts:
                mt=jnp.max(t,axis=0,keepdims=True)
                if lo>=half and a==0: mt=mt-shut
                m=jnp.maximum(m,mt)
            ps=[]; l=0.
            for a,b,t in parts+[(lo,hi,diag)]:
                mm=m+shut if (lo>=half and a==0) else m
                p=jnp.exp(t-mm)
                l=l+jnp.sum(p,axis=0,keepdims=True)
                ps.append(p.astype(BF))
            p=jnp.concatenate(ps,axis=0) if len(ps)>1 else ps[0]
            oh=nn(vTs[h][:,:hi],p)
            acc=acc+oh*(1.0/l)
            lse_ref[0,h:h+1,lo:hi]=m+jnp.log(l)
        o_ref[lo:hi,:]=acc.T.astype(BF)

def attend_fwd(qkv,fl,bq=256):
    N,C=qkv.shape; R=fl.shape[0]; L=N//R; D=C//3; G=D//128
    return pl.pallas_call(functools.partial(fwd_kernel,bq=bq),
        grid_spec=pltpu.PrefetchScalarGridSpec(num_scalar_prefetch=1,grid=(R,G),
          in_specs=[pl.BlockSpec((L,128),lambda r,g,fl:(r,g)),
                    pl.BlockSpec((L,128),lambda r,g,fl:(r,G+g)),
                    pl.BlockSpec((L,128),lambda r,g,fl:(r,2*G+g))],
          out_specs=[pl.BlockSpec((L,128),lambda r,g,fl:(r,g)),
                     pl.BlockSpec((1,2,L),lambda r,g,fl:(r*G+g,0,0))]),
        out_shape=[jax.ShapeDtypeStruct((N,D),BF),jax.ShapeDtypeStruct((R*G,2,L),F32)],
        compiler_params=pltpu.CompilerParams(vmem_limit_bytes=48<<20),
        cost_estimate=pl.CostEstimate(flops=2*2*R*L*L*D*2,bytes_accessed=N*D*8,transcendentals=R*L*L*12//2),
        name="attend_fwd")(fl,qkv,qkv,qkv)

def bwd_kernel(fl_ref,q_ref,k_ref,v_ref,do_ref,lse_ref,dq_ref,dk_ref,dv_ref,dk_acc,dv_acc,*,bq):
    L=q_ref.shape[0]; half=L//2
    second=fl_ref[pl.program_id(0)]<L
    shut=jnp.where(second,F32(1e9),F32(0.))
    q=q_ref[...]*BF(0.125); k=k_ref[...]; v=v_ref[...]; do=do_ref[...]
    kT=k.T
    sub=lax.broadcasted_iota(jnp.int32,kT.shape,0); zero=jnp.zeros_like(kT)
    kTs=(jnp.where(sub<64,kT,zero),jnp.where(sub<64,zero,kT))
    qs=halves(q); dos=halves(do)
    tri=lax.broadcasted_iota(jnp.int32,(bq,bq),0)<=lax.broadcasted_iota(jnp.int32,(bq,bq),1)
    nb=L//bq
    for j in reversed(range(nb)):
        lo=j*bq; hi=lo+bq
        dqT=jnp.zeros((128,bq),F32)
        dkp=None; dvp=None
        for h in range(2):
            qh=qs[h][lo:hi]; doh=dos[h][lo:hi]
            lse=lse_ref[0,h:h+1,lo:hi]
            s=nt(k[:hi],qh)
            dp=nt(v[:hi],doh)
            ps=[];
            cuts=[]
            if lo>0: cuts.append((0,min(lo,half)))
            if lo>half: cuts.append((half,lo))
            cuts.append((lo,hi))
            for a,b in cuts:
                ll=lse+shut if (lo>=half and b<=half) else lse
                t=s[a:b]-ll
                if a==lo: t=jnp.where(tri,t,NEG)
                ps.append(jnp.exp(t))
            p=jnp.concatenate(ps,axis=0) if len(ps)>1 else ps[0]
            delta=jnp.sum(p*dp,axis=0,keepdims=True)
            ds=(p*(dp-delta)).astype(BF)
            pb=p.astype(BF)
            dv_=nn(pb,doh); dk_=nn(ds,qh)
            dvp=dv_ if dvp is None else dvp+dv_
            dkp=dk_ if dkp is None else dkp+dk_
            dqT=dqT+nn(kTs[h][:,:hi],ds)
        if j==nb-1:
            dk_acc[...]=dkp; dv_acc[...]=dvp
        else:
            dk_acc[:hi]+=dkp; dv_acc[:hi]+=dvp
        dq_ref[lo:hi,:]=(dqT.T*0.125).astype(BF)
    dk_ref[...]=dk_acc[...].astype(BF); dv_ref[...]=dv_acc[...].astype(BF)

def attend_bwd(qkv,do,lse,fl,bq=256):
    N,C=qkv.shape; R=fl.shape[0]; L=N//R; D=C//3; G=D//128
    blk=lambda off: pl.BlockSpec((L,128),lambda r,g,fl:(r,off*G+g))
    return pl.pallas_call(functools.partial(bwd_kernel,bq=bq),
        grid_spec=pltpu.PrefetchScalarGridSpec(num_scalar_prefetch=1,grid=(R,G),
          in_specs=[blk(0),blk(1),blk(2),blk(0),pl.BlockSpec((1,2,L),lambda r,g,fl:(r*G+g,0,0))],
          out_specs=[blk(0),blk(0),blk(0)],
          scratch_shapes=[pltpu.VMEM((L,128),F32),pltpu.VMEM((L,128),F32)]),
        out_shape=[jax.ShapeDtypeStruct((N,D),BF)]*3,
        compiler_params=pltpu.CompilerParams(vmem_limit_bytes=48<<20),
        cost_estimate=pl.CostEstimate(flops=5*2*R*L*L*D*2,bytes_accessed=N*D*16,transcendentals=R*L*L*12//2),
        name="attend_bwd")(fl,qkv,qkv,qkv,do,lse)


def swap(x, mask):
    count = lax.axis_size(AX)
    return lax.ppermute(x, AX, [(i, i ^ mask) for i in range(count)])


def block_mesh():
    return lax.axis_size("dp") == 4 and lax.axis_size("fsdp") == 8


CORE, ZLO, ZHI, XBIT, YBIT = 1, 2, 4, 8, 16


def place_column(own, others):
    z = lax.rem(lax.axis_index("fsdp") // 2, 4)
    parts = [own] + others
    rows = []
    for k in range(4):
        pick = parts[k]
        for j in range(1, 4):
            pick = jnp.where(z == j, parts[k ^ j], pick)
        rows.append(pick)
    return jnp.stack(rows)


def assemble_kernel(*refs, cuts):
    n = 8
    ins = refs[:n]
    outs = refs[n : n + len(cuts)]
    sem = refs[-1]
    dp = lax.axis_index("dp")
    core = lax.rem(lax.axis_index("fsdp"), 2)
    copies = []
    for index in range(n):
        rel_dp, rel_core = index % 4, index // 4
        to_dp = (dp + rel_dp) - 2 * (dp & rel_dp)
        to_core = core if rel_core == 0 else 1 - core
        for at, (start, width) in enumerate(cuts):
            src = ins[index]
            if len(cuts) > 1:
                src = src.at[:, :, pl.ds(start, width)]
            copies.append(
                pltpu.make_async_copy(src, outs[at].at[to_dp, :, to_core], sem.at[index, at])
            )
    for c in copies:
        c.start()
    for c in copies:
        c.wait()


def assemble(parts, widths):
    r = parts[0].shape[1]
    cuts = []
    start = 0
    for width in widths:
        cuts.append((start, width))
        start += width
    outs = pl.pallas_call(
        functools.partial(assemble_kernel, cuts=cuts),
        in_specs=[pl.BlockSpec(memory_space=pl.ANY)] * 8,
        out_specs=[pl.BlockSpec(memory_space=pltpu.VMEM)] * len(widths),
        out_shape=[jax.ShapeDtypeStruct((4, 4, 2, r, w), BF) for w in widths],
        scratch_shapes=[pltpu.SemaphoreType.DMA((8, len(widths)))],
        cost_estimate=pl.CostEstimate(flops=0, bytes_accessed=4 * 32 * r * start, transcendentals=0),
        name="assemble",
    )(*parts)
    return [o.reshape(32 * r, o.shape[-1]) for o in outs]


def gather_rows(shard, first, widths):
    if not block_mesh():
        whole = lax.all_gather(shard, AX, axis=0, tiled=True)
        out = []
        start = 0
        for width in widths:
            out.append(whole[:, start : start + width])
            start += width
        return out
    second = XBIT + YBIT - first
    column = place_column(shard, [swap(shard, 2 * j) for j in range(1, 4)])
    near = swap(column, first)
    far = [swap(column, second), swap(near, second)]
    if first == XBIT:
        mine = [column, near, far[0], far[1]]
    else:
        mine = [column, far[0], near, far[1]]
    theirs = [swap(part, CORE) for part in mine]
    return assemble(mine + theirs, widths)


def scatter_rows(term, first):
    rows = term.shape[0]
    count = lax.axis_size(AX)
    r = rows // count
    if not block_mesh():
        return lax.psum_scatter(term.astype(F32), AX, scatter_dimension=0, tiled=True)
    width = term.shape[1]
    f = lax.axis_index("fsdp")
    d = lax.axis_index("dp")
    core, z = lax.rem(f, 2), f // 2
    xbit, ybit = lax.rem(d, 2), d // 2

    def fold(value, axis, bit, mask):
        kept = lax.dynamic_index_in_dim(value, bit, axis, keepdims=False)
        sent = lax.dynamic_index_in_dim(value, 1 - bit, axis, keepdims=False)
        return (kept.astype(F32) + swap(sent, mask).astype(F32)).astype(BF)

    value = term.reshape(2, 2, 4, 2, r, width)
    value = fold(value, 3, core, CORE)
    if first == XBIT:
        value = fold(value, 0, ybit, YBIT)
        value = fold(value, 0, xbit, XBIT)
    else:
        value = fold(value, 1, xbit, XBIT)
        value = fold(value, 0, ybit, YBIT)
    total = lax.dynamic_index_in_dim(value, z, 0, keepdims=False).astype(F32)
    for j in range(1, 4):
        other = lax.dynamic_index_in_dim(value, z ^ j, 0, keepdims=False)
        total = total + swap(other, 2 * j).astype(F32)
    return total


def layer_norm(values, gain, shift):
    centre = values - jnp.mean(values, axis=-1, keepdims=True)
    spread = jnp.mean(centre * centre, axis=-1, keepdims=True)
    return centre * lax.rsqrt(spread + EPS) * gain + shift


def inner_rows(left, right):
    return lax.dot_general(left, right, (((0,), (0,)), ((), ())), preferred_element_type=F32)


def times_transposed(left, right):
    return lax.dot_general(left, right, (((1,), (1,)), ((), ())), preferred_element_type=F32)


def column_sums(values):
    return jnp.sum(values.astype(F32), axis=0)


def gelu_pair(z):
    c = 0.7978845608028654
    t = jnp.tanh(c * (z + 0.044715 * z * z * z))
    value = 0.5 * z * (1.0 + t)
    slope = 0.5 * (1.0 + t) + 0.5 * z * (1.0 - t * t) * c * (1.0 + 3 * 0.044715 * z * z)
    return value.astype(BF), slope.astype(BF)


def pack_columns(vectors, wide, count):
    length = vectors[0].shape[0]
    ways = wide.shape[0] // length
    per = length // count
    spread = wide.reshape(count, ways, per).transpose(0, 2, 1).reshape(length, ways)
    block = jnp.concatenate([jnp.stack(vectors, axis=1), spread], axis=1)
    return jnp.pad(block, ((0, 0), (0, LANES - block.shape[1])))


def unpack_columns(block, vector_count, ways, count):
    length = block.shape[0]
    turned = block[:, : vector_count + ways].T
    wide = turned[vector_count:].reshape(ways, count, length // count).transpose(1, 0, 2).reshape(-1)
    return [turned[i] for i in range(vector_count)], wide


def gather_use(local, layer):
    (ga, sa, hw, qb, vb, mw, mb, gf, sf, ew, eb, sw, sb) = local
    small = pack_columns([ga, sa, qb, vb, mb, gf, sf, sb], eb, 1)
    width = hw.shape[1]
    if layer == 0:
        half = width // 2
        wa, sm = gather_rows(jnp.concatenate([hw[:, :half], small], axis=1), XBIT, [half, LANES])
        (wb,) = gather_rows(hw[:, half:], YBIT, [width - half])
        heads = jnp.concatenate([wa, wb], axis=1)
    else:
        heads, sm = gather_rows(jnp.concatenate([hw, small], axis=1), XBIT, [width, LANES])
    (mix,) = gather_rows(mw, YBIT, [mw.shape[1]])
    (expand,) = gather_rows(ew, XBIT, [ew.shape[1]])
    (shrink,) = gather_rows(sw, YBIT, [sw.shape[1]])
    vecs, wide = unpack_columns(sm, 8, eb.shape[0] // ga.shape[0], lax.axis_size(AX))
    vecs = [v.astype(F32) for v in vecs]
    return dict(zip(("ga", "sa", "qb", "vb", "mb", "gf", "sf", "sb"), vecs), eb=wide.astype(F32),
                heads=heads, mix=mix, expand=expand, shrink=shrink)


def forward_use(hidden, w, first_len):
    normed = layer_norm(hidden, w["ga"], w["sa"]).astype(BF)
    bias = jnp.concatenate([w["qb"], jnp.zeros_like(w["qb"]), w["vb"]])
    qkv = (jnp.dot(normed, w["heads"], preferred_element_type=F32) + bias).astype(BF)
    attended, lse = attend_fwd(qkv, first_len)
    middle = hidden + jnp.dot(attended, w["mix"], preferred_element_type=F32) + w["mb"]
    normed_two = layer_norm(middle, w["gf"], w["sf"]).astype(BF)
    expanded = jnp.dot(normed_two, w["expand"], preferred_element_type=F32) + w["eb"]
    activated, slope = gelu_pair(expanded)
    result = middle + jnp.dot(activated, w["shrink"], preferred_element_type=F32) + w["sb"]
    return result, (hidden, normed, qkv, attended, lse, middle, normed_two, activated, slope)


def backward_use(grad_out, kept, w, first_len):
    hidden, normed, qkv, attended, lse, middle, normed_two, activated, slope = kept
    width = hidden.shape[1]
    count = lax.axis_size(AX)
    grad_low = grad_out.astype(BF)
    shrink_term = inner_rows(activated, grad_low).astype(BF)
    shrink_share = scatter_rows(shrink_term, YBIT)
    sb = column_sums(grad_low)
    dz = (times_transposed(grad_low, w["shrink"]) * slope.astype(F32)).astype(BF)
    expand_share = scatter_rows(inner_rows(normed_two, dz).astype(BF), XBIT)
    eb = column_sums(dz)
    dc = times_transposed(dz, w["expand"])
    unused, norm_back = jax.vjp(layer_norm, middle, w["gf"], w["sf"])
    middle_norm, gf, sf = norm_back(dc)
    dm = grad_out + middle_norm
    dmb = dm.astype(BF)
    mix_share = scatter_rows(inner_rows(attended, dmb).astype(BF), YBIT)
    mb = column_sums(dmb)
    do = times_transposed(dmb, w["mix"]).astype(BF)
    dq, dk, dv = attend_bwd(qkv, do, lse, first_len)
    dqkv = jnp.concatenate([dq, dk, dv], axis=1)
    heads_term = inner_rows(normed, dqkv).astype(BF)
    qb = column_sums(dq)
    vb = column_sums(dv)
    da = times_transposed(dqkv, w["heads"])
    unused, first_back = jax.vjp(layer_norm, hidden, w["ga"], w["sa"])
    hidden_norm, ga, sa = first_back(da)
    small = pack_columns([ga, sa, qb, vb, mb, gf, sf, sb], eb, count).astype(BF)
    heads_share = scatter_rows(jnp.concatenate([heads_term, small], axis=1), XBIT)
    vecs, wide = unpack_columns(heads_share[:, 3 * width :], 8, eb.shape[0] // width, 1)
    ga, sa, qb, vb, mb, gf, sf, sb = vecs
    return dm + hidden_norm, (
        ga, sa, heads_share[:, : 3 * width], qb, vb, mix_share, mb, gf, sf, expand_share, wide,
        shrink_share, sb,
    )


def pick_shards(stacks, source):
    return tuple(lax.dynamic_index_in_dim(stack, source, 0, keepdims=False) for stack in stacks)


def place_terms(sources, shares):
    ids = lax.iota(jnp.int32, UNIQUE)
    out = []
    for items in zip(*shares):
        total = 0.0
        for source, item in zip(sources, items):
            chosen = (ids == source).reshape((UNIQUE,) + (1,) * item.ndim)
            total = total + jnp.where(chosen, item[None], 0.0)
        out.append(total)
    return out


def body(tokens, cotangent, tie_map, first_length, *stacks):
    hidden = tokens.astype(F32)
    sources = [tie_map[i] for i in range(LAYERS)]
    weights = [gather_use(pick_shards(stacks, s), i) for i, s in enumerate(sources)]
    kept = []
    for i in range(LAYERS):
        hidden, saved = forward_use(hidden, weights[i], first_length)
        kept.append(saved)
    grad = cotangent.astype(F32)
    shares = [None] * LAYERS
    for i in reversed(range(LAYERS)):
        grad, shares[i] = backward_use(grad, kept[i], weights[i], first_length)
    return (hidden.astype(BF), grad.astype(BF), *place_terms(sources, shares))


def solution(mesh):
    rows = P(AX, None)
    flat = P(None, AX)
    deep = P(None, AX, None)
    weights = (flat, flat, deep, flat, flat, deep, flat, flat, flat, deep, flat, deep, flat)
    return jax.shard_map(
        body,
        mesh=mesh,
        in_specs=(rows, rows, P(), P(AX)) + weights,
        out_specs=(rows, rows) + weights,
        check_vma=False,
    )
```

```python
import functools

import jax
import jax.numpy as jnp
from jax import lax
from jax.experimental import pallas as pl
from jax.experimental.pallas import tpu as pltpu
from jax.sharding import PartitionSpec as P

LAYERS = 2
UNIQUE = 4
F32 = jnp.float32
BF = jnp.bfloat16
AX = ("dp", "fsdp")
LANES = 128
EPS = 1e-05

NEG=-1e9
def nt(a,b): return lax.dot_general(a,b,(((1,),(1,)),((),())),preferred_element_type=F32)
def nn(a,b): return lax.dot_general(a,b,(((1,),(0,)),((),())),preferred_element_type=F32)
def halves(x):
    lane=lax.broadcasted_iota(jnp.int32,x.shape,1)
    z=jnp.zeros_like(x)
    return jnp.where(lane<64,x,z), jnp.where(lane<64,z,x)

def fwd_kernel(fl_ref,q_ref,k_ref,v_ref,o_ref,lse_ref,*,bq):
    L=q_ref.shape[0]; half=L//2
    second=fl_ref[pl.program_id(0)]<L
    shut=jnp.where(second,F32(1e9),F32(0.))
    q=q_ref[...]*BF(0.125); k=k_ref[...]; vT=v_ref[...].T
    sub=lax.broadcasted_iota(jnp.int32,vT.shape,0)
    zero=jnp.zeros_like(vT)
    vTs=(jnp.where(sub<64,vT,zero),jnp.where(sub<64,zero,vT))
    qs=halves(q)
    tri=lax.broadcasted_iota(jnp.int32,(bq,bq),0)<=lax.broadcasted_iota(jnp.int32,(bq,bq),1)
    for j in range(L//bq):
        lo=j*bq; hi=lo+bq
        acc=jnp.zeros((128,bq),F32)
        for h in range(2):
            qh=qs[h][lo:hi]
            s=nt(k[:hi],qh)
            parts=[]
            if lo>0 : parts.append((0,min(lo,half),s[:min(lo,half)]))
            if lo>half: parts.append((half,lo,s[half:lo]))
            diag=jnp.where(tri,s[lo:],NEG)
            m=jnp.max(diag,axis=0,keepdims=True)
            for a,b,t in parts:
                mt=jnp.max(t,axis=0,keepdims=True)
                if lo>=half and a==0: mt=mt-shut
                m=jnp.maximum(m,mt)
            ps=[]; l=0.
            for a,b,t in parts+[(lo,hi,diag)]:
                mm=m+shut if (lo>=half and a==0) else m
                p=jnp.exp(t-mm)
                l=l+jnp.sum(p,axis=0,keepdims=True)
                ps.append(p.astype(BF))
            p=jnp.concatenate(ps,axis=0) if len(ps)>1 else ps[0]
            oh=nn(vTs[h][:,:hi],p)
            acc=acc+oh*(1.0/l)
            lse_ref[0,h:h+1,lo:hi]=m+jnp.log(l)
        o_ref[lo:hi,:]=acc.T.astype(BF)

def attend_fwd(qkv,fl,bq=256):
    N,C=qkv.shape; R=fl.shape[0]; L=N//R; D=C//3; G=D//128
    return pl.pallas_call(functools.partial(fwd_kernel,bq=bq),
        grid_spec=pltpu.PrefetchScalarGridSpec(num_scalar_prefetch=1,grid=(R,G),
          in_specs=[pl.BlockSpec((L,128),lambda r,g,fl:(r,g)),
                    pl.BlockSpec((L,128),lambda r,g,fl:(r,G+g)),
                    pl.BlockSpec((L,128),lambda r,g,fl:(r,2*G+g))],
          out_specs=[pl.BlockSpec((L,128),lambda r,g,fl:(r,g)),
                     pl.BlockSpec((1,2,L),lambda r,g,fl:(r*G+g,0,0))]),
        out_shape=[jax.ShapeDtypeStruct((N,D),BF),jax.ShapeDtypeStruct((R*G,2,L),F32)],
        compiler_params=pltpu.CompilerParams(vmem_limit_bytes=48<<20),
        cost_estimate=pl.CostEstimate(flops=2*2*R*L*L*D*2,bytes_accessed=N*D*8,transcendentals=R*L*L*12//2),
        name="attend_fwd")(fl,qkv,qkv,qkv)

def bwd_kernel(fl_ref,q_ref,k_ref,v_ref,do_ref,lse_ref,dq_ref,dk_ref,dv_ref,dk_acc,dv_acc,*,bq):
    L=q_ref.shape[0]; half=L//2
    second=fl_ref[pl.program_id(0)]<L
    shut=jnp.where(second,F32(1e9),F32(0.))
    q=q_ref[...]*BF(0.125); k=k_ref[...]; v=v_ref[...]; do=do_ref[...]
    kT=k.T
    sub=lax.broadcasted_iota(jnp.int32,kT.shape,0); zero=jnp.zeros_like(kT)
    kTs=(jnp.where(sub<64,kT,zero),jnp.where(sub<64,zero,kT))
    qs=halves(q); dos=halves(do)
    tri=lax.broadcasted_iota(jnp.int32,(bq,bq),0)<=lax.broadcasted_iota(jnp.int32,(bq,bq),1)
    nb=L//bq
    for j in reversed(range(nb)):
        lo=j*bq; hi=lo+bq
        dqT=jnp.zeros((128,bq),F32)
        dkp=None; dvp=None
        for h in range(2):
            qh=qs[h][lo:hi]; doh=dos[h][lo:hi]
            lse=lse_ref[0,h:h+1,lo:hi]
            s=nt(k[:hi],qh)
            dp=nt(v[:hi],doh)
            ps=[];
            cuts=[]
            if lo>0: cuts.append((0,min(lo,half)))
            if lo>half: cuts.append((half,lo))
            cuts.append((lo,hi))
            for a,b in cuts:
                ll=lse+shut if (lo>=half and b<=half) else lse
                t=s[a:b]-ll
                if a==lo: t=jnp.where(tri,t,NEG)
                ps.append(jnp.exp(t))
            p=jnp.concatenate(ps,axis=0) if len(ps)>1 else ps[0]
            delta=jnp.sum(p*dp,axis=0,keepdims=True)
            ds=(p*(dp-delta)).astype(BF)
            pb=p.astype(BF)
            dv_=nn(pb,doh); dk_=nn(ds,qh)
            dvp=dv_ if dvp is None else dvp+dv_
            dkp=dk_ if dkp is None else dkp+dk_
            dqT=dqT+nn(kTs[h][:,:hi],ds)
        if j==nb-1:
            dk_acc[...]=dkp; dv_acc[...]=dvp
        else:
            dk_acc[:hi]+=dkp; dv_acc[:hi]+=dvp
        dq_ref[lo:hi,:]=(dqT.T*0.125).astype(BF)
    dk_ref[...]=dk_acc[...].astype(BF); dv_ref[...]=dv_acc[...].astype(BF)

def attend_bwd(qkv,do,lse,fl,bq=256):
    N,C=qkv.shape; R=fl.shape[0]; L=N//R; D=C//3; G=D//128
    blk=lambda off: pl.BlockSpec((L,128),lambda r,g,fl:(r,off*G+g))
    return pl.pallas_call(functools.partial(bwd_kernel,bq=bq),
        grid_spec=pltpu.PrefetchScalarGridSpec(num_scalar_prefetch=1,grid=(R,G),
          in_specs=[blk(0),blk(1),blk(2),blk(0),pl.BlockSpec((1,2,L),lambda r,g,fl:(r*G+g,0,0))],
          out_specs=[blk(0),blk(0),blk(0)],
          scratch_shapes=[pltpu.VMEM((L,128),F32),pltpu.VMEM((L,128),F32)]),
        out_shape=[jax.ShapeDtypeStruct((N,D),BF)]*3,
        compiler_params=pltpu.CompilerParams(vmem_limit_bytes=48<<20),
        cost_estimate=pl.CostEstimate(flops=5*2*R*L*L*D*2,bytes_accessed=N*D*16,transcendentals=R*L*L*12//2),
        name="attend_bwd")(fl,qkv,qkv,qkv,do,lse)


MESH = pl.DeviceIdType.MESH


def block_mesh():
    return lax.axis_size("dp") == 4 and lax.axis_size("fsdp") == 8


class Place:
    def __init__(self):
        d = lax.axis_index("dp")
        f = lax.axis_index("fsdp")
        self.y, self.x = lax.div(d, 2), lax.rem(d, 2)
        self.z, self.c = lax.div(f, 2), lax.rem(f, 2)
        self.zs = [self.z + 1 - 2 * lax.rem(self.z, 2), lax.rem(self.z + 2, 4), 3 - self.z]
        self.to_core = (d, 2 * self.z + 1 - self.c)
        self.to_x = (2 * self.y + 1 - self.x, f)
        self.to_y = (2 * (1 - self.y) + self.x, f)
        self.to_z = [(d, 2 * zz + self.c) for zz in self.zs]

    def greet(self):
        barrier = pltpu.get_barrier_semaphore()
        peers = [self.to_core, self.to_x, self.to_y] + self.to_z
        for peer in peers:
            pl.semaphore_signal(barrier, inc=1, device_id=peer, device_id_type=MESH)
        pl.semaphore_wait(barrier, len(peers))


ALL = slice(None)


class Gather:
    COPIES = 12
    STEPS = 5

    def __init__(self, me, shard, out, send, recv, local):
        self.me, self.shard, self.out, self.send, self.recv = me, shard, out, send, recv
        self.width = shard.shape[-1]
        self.cut = (self.width // 256 + self.width // 128 % 2) * 128
        y, x, z, c = me.y, me.x, me.z, me.c
        left, right = pl.ds(0, self.cut), pl.ds(self.cut, self.width - self.cut)
        self.own = pltpu.make_async_copy(shard, out.at[y, x, z, c], local)
        o = out.at
        self.plan = [(None, me.to_z[j], out.at[y, x, z, c]) for j in range(3)] + [
            (None, me.to_x, o[y, x, ALL, c, ALL, left]),
            (None, me.to_y, o[y, x, ALL, c, ALL, right]),
            (None, me.to_core, o[y, x, ALL, c]),
            (None, me.to_y, o[y, ALL, ALL, c, ALL, left]),
            (None, me.to_x, o[ALL, x, ALL, c, ALL, right]),
            (None, me.to_core, o[y, 1 - x, ALL, c, ALL, left]),
            (None, me.to_core, o[1 - y, x, ALL, c, ALL, right]),
            (None, me.to_core, o[1 - y, ALL, ALL, c, ALL, left]),
            (None, me.to_core, o[ALL, 1 - x, ALL, c, ALL, right]),
        ]

    def copy(self, k):
        peer, ref = self.plan[k][1:]
        return pltpu.make_async_remote_copy(
            src_ref=self.shard if k < 3 else ref, dst_ref=ref, send_sem=self.send.at[k],
            recv_sem=self.recv.at[k], device_id=peer, device_id_type=MESH)

    def run(self, step):
        waits, starts = [
            ((), (0, 1, 2)),
            ((0, 1, 2), (3, 4, 5)),
            ((3, 4), (6, 7, 8, 9)),
            ((6, 7), (10, 11)),
            ((5, 8, 9, 10, 11), ()),
        ][step]
        if step == 0:
            self.own.start()
        for k in waits:
            self.copy(k).wait_recv()
        if step == 1:
            self.own.wait()
        for k in starts:
            self.copy(k).start()
        if step == 4:
            for k in range(12):
                self.copy(k).wait_send()


class Scatter:
    COPIES = 8
    STEPS = 5

    def __init__(self, me, term, out, own, r0, r1, r2, r3, send, recv, local):
        self.me, self.out, self.own, self.r = me, out, own, (r0, r1, r2, r3)
        self.send, self.recv = send, recv
        self.width = own.shape[-1]
        self.cut = (self.width // 256 + self.width // 128 % 2) * 128
        y, x, z, c = me.y, me.x, me.z, me.c
        left, right = pl.ds(0, self.cut), pl.ds(self.cut, self.width - self.cut)
        self.mine = pltpu.make_async_copy(term.at[ALL, ALL, ALL, c], own, local)
        self.left, self.right = left, right
        self.plan = [
            (term.at[ALL, ALL, ALL, 1 - c], me.to_core, r0),
            (own.at[1 - y, ALL, ALL, ALL, left], me.to_y, r1.at[ALL, ALL, ALL, left]),
            (own.at[ALL, 1 - x, ALL, ALL, right], me.to_x, r1.at[ALL, ALL, ALL, right]),
            (own.at[y, 1 - x, ALL, ALL, left], me.to_x, r2.at[ALL, ALL, left]),
            (own.at[1 - y, x, ALL, ALL, right], me.to_y, r2.at[ALL, ALL, right]),
        ] + [(own.at[y, x, me.zs[j]], me.to_z[j], r3.at[j]) for j in range(3)]

    def copy(self, k):
        src, peer, dst = self.plan[k]
        return pltpu.make_async_remote_copy(
            src_ref=src, dst_ref=dst, send_sem=self.send.at[k], recv_sem=self.recv.at[k],
            device_id=peer, device_id_type=MESH)

    def run(self, step):
        y, x, z = self.me.y, self.me.x, self.me.z
        own, (r0, r1, r2, r3) = self.own, self.r
        left, right = self.left, self.right
        if step == 0:
            self.mine.start()
            self.copy(0).start()
        elif step == 1:
            self.mine.wait()
            self.copy(0).wait_recv()

            @pl.loop(0, 4)
            def _(k):
                for a in range(2):
                    for b in range(2):
                        own[a, b, k] = own[a, b, k] + r0[a, b, k]

            self.copy(1).start()
            self.copy(2).start()
        elif step == 2:
            self.copy(1).wait_recv()
            self.copy(2).wait_recv()

            @pl.loop(0, 4)
            def _(k):
                for a in range(2):
                    own[y, a, k, :, left] = own[y, a, k, :, left] + r1[a, k, :, left]
                    own[a, x, k, :, right] = own[a, x, k, :, right] + r1[a, k, :, right]

            self.copy(3).start()
            self.copy(4).start()
        elif step == 3:
            self.copy(3).wait_recv()
            self.copy(4).wait_recv()

            @pl.loop(0, 4)
            def _(k):
                own[y, x, k] = own[y, x, k] + r2[k]

            for k in (5, 6, 7):
                self.copy(k).start()
        else:
            total = own[y, x, z].astype(F32)
            for k in (5, 6, 7):
                self.copy(k).wait_recv()
                total = total + r3[k - 5].astype(F32)
            self.out[...] = total
            for k in range(8):
                self.copy(k).wait_send()


def host_specs(kind, arrays):
    n = len(arrays)
    sems = [pltpu.SemaphoreType.DMA((n, kind.COPIES)), pltpu.SemaphoreType.DMA((n, kind.COPIES)),
            pltpu.SemaphoreType.DMA((n,))]
    if kind is Gather:
        ins = [pl.BlockSpec(memory_space=pltpu.VMEM)] * n
        outs = [pl.BlockSpec(memory_space=pl.ANY)] * n
        shapes = [jax.ShapeDtypeStruct((2, 2, 4, 2) + a.shape, a.dtype) for a in arrays]
        return ins, outs, shapes, sems
    ins = [pl.BlockSpec(memory_space=pl.ANY)] * n
    outs = [pl.BlockSpec(memory_space=pltpu.VMEM)] * n
    shapes = [jax.ShapeDtypeStruct(a.shape[4:], F32) for a in arrays]
    scratch = []
    for a in arrays:
        tail = a.shape[4:]
        for lead in ((2, 2, 4), (2, 2, 4), (2, 4), (4,), (3,)):
            scratch.append(pltpu.VMEM(lead + tail, a.dtype))
    return ins, outs, shapes, scratch + sems


def host_build(kind, ins, outs, scratch):
    me = Place()
    send, recv, local = scratch[-3:]
    jobs = []
    for i in range(len(ins)):
        extra = scratch[5 * i : 5 * i + 5] if kind is Scatter else ()
        jobs.append(kind(me, ins[i], outs[i], *extra, send.at[i], recv.at[i], local.at[i]))
    return me, jobs


def in_order(count, steps):
    return [(i, t - i) for t in range(count + steps - 1) for i in range(count) if 0 <= t - i < steps]


def comm_kernel(*refs, kind, n):
    me, jobs = host_build(kind, refs[:n], refs[n : 2 * n], refs[2 * n :])
    me.greet()
    for i in range(n):
        jobs[i].run(0)
    for i, t in in_order(n, kind.STEPS):
        if t > 0:
            jobs[i].run(t)


def exchange(kind, arrays, ident, name):
    n = len(arrays)
    ins, outs, shapes, scratch = host_specs(kind, arrays)
    return pl.pallas_call(
        functools.partial(comm_kernel, kind=kind, n=n),
        in_specs=ins, out_specs=outs, out_shape=shapes, scratch_shapes=scratch,
        compiler_params=pltpu.CompilerParams(
            collective_id=ident, has_side_effects=True, vmem_limit_bytes=48 << 20),
        name=name)(*arrays)


def gather_all(shards, ident):
    if not block_mesh():
        return [lax.all_gather(a, AX, axis=0, tiled=True) for a in shards]
    wide = exchange(Gather, shards, ident, "gather")
    return [w.reshape(-1, w.shape[-1]) for w in wide]


def scatter_all(terms, ident):
    if not block_mesh():
        return [lax.psum_scatter(t.astype(F32), AX, scatter_dimension=0, tiled=True) for t in terms]
    return exchange(Scatter, [t.reshape(2, 2, 4, 2, -1, t.shape[-1]) for t in terms], ident, "scatter")


def layer_norm(values, gain, shift):
    centre = values - jnp.mean(values, axis=-1, keepdims=True)
    spread = jnp.mean(centre * centre, axis=-1, keepdims=True)
    return centre * lax.rsqrt(spread + EPS) * gain + shift


def inner_rows(left, right):
    return lax.dot_general(left, right, (((0,), (0,)), ((), ())), preferred_element_type=F32)


def times_transposed(left, right):
    return lax.dot_general(left, right, (((1,), (1,)), ((), ())), preferred_element_type=F32)


def column_sums(values):
    return jnp.sum(values.astype(F32), axis=0)


def gelu_pair(z):
    c = 0.7978845608028654
    t = jnp.tanh(c * (z + 0.044715 * z * z * z))
    value = 0.5 * z * (1.0 + t)
    slope = 0.5 * (1.0 + t) + 0.5 * z * (1.0 - t * t) * c * (1.0 + 3 * 0.044715 * z * z)
    return value.astype(BF), slope.astype(BF)


def pack_columns(vectors, wide, count):
    length = vectors[0].shape[0]
    ways = wide.shape[0] // length
    per = length // count
    spread = wide.reshape(count, ways, per).transpose(0, 2, 1).reshape(length, ways)
    block = jnp.concatenate([jnp.stack(vectors, axis=1), spread], axis=1)
    return jnp.pad(block, ((0, 0), (0, LANES - block.shape[1])))


def unpack_columns(block, vector_count, ways, count):
    length = block.shape[0]
    turned = block[:, : vector_count + ways].T
    wide = turned[vector_count:].reshape(ways, count, length // count).transpose(1, 0, 2).reshape(-1)
    return [turned[i] for i in range(vector_count)], wide


def local_shards(local):
    (ga, sa, hw, qb, vb, mw, mb, gf, sf, ew, eb, sw, sb) = local
    small = pack_columns([ga, sa, qb, vb, mb, gf, sf, sb], eb, 1)
    return [jnp.concatenate([hw, small], axis=1), mw, ew, sw]


def as_weights(whole, width, ways):
    heads, mix, expand, shrink = whole
    vecs, wide = unpack_columns(heads[:, 3 * width :], 8, ways, lax.axis_size(AX))
    vecs = [v.astype(F32) for v in vecs]
    return dict(zip(("ga", "sa", "qb", "vb", "mb", "gf", "sf", "sb"), vecs), eb=wide.astype(F32),
                heads=heads[:, : 3 * width], mix=mix, expand=expand, shrink=shrink)


def forward_use(hidden, w, first_len):
    normed = layer_norm(hidden, w["ga"], w["sa"]).astype(BF)
    bias = jnp.concatenate([w["qb"], jnp.zeros_like(w["qb"]), w["vb"]])
    qkv = (jnp.dot(normed, w["heads"], preferred_element_type=F32) + bias).astype(BF)
    attended, lse = attend_fwd(qkv, first_len)
    middle = hidden + jnp.dot(attended, w["mix"], preferred_element_type=F32) + w["mb"]
    normed_two = layer_norm(middle, w["gf"], w["sf"]).astype(BF)
    expanded = jnp.dot(normed_two, w["expand"], preferred_element_type=F32) + w["eb"]
    activated, slope = gelu_pair(expanded)
    result = middle + jnp.dot(activated, w["shrink"], preferred_element_type=F32) + w["sb"]
    return result, (hidden, normed, qkv, attended, lse, middle, normed_two, activated, slope)


def backward_use(grad_out, kept, w, first_len):
    hidden, normed, qkv, attended, lse, middle, normed_two, activated, slope = kept
    count = lax.axis_size(AX)
    grad_low = grad_out.astype(BF)
    shrink_term = inner_rows(activated, grad_low).astype(BF)
    sb = column_sums(grad_low)
    dz = (times_transposed(grad_low, w["shrink"]) * slope.astype(F32)).astype(BF)
    expand_term = inner_rows(normed_two, dz).astype(BF)
    eb = column_sums(dz)
    dc = times_transposed(dz, w["expand"])
    unused, norm_back = jax.vjp(layer_norm, middle, w["gf"], w["sf"])
    middle_norm, gf, sf = norm_back(dc)
    dm = grad_out + middle_norm
    dmb = dm.astype(BF)
    mix_term = inner_rows(attended, dmb).astype(BF)
    mb = column_sums(dmb)
    do = times_transposed(dmb, w["mix"]).astype(BF)
    dq, dk, dv = attend_bwd(qkv, do, lse, first_len)
    dqkv = jnp.concatenate([dq, dk, dv], axis=1)
    heads_term = inner_rows(normed, dqkv).astype(BF)
    qb = column_sums(dq)
    vb = column_sums(dv)
    da = times_transposed(dqkv, w["heads"])
    unused, first_back = jax.vjp(layer_norm, hidden, w["ga"], w["sa"])
    hidden_norm, ga, sa = first_back(da)
    small = pack_columns([ga, sa, qb, vb, mb, gf, sf, sb], eb, count)
    return dm + hidden_norm, (shrink_term, expand_term, mix_term, heads_term), small


def as_shares(shrink, expand, mix, heads, small):
    vecs, wide = unpack_columns(small, 8, shrink.shape[0] // heads.shape[0], 1)
    ga, sa, qb, vb, mb, gf, sf, sb = vecs
    return ga, sa, heads, qb, vb, mix, mb, gf, sf, expand, wide, shrink, sb


def pick_shards(stacks, source):
    return tuple(lax.dynamic_index_in_dim(stack, source, 0, keepdims=False) for stack in stacks)


def place_terms(sources, shares):
    ids = lax.iota(jnp.int32, UNIQUE)
    out = []
    for items in zip(*shares):
        total = 0.0
        for source, item in zip(sources, items):
            chosen = (ids == source).reshape((UNIQUE,) + (1,) * item.ndim)
            total = total + jnp.where(chosen, item[None], 0.0)
        out.append(total)
    return out


def body(tokens, cotangent, tie_map, first_length, *stacks):
    hidden = tokens.astype(F32)
    width = hidden.shape[1]
    sources = [tie_map[i] for i in range(LAYERS)]
    shards = [local_shards(pick_shards(stacks, s)) for s in sources]
    ways = shards[0][3].shape[0] // shards[0][0].shape[0]
    whole = gather_all(shards[0] + shards[1], 0)
    weights = [as_weights(whole[4 * i : 4 * i + 4], width, ways) for i in range(LAYERS)]
    kept = []
    for i in range(LAYERS):
        hidden, saved = forward_use(hidden, weights[i], first_length)
        kept.append(saved)
    grad = cotangent.astype(F32)
    terms, small = [None] * LAYERS, [None] * LAYERS
    for i in reversed(range(LAYERS)):
        grad, terms[i], small[i] = backward_use(grad, kept[i], weights[i], first_length)
    late = scatter_all(list(terms[1]), 1)
    early = scatter_all(list(terms[0]) + [jnp.concatenate(small, axis=1)], 2)
    shares = [as_shares(*early[:4], early[4][:, :LANES]), as_shares(*late, early[4][:, LANES:])]
    return (hidden.astype(BF), grad.astype(BF), *place_terms(sources, shares))


def solution(mesh):
    rows = P(AX, None)
    flat = P(None, AX)
    deep = P(None, AX, None)
    weights = (flat, flat, deep, flat, flat, deep, flat, flat, flat, deep, flat, deep, flat)
    return jax.shard_map(
        body,
        mesh=mesh,
        in_specs=(rows, rows, P(), P(AX)) + weights,
        out_specs=(rows, rows) + weights,
        check_vma=False,
    )
```

```python
import functools

import jax
import jax.numpy as jnp
from jax import lax
from jax.experimental import pallas as pl
from jax.experimental.pallas import tpu as pltpu
from jax.sharding import PartitionSpec as P

LAYERS = 2
UNIQUE = 4
F32 = jnp.float32
BF = jnp.bfloat16
AX = ("dp", "fsdp")
LANES = 128
EPS = 1e-05

NEG=-1e9
def nt(a,b): return lax.dot_general(a,b,(((1,),(1,)),((),())),preferred_element_type=F32)
def nn(a,b): return lax.dot_general(a,b,(((1,),(0,)),((),())),preferred_element_type=F32)
def halves(x):
    lane=lax.broadcasted_iota(jnp.int32,x.shape,1)
    z=jnp.zeros_like(x)
    return jnp.where(lane<64,x,z), jnp.where(lane<64,z,x)

def fwd_kernel(fl_ref,q_ref,k_ref,v_ref,*rest,bq,host):
    n=host.count
    o_ref,lse_ref=rest[n:n+2]
    jobs=host.enter(rest[:n],rest[n+2:2*n+2],rest[2*n+2:])
    L=q_ref.shape[0]; half=L//2
    second=fl_ref[pl.program_id(0)]<L
    shut=jnp.where(second,F32(1e9),F32(0.))
    q=q_ref[...]*BF(0.125); k=k_ref[...]; vT=v_ref[...].T
    sub=lax.broadcasted_iota(jnp.int32,vT.shape,0)
    zero=jnp.zeros_like(vT)
    vTs=(jnp.where(sub<64,vT,zero),jnp.where(sub<64,zero,vT))
    qs=halves(q)
    tri=lax.broadcasted_iota(jnp.int32,(bq,bq),0)<=lax.broadcasted_iota(jnp.int32,(bq,bq),1)
    for j in range(L//bq):
        lo=j*bq; hi=lo+bq
        acc=jnp.zeros((128,bq),F32)
        for h in range(2):
            qh=qs[h][lo:hi]
            s=nt(k[:hi],qh)
            parts=[]
            if lo>0 : parts.append((0,min(lo,half),s[:min(lo,half)]))
            if lo>half: parts.append((half,lo,s[half:lo]))
            diag=jnp.where(tri,s[lo:],NEG)
            m=jnp.max(diag,axis=0,keepdims=True)
            for a,b,t in parts:
                mt=jnp.max(t,axis=0,keepdims=True)
                if lo>=half and a==0: mt=mt-shut
                m=jnp.maximum(m,mt)
            ps=[]; l=0.
            for a,b,t in parts+[(lo,hi,diag)]:
                mm=m+shut if (lo>=half and a==0) else m
                p=jnp.exp(t-mm)
                l=l+jnp.sum(p,axis=0,keepdims=True)
                ps.append(p.astype(BF))
            p=jnp.concatenate(ps,axis=0) if len(ps)>1 else ps[0]
            oh=nn(vTs[h][:,:hi],p)
            acc=acc+oh*(1.0/l)
            lse_ref[0,h:h+1,lo:hi]=m+jnp.log(l)
        o_ref[lo:hi,:]=acc.T.astype(BF)
    host.leave(jobs)

def attend_fwd(qkv,fl,host,bq=256):
    N,C=qkv.shape; R=fl.shape[0]; L=N//R; D=C//3; G=D//128
    return pl.pallas_call(functools.partial(fwd_kernel,bq=bq,host=host),
        grid_spec=pltpu.PrefetchScalarGridSpec(num_scalar_prefetch=1,grid=(R,G),
          in_specs=[pl.BlockSpec((L,128),lambda r,g,fl:(r,g)),
                    pl.BlockSpec((L,128),lambda r,g,fl:(r,G+g)),
                    pl.BlockSpec((L,128),lambda r,g,fl:(r,2*G+g))]+host.ins,
          out_specs=[pl.BlockSpec((L,128),lambda r,g,fl:(r,g)),
                     pl.BlockSpec((1,2,L),lambda r,g,fl:(r*G+g,0,0))]+host.outs,
          scratch_shapes=host.scratch),
        out_shape=[jax.ShapeDtypeStruct((N,D),BF),jax.ShapeDtypeStruct((R*G,2,L),F32)]+host.shapes,
        compiler_params=host.params(),
        cost_estimate=pl.CostEstimate(flops=2*2*R*L*L*D*2,bytes_accessed=N*D*8,transcendentals=R*L*L*12//2),
        name="attend_fwd")(fl,qkv,qkv,qkv,*host.arrays)

def bwd_kernel(fl_ref,q_ref,k_ref,v_ref,do_ref,lse_ref,*rest,bq,host):
    n=host.count
    dq_ref,dk_ref,dv_ref=rest[n:n+3]
    dk_acc,dv_acc=rest[2*n+3:2*n+5]
    jobs=host.enter(rest[:n],rest[n+3:2*n+3],rest[2*n+5:])
    L=q_ref.shape[0]; half=L//2
    second=fl_ref[pl.program_id(0)]<L
    shut=jnp.where(second,F32(1e9),F32(0.))
    q=q_ref[...]*BF(0.125); k=k_ref[...]; v=v_ref[...]; do=do_ref[...]
    kT=k.T
    sub=lax.broadcasted_iota(jnp.int32,kT.shape,0); zero=jnp.zeros_like(kT)
    kTs=(jnp.where(sub<64,kT,zero),jnp.where(sub<64,zero,kT))
    qs=halves(q); dos=halves(do)
    tri=lax.broadcasted_iota(jnp.int32,(bq,bq),0)<=lax.broadcasted_iota(jnp.int32,(bq,bq),1)
    nb=L//bq
    for j in reversed(range(nb)):
        lo=j*bq; hi=lo+bq
        dqT=jnp.zeros((128,bq),F32)
        dkp=None; dvp=None
        for h in range(2):
            qh=qs[h][lo:hi]; doh=dos[h][lo:hi]
            lse=lse_ref[0,h:h+1,lo:hi]
            s=nt(k[:hi],qh)
            dp=nt(v[:hi],doh)
            ps=[];
            cuts=[]
            if lo>0: cuts.append((0,min(lo,half)))
            if lo>half: cuts.append((half,lo))
            cuts.append((lo,hi))
            for a,b in cuts:
                ll=lse+shut if (lo>=half and b<=half) else lse
                t=s[a:b]-ll
                if a==lo: t=jnp.where(tri,t,NEG)
                ps.append(jnp.exp(t))
            p=jnp.concatenate(ps,axis=0) if len(ps)>1 else ps[0]
            delta=jnp.sum(p*dp,axis=0,keepdims=True)
            ds=(p*(dp-delta)).astype(BF)
            pb=p.astype(BF)
            dv_=nn(pb,doh); dk_=nn(ds,qh)
            dvp=dv_ if dvp is None else dvp+dv_
            dkp=dk_ if dkp is None else dkp+dk_
            dqT=dqT+nn(kTs[h][:,:hi],ds)
        if j==nb-1:
            dk_acc[...]=dkp; dv_acc[...]=dvp
        else:
            dk_acc[:hi]+=dkp; dv_acc[:hi]+=dvp
        dq_ref[lo:hi,:]=(dqT.T*0.125).astype(BF)
    dk_ref[...]=dk_acc[...].astype(BF); dv_ref[...]=dv_acc[...].astype(BF)
    host.leave(jobs)

def attend_bwd(qkv,do,lse,fl,host,bq=256):
    N,C=qkv.shape; R=fl.shape[0]; L=N//R; D=C//3; G=D//128
    blk=lambda off: pl.BlockSpec((L,128),lambda r,g,fl:(r,off*G+g))
    return pl.pallas_call(functools.partial(bwd_kernel,bq=bq,host=host),
        grid_spec=pltpu.PrefetchScalarGridSpec(num_scalar_prefetch=1,grid=(R,G),
          in_specs=[blk(0),blk(1),blk(2),blk(0),pl.BlockSpec((1,2,L),lambda r,g,fl:(r*G+g,0,0))]+host.ins,
          out_specs=[blk(0),blk(0),blk(0)]+host.outs,
          scratch_shapes=[pltpu.VMEM((L,128),F32),pltpu.VMEM((L,128),F32)]+host.scratch),
        out_shape=[jax.ShapeDtypeStruct((N,D),BF)]*3+host.shapes,
        compiler_params=host.params(),
        cost_estimate=pl.CostEstimate(flops=5*2*R*L*L*D*2,bytes_accessed=N*D*16,transcendentals=R*L*L*12//2),
        name="attend_bwd")(fl,qkv,qkv,qkv,do,lse,*host.arrays)


MESH = pl.DeviceIdType.MESH


def block_mesh():
    return lax.axis_size("dp") == 4 and lax.axis_size("fsdp") == 8


class Place:
    def __init__(self):
        d = lax.axis_index("dp")
        f = lax.axis_index("fsdp")
        self.y, self.x = lax.div(d, 2), lax.rem(d, 2)
        self.z, self.c = lax.div(f, 2), lax.rem(f, 2)
        self.zs = [self.z + 1 - 2 * lax.rem(self.z, 2), lax.rem(self.z + 2, 4), 3 - self.z]
        self.to_core = (d, 2 * self.z + 1 - self.c)
        self.to_x = (2 * self.y + 1 - self.x, f)
        self.to_y = (2 * (1 - self.y) + self.x, f)
        self.to_z = [(d, 2 * zz + self.c) for zz in self.zs]

    def greet(self):
        barrier = pltpu.get_barrier_semaphore()
        peers = [self.to_core, self.to_x, self.to_y] + self.to_z
        for peer in peers:
            pl.semaphore_signal(barrier, inc=1, device_id=peer, device_id_type=MESH)
        pl.semaphore_wait(barrier, len(peers))


ALL = slice(None)


class Gather:
    COPIES = 12
    STEPS = 5

    def __init__(self, me, shard, out, send, recv, local):
        self.me, self.shard, self.out, self.send, self.recv = me, shard, out, send, recv
        self.width = shard.shape[-1]
        self.cut = (self.width // 256 + self.width // 128 % 2) * 128
        y, x, z, c = me.y, me.x, me.z, me.c
        left, right = pl.ds(0, self.cut), pl.ds(self.cut, self.width - self.cut)
        self.own = pltpu.make_async_copy(shard, out.at[y, x, z, c], local)
        o = out.at
        self.plan = [(None, me.to_z[j], out.at[y, x, z, c]) for j in range(3)] + [
            (None, me.to_x, o[y, x, ALL, c, ALL, left]),
            (None, me.to_y, o[y, x, ALL, c, ALL, right]),
            (None, me.to_core, o[y, x, ALL, c]),
            (None, me.to_y, o[y, ALL, ALL, c, ALL, left]),
            (None, me.to_x, o[ALL, x, ALL, c, ALL, right]),
            (None, me.to_core, o[y, 1 - x, ALL, c, ALL, left]),
            (None, me.to_core, o[1 - y, x, ALL, c, ALL, right]),
            (None, me.to_core, o[1 - y, ALL, ALL, c, ALL, left]),
            (None, me.to_core, o[ALL, 1 - x, ALL, c, ALL, right]),
        ]

    def copy(self, k):
        peer, ref = self.plan[k][1:]
        return pltpu.make_async_remote_copy(
            src_ref=self.shard if k < 3 else ref, dst_ref=ref, send_sem=self.send.at[k],
            recv_sem=self.recv.at[k], device_id=peer, device_id_type=MESH)

    def run(self, step):
        waits, starts = [
            ((), (0, 1, 2)),
            ((0, 1, 2), (3, 4, 5)),
            ((3, 4), (6, 7, 8, 9)),
            ((6, 7), (10, 11)),
            ((5, 8, 9, 10, 11), ()),
        ][step]
        if step == 0:
            self.own.start()
        for k in waits:
            self.copy(k).wait_recv()
        if step == 1:
            self.own.wait()
        for k in starts:
            self.copy(k).start()
        if step == 4:
            for k in range(12):
                self.copy(k).wait_send()


class Scatter:
    COPIES = 8
    STEPS = 5

    def __init__(self, me, term, out, own, r0, r1, r2, r3, send, recv, local):
        self.me, self.out, self.own, self.r = me, out, own, (r0, r1, r2, r3)
        self.send, self.recv = send, recv
        self.width = own.shape[-1]
        self.cut = (self.width // 256 + self.width // 128 % 2) * 128
        y, x, z, c = me.y, me.x, me.z, me.c
        left, right = pl.ds(0, self.cut), pl.ds(self.cut, self.width - self.cut)
        self.mine = pltpu.make_async_copy(term.at[ALL, ALL, ALL, c], own, local)
        self.left, self.right = left, right
        self.plan = [
            (term.at[ALL, ALL, ALL, 1 - c], me.to_core, r0),
            (own.at[1 - y, ALL, ALL, ALL, left], me.to_y, r1.at[ALL, ALL, ALL, left]),
            (own.at[ALL, 1 - x, ALL, ALL, right], me.to_x, r1.at[ALL, ALL, ALL, right]),
            (own.at[y, 1 - x, ALL, ALL, left], me.to_x, r2.at[ALL, ALL, left]),
            (own.at[1 - y, x, ALL, ALL, right], me.to_y, r2.at[ALL, ALL, right]),
        ] + [(own.at[y, x, me.zs[j]], me.to_z[j], r3.at[j]) for j in range(3)]

    def copy(self, k):
        src, peer, dst = self.plan[k]
        return pltpu.make_async_remote_copy(
            src_ref=src, dst_ref=dst, send_sem=self.send.at[k], recv_sem=self.recv.at[k],
            device_id=peer, device_id_type=MESH)

    def run(self, step):
        y, x, z = self.me.y, self.me.x, self.me.z
        own, (r0, r1, r2, r3) = self.own, self.r
        left, right = self.left, self.right
        if step == 0:
            self.mine.start()
            self.copy(0).start()
        elif step == 1:
            self.mine.wait()
            self.copy(0).wait_recv()

            @pl.loop(0, 4)
            def _(k):
                for a in range(2):
                    for b in range(2):
                        own[a, b, k] = own[a, b, k] + r0[a, b, k]

            self.copy(1).start()
            self.copy(2).start()
        elif step == 2:
            self.copy(1).wait_recv()
            self.copy(2).wait_recv()

            @pl.loop(0, 4)
            def _(k):
                for a in range(2):
                    own[y, a, k, :, left] = own[y, a, k, :, left] + r1[a, k, :, left]
                    own[a, x, k, :, right] = own[a, x, k, :, right] + r1[a, k, :, right]

            self.copy(3).start()
            self.copy(4).start()
        elif step == 3:
            self.copy(3).wait_recv()
            self.copy(4).wait_recv()

            @pl.loop(0, 4)
            def _(k):
                own[y, x, k] = own[y, x, k] + r2[k]

            for k in (5, 6, 7):
                self.copy(k).start()
        else:
            total = own[y, x, z].astype(F32)
            for k in (5, 6, 7):
                self.copy(k).wait_recv()
                total = total + r3[k - 5].astype(F32)
            self.out[...] = total
            for k in range(8):
                self.copy(k).wait_send()


def host_specs(kind, arrays):
    n = len(arrays)
    sems = [pltpu.SemaphoreType.DMA((n, kind.COPIES)), pltpu.SemaphoreType.DMA((n, kind.COPIES)),
            pltpu.SemaphoreType.DMA((n,))]
    if kind is Gather:
        ins = [pl.BlockSpec(memory_space=pltpu.VMEM)] * n
        outs = [pl.BlockSpec(memory_space=pl.ANY)] * n
        shapes = [jax.ShapeDtypeStruct((2, 2, 4, 2) + a.shape, a.dtype) for a in arrays]
        return ins, outs, shapes, sems
    ins = [pl.BlockSpec(memory_space=pl.ANY)] * n
    outs = [pl.BlockSpec(memory_space=pltpu.VMEM)] * n
    shapes = [jax.ShapeDtypeStruct(a.shape[4:], F32) for a in arrays]
    scratch = []
    for a in arrays:
        tail = a.shape[4:]
        for lead in ((2, 2, 4), (2, 2, 4), (2, 4), (4,), (3,)):
            scratch.append(pltpu.VMEM(lead + tail, a.dtype))
    return ins, outs, shapes, scratch + sems


def host_build(kind, ins, outs, scratch):
    me = Place()
    send, recv, local = scratch[-3:]
    jobs = []
    for i in range(len(ins)):
        extra = scratch[5 * i : 5 * i + 5] if kind is Scatter else ()
        jobs.append(kind(me, ins[i], outs[i], *extra, send.at[i], recv.at[i], local.at[i]))
    return me, jobs


def in_order(count, steps):
    return [(i, t - i) for t in range(count + steps - 1) for i in range(count) if 0 <= t - i < steps]


class Host:
    def __init__(self, kind=None, arrays=(), ident=None, plan=None, axis=1):
        self.kind, self.ident, self.plan, self.axis = kind, ident, plan, axis
        self.used = bool(arrays) and block_mesh()
        self.source = list(arrays)
        self.arrays, self.ins, self.outs, self.shapes, self.scratch = [], [], [], [], []
        if self.used:
            if kind is Scatter:
                arrays = [a.reshape(2, 2, 4, 2, -1, a.shape[-1]) for a in arrays]
            self.arrays = list(arrays)
            self.ins, self.outs, self.shapes, self.scratch = host_specs(kind, self.arrays)
        self.count = len(self.arrays)

    def params(self):
        if not self.used:
            return pltpu.CompilerParams(vmem_limit_bytes=48 << 20)
        return pltpu.CompilerParams(
            collective_id=self.ident, has_side_effects=True, vmem_limit_bytes=56 << 20)

    def enter(self, ins, outs, scratch):
        if not self.used:
            return None
        me, jobs = host_build(self.kind, ins, outs, scratch)
        now = pl.program_id(self.axis)

        @pl.when(now == 0)
        def _():
            me.greet()
            for job in jobs:
                job.run(0)

        for g, todo in enumerate(self.plan[:-1]):
            if todo:
                @pl.when(now == g)
                def _():
                    for i, t in todo:
                        jobs[i].run(t)

        return jobs

    def leave(self, jobs):
        if not self.used:
            return
        @pl.when(pl.program_id(self.axis) == len(self.plan) - 2)
        def _():
            for i, t in self.plan[-1]:
                jobs[i].run(t)

    def results(self, values):
        if self.used and self.kind is Gather:
            return [w.reshape(-1, w.shape[-1]) for w in values]
        if self.used:
            return list(values)
        return plain(self.kind, self.source)


def plain(kind, arrays):
    if kind is Gather:
        return [lax.all_gather(a, AX, axis=0, tiled=True) for a in arrays]
    return [lax.psum_scatter(t.astype(F32), AX, scatter_dimension=0, tiled=True) for t in arrays]


def alone_kernel(*refs, host):
    n = host.count
    jobs = host.enter(refs[:n], refs[n : 2 * n], refs[2 * n :])
    host.leave(jobs)


def exchange(kind, arrays, ident, name):
    steps = [e for e in in_order(len(arrays), kind.STEPS) if e[1] > 0]
    host = Host(kind, arrays, ident, [[], steps], axis=0)
    if not host.used:
        return plain(kind, arrays)
    return host.results(pl.pallas_call(
        functools.partial(alone_kernel, host=host), grid=(1,),
        in_specs=host.ins, out_specs=host.outs, out_shape=host.shapes, scratch_shapes=host.scratch,
        compiler_params=host.params(), name=name)(*host.arrays))


def layer_norm(values, gain, shift):
    centre = values - jnp.mean(values, axis=-1, keepdims=True)
    spread = jnp.mean(centre * centre, axis=-1, keepdims=True)
    return centre * lax.rsqrt(spread + EPS) * gain + shift


def inner_rows(left, right):
    return lax.dot_general(left, right, (((0,), (0,)), ((), ())), preferred_element_type=F32)


def times_transposed(left, right):
    return lax.dot_general(left, right, (((1,), (1,)), ((), ())), preferred_element_type=F32)


def column_sums(values):
    return jnp.sum(values.astype(F32), axis=0)


def gelu_pair(z):
    c = 0.7978845608028654
    t = jnp.tanh(c * (z + 0.044715 * z * z * z))
    value = 0.5 * z * (1.0 + t)
    slope = 0.5 * (1.0 + t) + 0.5 * z * (1.0 - t * t) * c * (1.0 + 3 * 0.044715 * z * z)
    return value.astype(BF), slope.astype(BF)


def pack_columns(vectors, wide, count):
    length = vectors[0].shape[0]
    ways = wide.shape[0] // length
    per = length // count
    spread = wide.reshape(count, ways, per).transpose(0, 2, 1).reshape(length, ways)
    block = jnp.concatenate([jnp.stack(vectors, axis=1), spread], axis=1)
    return jnp.pad(block, ((0, 0), (0, LANES - block.shape[1])))


def unpack_columns(block, vector_count, ways, count):
    length = block.shape[0]
    turned = block[:, : vector_count + ways].T
    wide = turned[vector_count:].reshape(ways, count, length // count).transpose(1, 0, 2).reshape(-1)
    return [turned[i] for i in range(vector_count)], wide


def local_shards(local):
    (ga, sa, hw, qb, vb, mw, mb, gf, sf, ew, eb, sw, sb) = local
    small = pack_columns([ga, sa, qb, vb, mb, gf, sf, sb], eb, 1)
    return [jnp.concatenate([hw, small], axis=1), mw, ew, sw]


def use_heads(heads, width, ways):
    vecs, wide = unpack_columns(heads[:, 3 * width :], 8, ways, lax.axis_size(AX))
    vecs = [v.astype(F32) for v in vecs]
    return dict(zip(("ga", "sa", "qb", "vb", "mb", "gf", "sf", "sb"), vecs), eb=wide.astype(F32),
                heads=heads[:, : 3 * width])


def forward_use(hidden, w, first_len, host):
    normed = layer_norm(hidden, w["ga"], w["sa"]).astype(BF)
    bias = jnp.concatenate([w["qb"], jnp.zeros_like(w["qb"]), w["vb"]])
    qkv = (jnp.dot(normed, w["heads"], preferred_element_type=F32) + bias).astype(BF)
    attended, lse, *more = attend_fwd(qkv, first_len, host)
    more = host.results(more)
    w.update(zip(("mix", "expand", "shrink"), more))
    middle = hidden + jnp.dot(attended, w["mix"], preferred_element_type=F32) + w["mb"]
    normed_two = layer_norm(middle, w["gf"], w["sf"]).astype(BF)
    expanded = jnp.dot(normed_two, w["expand"], preferred_element_type=F32) + w["eb"]
    activated, slope = gelu_pair(expanded)
    result = middle + jnp.dot(activated, w["shrink"], preferred_element_type=F32) + w["sb"]
    return result, (hidden, normed, qkv, attended, lse, middle, normed_two, activated, slope), more[3:]


def backward_use(grad_out, kept, w, first_len, carried, ident, plan):
    hidden, normed, qkv, attended, lse, middle, normed_two, activated, slope = kept
    count = lax.axis_size(AX)
    grad_low = grad_out.astype(BF)
    shrink_term = inner_rows(activated, grad_low).astype(BF)
    sb = column_sums(grad_low)
    dz = (times_transposed(grad_low, w["shrink"]) * slope.astype(F32)).astype(BF)
    expand_term = inner_rows(normed_two, dz).astype(BF)
    eb = column_sums(dz)
    dc = times_transposed(dz, w["expand"])
    unused, norm_back = jax.vjp(layer_norm, middle, w["gf"], w["sf"])
    middle_norm, gf, sf = norm_back(dc)
    dm = grad_out + middle_norm
    dmb = dm.astype(BF)
    mix_term = inner_rows(attended, dmb).astype(BF)
    mb = column_sums(dmb)
    do = times_transposed(dmb, w["mix"]).astype(BF)
    host = Host(Scatter, [shrink_term, expand_term, mix_term] + carried, ident, plan)
    dq, dk, dv, *more = attend_bwd(qkv, do, lse, first_len, host)
    more = host.results(more)
    dqkv = jnp.concatenate([dq, dk, dv], axis=1)
    heads_term = inner_rows(normed, dqkv).astype(BF)
    qb = column_sums(dq)
    vb = column_sums(dv)
    da = times_transposed(dqkv, w["heads"])
    unused, first_back = jax.vjp(layer_norm, hidden, w["ga"], w["sa"])
    hidden_norm, ga, sa = first_back(da)
    small = pack_columns([ga, sa, qb, vb, mb, gf, sf, sb], eb, count)
    return dm + hidden_norm, more, heads_term, small


def as_shares(shrink, expand, mix, heads, small):
    vecs, wide = unpack_columns(small, 8, shrink.shape[0] // heads.shape[0], 1)
    ga, sa, qb, vb, mb, gf, sf, sb = vecs
    return ga, sa, heads, qb, vb, mix, mb, gf, sf, expand, wide, shrink, sb


FORWARD_PLANS = (
    [[], [(0, 1)], [(0, 2)], [(0, 3)], [(1, 1)], [(1, 2), (0, 4)],
     [(2, 1), (1, 3), (3, 1), (2, 2), (3, 2), (2, 3), (3, 3), (1, 4), (2, 4), (3, 4)]],
    [[], [(0, 1)], [(0, 2)], [(0, 3)], [(1, 1)], [(1, 2), (0, 4)],
     [(2, 1), (1, 3), (2, 2), (2, 3), (1, 4), (2, 4)]],
)
BACKWARD_PLANS = (
    [[], [(0, 1)], [(1, 1)], [(2, 1)], [(0, 2)], [(1, 2)],
     [(0, 3), (2, 2), (1, 3), (2, 3), (0, 4), (1, 4), (2, 4)]],
    [[], [(0, 1)], [(1, 1)], [(3, 1), (2, 1)], [(0, 2)], [(1, 2)],
     [(0, 3), (3, 2), (2, 2), (1, 3), (3, 3), (2, 3), (0, 4), (1, 4), (3, 4), (2, 4)]],
)


def pick_shards(stacks, source):
    return tuple(lax.dynamic_index_in_dim(stack, source, 0, keepdims=False) for stack in stacks)


def place_terms(sources, shares):
    ids = lax.iota(jnp.int32, UNIQUE)
    out = []
    for items in zip(*shares):
        total = 0.0
        for source, item in zip(sources, items):
            chosen = (ids == source).reshape((UNIQUE,) + (1,) * item.ndim)
            total = total + jnp.where(chosen, item[None], 0.0)
        out.append(total)
    return out


def body(tokens, cotangent, tie_map, first_length, *stacks):
    hidden = tokens.astype(F32)
    width = hidden.shape[1]
    sources = [tie_map[i] for i in range(LAYERS)]
    shards = [local_shards(pick_shards(stacks, s)) for s in sources]
    ways = shards[0][3].shape[0] // shards[0][0].shape[0]
    (heads,) = exchange(Gather, shards[0][:1], 0, "gather")
    kept, weights = [], []
    loads = [shards[0][1:] + shards[1][:1], shards[1][1:]]
    for i in range(LAYERS):
        weights.append(use_heads(heads, width, ways))
        host = Host(Gather, loads[i], 1 + i, FORWARD_PLANS[i])
        hidden, saved, spare = forward_use(hidden, weights[i], first_length, host)
        heads = spare[0] if spare else None
        kept.append(saved)
    grad = cotangent.astype(F32)
    grad, late, heads_late, small_late = backward_use(
        grad, kept[1], weights[1], first_length, [], 3, BACKWARD_PLANS[0])
    grad, early, heads_early, small_early = backward_use(
        grad, kept[0], weights[0], first_length, [heads_late], 4, BACKWARD_PLANS[1])
    heads_early, small = exchange(
        Scatter, [heads_early, jnp.concatenate([small_early, small_late], axis=1)], 5, "scatter")
    shares = [as_shares(*early[:3], heads_early, small[:, :LANES]),
              as_shares(*late, early[3], small[:, LANES:])]
    return (hidden.astype(BF), grad.astype(BF), *place_terms(sources, shares))


def solution(mesh):
    rows = P(AX, None)
    flat = P(None, AX)
    deep = P(None, AX, None)
    weights = (flat, flat, deep, flat, flat, deep, flat, flat, flat, deep, flat, deep, flat)
    return jax.shard_map(
        body,
        mesh=mesh,
        in_specs=(rows, rows, P(), P(AX)) + weights,
        out_specs=(rows, rows) + weights,
        check_vma=False,
    )
```

```python
import functools

import jax
import jax.numpy as jnp
from jax import lax
from jax.experimental import pallas as pl
from jax.experimental.pallas import tpu as pltpu
from jax.sharding import PartitionSpec as P

LAYERS = 2
UNIQUE = 4
F32 = jnp.float32
BF = jnp.bfloat16
AX = ("dp", "fsdp")
LANES = 128
EPS = 1e-05

NEG=-1e9
def nt(a,b): return lax.dot_general(a,b,(((1,),(1,)),((),())),preferred_element_type=F32)
def nn(a,b): return lax.dot_general(a,b,(((1,),(0,)),((),())),preferred_element_type=F32)
def halves(x):
    lane=lax.broadcasted_iota(jnp.int32,x.shape,1)
    z=jnp.zeros_like(x)
    return jnp.where(lane<64,x,z), jnp.where(lane<64,z,x)

def fwd_kernel(fl_ref,q_ref,k_ref,v_ref,*rest,bq,host):
    n=host.count
    o_ref,lse_ref=rest[n:n+2]
    jobs=host.enter(rest[:n],rest[n+2:2*n+2],rest[2*n+2:])
    L=q_ref.shape[0]; half=L//2
    second=fl_ref[pl.program_id(0)]<L
    shut=jnp.where(second,F32(1e9),F32(0.))
    q=q_ref[...]*BF(0.125); k=k_ref[...]; vT=v_ref[...].T
    sub=lax.broadcasted_iota(jnp.int32,vT.shape,0)
    zero=jnp.zeros_like(vT)
    vTs=(jnp.where(sub<64,vT,zero),jnp.where(sub<64,zero,vT))
    qs=halves(q)
    tri=lax.broadcasted_iota(jnp.int32,(bq,bq),0)<=lax.broadcasted_iota(jnp.int32,(bq,bq),1)
    for j in range(L//bq):
        host.tick(jobs,j)
        lo=j*bq; hi=lo+bq
        acc=jnp.zeros((128,bq),F32)
        for h in range(2):
            qh=qs[h][lo:hi]
            s=nt(k[:hi],qh)
            parts=[]
            if lo>0 : parts.append((0,min(lo,half),s[:min(lo,half)]))
            if lo>half: parts.append((half,lo,s[half:lo]))
            diag=jnp.where(tri,s[lo:],NEG)
            m=jnp.max(diag,axis=0,keepdims=True)
            for a,b,t in parts:
                mt=jnp.max(t,axis=0,keepdims=True)
                if lo>=half and a==0: mt=mt-shut
                m=jnp.maximum(m,mt)
            ps=[]; l=0.
            for a,b,t in parts+[(lo,hi,diag)]:
                mm=m+shut if (lo>=half and a==0) else m
                p=jnp.exp(t-mm)
                l=l+jnp.sum(p,axis=0,keepdims=True)
                ps.append(p.astype(BF))
            p=jnp.concatenate(ps,axis=0) if len(ps)>1 else ps[0]
            oh=nn(vTs[h][:,:hi],p)
            acc=acc+oh*(1.0/l)
            lse_ref[0,h:h+1,lo:hi]=m+jnp.log(l)
        o_ref[lo:hi,:]=acc.T.astype(BF)
    host.leave(jobs)

def attend_fwd(qkv,fl,host,bq=256):
    N,C=qkv.shape; R=fl.shape[0]; L=N//R; D=C//3; G=D//128
    return pl.pallas_call(functools.partial(fwd_kernel,bq=bq,host=host),
        grid_spec=pltpu.PrefetchScalarGridSpec(num_scalar_prefetch=1,grid=(R,G),
          in_specs=[pl.BlockSpec((L,128),lambda r,g,fl:(r,g)),
                    pl.BlockSpec((L,128),lambda r,g,fl:(r,G+g)),
                    pl.BlockSpec((L,128),lambda r,g,fl:(r,2*G+g))]+host.ins,
          out_specs=[pl.BlockSpec((L,128),lambda r,g,fl:(r,g)),
                     pl.BlockSpec((1,2,L),lambda r,g,fl:(r*G+g,0,0))]+host.outs,
          scratch_shapes=host.scratch),
        out_shape=[jax.ShapeDtypeStruct((N,D),BF),jax.ShapeDtypeStruct((R*G,2,L),F32)]+host.shapes,
        compiler_params=host.params(),
        cost_estimate=pl.CostEstimate(flops=2*2*R*L*L*D*2,bytes_accessed=N*D*8,transcendentals=R*L*L*12//2),
        name="attend_fwd")(fl,qkv,qkv,qkv,*host.arrays)

def bwd_kernel(fl_ref,q_ref,k_ref,v_ref,do_ref,lse_ref,*rest,bq,host):
    n=host.count
    dq_ref,dk_ref,dv_ref=rest[n:n+3]
    dk_acc,dv_acc=rest[2*n+3:2*n+5]
    jobs=host.enter(rest[:n],rest[n+3:2*n+3],rest[2*n+5:])
    L=q_ref.shape[0]; half=L//2
    second=fl_ref[pl.program_id(0)]<L
    shut=jnp.where(second,F32(1e9),F32(0.))
    q=q_ref[...]*BF(0.125); k=k_ref[...]; v=v_ref[...]; do=do_ref[...]
    kT=k.T
    sub=lax.broadcasted_iota(jnp.int32,kT.shape,0); zero=jnp.zeros_like(kT)
    kTs=(jnp.where(sub<64,kT,zero),jnp.where(sub<64,zero,kT))
    qs=halves(q); dos=halves(do)
    tri=lax.broadcasted_iota(jnp.int32,(bq,bq),0)<=lax.broadcasted_iota(jnp.int32,(bq,bq),1)
    nb=L//bq
    for j in reversed(range(nb)):
        host.tick(jobs,nb-1-j)
        lo=j*bq; hi=lo+bq
        dqT=jnp.zeros((128,bq),F32)
        dkp=None; dvp=None
        for h in range(2):
            qh=qs[h][lo:hi]; doh=dos[h][lo:hi]
            lse=lse_ref[0,h:h+1,lo:hi]
            s=nt(k[:hi],qh)
            dp=nt(v[:hi],doh)
            ps=[];
            cuts=[]
            if lo>0: cuts.append((0,min(lo,half)))
            if lo>half: cuts.append((half,lo))
            cuts.append((lo,hi))
            for a,b in cuts:
                ll=lse+shut if (lo>=half and b<=half) else lse
                t=s[a:b]-ll
                if a==lo: t=jnp.where(tri,t,NEG)
                ps.append(jnp.exp(t))
            p=jnp.concatenate(ps,axis=0) if len(ps)>1 else ps[0]
            delta=jnp.sum(p*dp,axis=0,keepdims=True)
            ds=(p*(dp-delta)).astype(BF)
            pb=p.astype(BF)
            dv_=nn(pb,doh); dk_=nn(ds,qh)
            dvp=dv_ if dvp is None else dvp+dv_
            dkp=dk_ if dkp is None else dkp+dk_
            dqT=dqT+nn(kTs[h][:,:hi],ds)
        if j==nb-1:
            dk_acc[...]=dkp; dv_acc[...]=dvp
        else:
            dk_acc[:hi]+=dkp; dv_acc[:hi]+=dvp
        dq_ref[lo:hi,:]=(dqT.T*0.125).astype(BF)
    dk_ref[...]=dk_acc[...].astype(BF); dv_ref[...]=dv_acc[...].astype(BF)
    host.leave(jobs)

def attend_bwd(qkv,do,lse,fl,host,bq=256):
    N,C=qkv.shape; R=fl.shape[0]; L=N//R; D=C//3; G=D//128
    blk=lambda off: pl.BlockSpec((L,128),lambda r,g,fl:(r,off*G+g))
    return pl.pallas_call(functools.partial(bwd_kernel,bq=bq,host=host),
        grid_spec=pltpu.PrefetchScalarGridSpec(num_scalar_prefetch=1,grid=(R,G),
          in_specs=[blk(0),blk(1),blk(2),blk(0),pl.BlockSpec((1,2,L),lambda r,g,fl:(r*G+g,0,0))]+host.ins,
          out_specs=[blk(0),blk(0),blk(0)]+host.outs,
          scratch_shapes=[pltpu.VMEM((L,128),F32),pltpu.VMEM((L,128),F32)]+host.scratch),
        out_shape=[jax.ShapeDtypeStruct((N,D),BF)]*3+host.shapes,
        compiler_params=host.params(),
        cost_estimate=pl.CostEstimate(flops=5*2*R*L*L*D*2,bytes_accessed=N*D*16,transcendentals=R*L*L*12//2),
        name="attend_bwd")(fl,qkv,qkv,qkv,do,lse,*host.arrays)


MESH = pl.DeviceIdType.MESH


def block_mesh():
    return lax.axis_size("dp") == 4 and lax.axis_size("fsdp") == 8


class Place:
    def __init__(self):
        d = lax.axis_index("dp")
        f = lax.axis_index("fsdp")
        self.y, self.x = lax.div(d, 2), lax.rem(d, 2)
        self.z, self.c = lax.div(f, 2), lax.rem(f, 2)
        self.zs = [self.z + 1 - 2 * lax.rem(self.z, 2), lax.rem(self.z + 2, 4), 3 - self.z]
        self.to_core = (d, 2 * self.z + 1 - self.c)
        self.to_x = (2 * self.y + 1 - self.x, f)
        self.to_y = (2 * (1 - self.y) + self.x, f)
        self.to_z = [(d, 2 * zz + self.c) for zz in self.zs]

    def greet(self):
        barrier = pltpu.get_barrier_semaphore()
        peers = [self.to_core, self.to_x, self.to_y] + self.to_z
        for peer in peers:
            pl.semaphore_signal(barrier, inc=1, device_id=peer, device_id_type=MESH)
        pl.semaphore_wait(barrier, len(peers))


ALL = slice(None)


class Gather:
    COPIES = 8
    STEPS = 5
    LINKS = ((("z", 8), ), (("first", 8), ("core", 4)), (("second", 16), ("core", 4)), (("core", 8), ))

    def __init__(self, me, shard, out, scratch, cols, x_first, send, recv, local):
        self.send, self.recv = send, recv
        y, x, z, c = me.y, me.x, me.z, me.c
        cols = pl.ds(*cols)
        o = out.at
        mine = o[y, x, z, c, :, cols]
        self.shard = shard.at[:, cols]
        self.own = pltpu.make_async_copy(self.shard, mine, local)
        if x_first:
            links, far, near, rest = (me.to_x, me.to_y), (y, ALL), (y, 1 - x), (1 - y, ALL)
        else:
            links, far, near, rest = (me.to_y, me.to_x), (ALL, x), (1 - y, x), (ALL, 1 - x)
        tail = (ALL, c, ALL, cols)
        self.plan = [(me.to_z[k], mine) for k in range(3)] + [
            (links[0], o[(y, x) + tail]), (links[1], o[far + tail]), (me.to_core, o[(y, x) + tail]),
            (me.to_core, o[near + tail]), (me.to_core, o[rest + tail])]

    def copy(self, k):
        peer, ref = self.plan[k]
        return pltpu.make_async_remote_copy(
            src_ref=self.shard if k < 3 else ref, dst_ref=ref, send_sem=self.send.at[k],
            recv_sem=self.recv.at[k], device_id=peer, device_id_type=MESH)

    def run(self, step):
        waits, starts = [
            ((), (0, 1, 2)), ((0, 1, 2), (3, 5)), ((3,), (4, 6)), ((4,), (7,)), ((5, 6, 7), ())][step]
        if step == 0:
            self.own.start()
        for k in waits:
            self.copy(k).wait_recv()
        if step == 1:
            self.own.wait()
        for k in starts:
            self.copy(k).start()
        if step == 4:
            for k in range(8):
                self.copy(k).wait_send()


class Scatter:
    COPIES = 6
    STEPS = 5
    LINKS = ((("core", 16), ), (("first", 16), ), (("second", 8), ), (("z", 8), ))

    def __init__(self, me, term, out, scratch, cols, x_first, send, recv, local):
        self.me, self.out = me, out
        self.own, self.r = scratch[0], scratch[1:]
        self.send, self.recv = send, recv
        self.cols, self.x_first = pl.ds(*cols), x_first
        own, (r0, r1, r2, r3) = self.own, self.r
        y, x, z, c = me.y, me.x, me.z, me.c
        self.mine = pltpu.make_async_copy(term.at[ALL, ALL, ALL, c, :, self.cols], own, local)
        if x_first:
            pair = [(own.at[ALL, 1 - x], me.to_x, r1), (own.at[1 - y, x], me.to_y, r2)]
        else:
            pair = [(own.at[1 - y], me.to_y, r1), (own.at[y, 1 - x], me.to_x, r2)]
        self.plan = [(term.at[ALL, ALL, ALL, 1 - c, :, self.cols], me.to_core, r0)] + pair + [
            (own.at[y, x, me.zs[k]], me.to_z[k], r3.at[k]) for k in range(3)]

    def copy(self, k):
        src, peer, dst = self.plan[k]
        return pltpu.make_async_remote_copy(
            src_ref=src, dst_ref=dst, send_sem=self.send.at[k], recv_sem=self.recv.at[k],
            device_id=peer, device_id_type=MESH)

    def run(self, step):
        y, x, z = self.me.y, self.me.x, self.me.z
        own, (r0, r1, r2, r3) = self.own, self.r
        if step == 0:
            self.mine.start()
            self.copy(0).start()
        elif step == 1:
            self.mine.wait()
            self.copy(0).wait_recv()

            @pl.loop(0, 4)
            def _(k):
                for a in range(2):
                    for b in range(2):
                        own[a, b, k] = own[a, b, k] + r0[a, b, k]

            self.copy(1).start()
        elif step == 2:
            self.copy(1).wait_recv()

            @pl.loop(0, 4)
            def _(k):
                for a in range(2):
                    if self.x_first:
                        own[a, x, k] = own[a, x, k] + r1[a, k]
                    else:
                        own[y, a, k] = own[y, a, k] + r1[a, k]

            self.copy(2).start()
        elif step == 3:
            self.copy(2).wait_recv()

            @pl.loop(0, 4)
            def _(k):
                own[y, x, k] = own[y, x, k] + r2[k]

            for k in (3, 4, 5):
                self.copy(k).start()
        else:
            total = own[y, x, z].astype(F32)
            for k in (3, 4, 5):
                self.copy(k).wait_recv()
                total = total + r3[k - 3].astype(F32)
            self.out[:, self.cols] = total
            for k in range(6):
                self.copy(k).wait_send()


def cut_jobs(arrays, kind, pieces):
    jobs = []
    for i, a in enumerate(arrays):
        units = a.shape[-1] // 128
        n = min(pieces, units)
        start = 0
        for k in range(n):
            width = 128 * (units // n + (1 if k < units % n else 0))
            jobs.append((i, (start, width), len(jobs) % 2 == 0))
            start += width
    return jobs


def plan_jobs(kind, jobs, rows, slots):
    free = dict.fromkeys("xyzc", 0.0)
    ready = {}

    def start(i, step, now):
        array, (unused, width), x_first = jobs[i]
        done = now
        names = {"z": "z", "core": "c", "first": "x" if x_first else "y", "second": "y" if x_first else "x"}
        if step < len(kind.LINKS):
            for link, blocks in kind.LINKS[step]:
                name = names[link]
                rate = 500e3 if name == "c" else 88e3
                free[name] = max(free[name], now) + blocks * rows[array] * width * 2 / rate
                if not (kind is Gather and name == "c" and step < 3):
                    done = max(done, free[name])
        if step < kind.STEPS - 1:
            ready[i, step + 1] = done + 1.8

    for i in range(len(jobs)):
        start(i, 0, 0.0)
    now, plan = 0.0, []
    cost = 0.1 if kind is Gather else 0.5
    for length in slots:
        todo = []
        while True:
            can = sorted((e for e in ready if ready[e] <= now and e[1] < kind.STEPS - 1), key=lambda e: (-e[1], e[0]))
            if not can:
                break
            ready.pop(can[0])
            now += cost
            start(*can[0], now)
            todo.append(can[0])
        plan.append(todo)
        now += length
    todo = []
    while ready:
        e = min(ready, key=lambda e: (max(ready[e], now), -e[1], e[0]))
        now = max(ready.pop(e), now) + cost
        start(*e, now)
        todo.append(e)
    return plan + [todo]


class Host:
    def __init__(self, kind=None, arrays=(), ident=None, slots=(), per=1, axis=1, pieces=2):
        self.kind, self.ident, self.per, self.axis = kind, ident, per, axis
        self.used = bool(arrays) and block_mesh()
        self.source = list(arrays)
        self.arrays, self.ins, self.outs, self.shapes, self.scratch = [], [], [], [], []
        if self.used:
            self.build(arrays, slots, pieces)
        self.count = len(self.arrays)

    def build(self, arrays, slots, pieces):
        kind = self.kind
        if kind is Scatter:
            arrays = [a.reshape(2, 2, 4, 2, -1, a.shape[-1]) for a in arrays]
        self.arrays = arrays = list(arrays)
        n = len(arrays)
        self.jobs = jobs = cut_jobs(arrays, kind, pieces)
        rows = [a.shape[-2] * a.dtype.itemsize // 2 for a in arrays]
        self.plan = plan_jobs(kind, jobs, rows, slots)
        m = len(jobs)
        any_space, vmem = pl.BlockSpec(memory_space=pl.ANY), pl.BlockSpec(memory_space=pltpu.VMEM)
        if kind is Gather:
            self.ins, self.outs = [vmem] * n, [any_space] * n
            self.shapes = [jax.ShapeDtypeStruct((2, 2, 4, 2) + a.shape, a.dtype) for a in arrays]
        else:
            self.ins, self.outs = [any_space] * n, [vmem] * n
            self.shapes = [jax.ShapeDtypeStruct(a.shape[4:], F32) for a in arrays]
            for i, (unused, width), unused in jobs:
                for lead in ((2, 2, 4), (2, 2, 4), (2, 4), (4,), (3,)):
                    self.scratch.append(pltpu.VMEM(lead + (arrays[i].shape[-2], width), arrays[i].dtype))
        self.scratch = self.scratch + [
            pltpu.SemaphoreType.DMA((m, kind.COPIES)), pltpu.SemaphoreType.DMA((m, kind.COPIES)),
            pltpu.SemaphoreType.DMA((m,))]

    def params(self):
        if not self.used:
            return pltpu.CompilerParams(vmem_limit_bytes=48 << 20)
        return pltpu.CompilerParams(
            collective_id=self.ident, has_side_effects=True, vmem_limit_bytes=56 << 20)

    def enter(self, ins, outs, scratch):
        if not self.used:
            return None
        me = Place()
        send, recv, local = scratch[-3:]
        work = []
        for k, (i, cols, x_first) in enumerate(self.jobs):
            own = scratch[5 * k : 5 * k + 5] if self.kind is Scatter else ()
            work.append(self.kind(me, ins[i], outs[i], own, cols, x_first, send.at[k], recv.at[k], local.at[k]))
        self.now = pl.program_id(self.axis)

        @pl.when(self.now == 0)
        def _():
            me.greet()
            for job in work:
                job.run(0)

        return work

    def tick(self, work, at):
        if not self.used:
            return
        for g in range((len(self.plan) - 1) // self.per):
            todo = self.plan[g * self.per + at]
            if todo:
                @pl.when(self.now == g)
                def _():
                    for i, t in todo:
                        work[i].run(t)

    def leave(self, work):
        if not self.used:
            return

        @pl.when(self.now == (len(self.plan) - 1) // self.per - 1)
        def _():
            for i, t in self.plan[-1]:
                work[i].run(t)

    def results(self, values):
        if self.used and self.kind is Gather:
            return [w.reshape(-1, w.shape[-1]) for w in values]
        if self.used:
            return list(values)
        return plain(self.kind, self.source)


def plain(kind, arrays):
    if kind is Gather:
        return [lax.all_gather(a, AX, axis=0, tiled=True) for a in arrays]
    return [lax.psum_scatter(t.astype(F32), AX, scatter_dimension=0, tiled=True) for t in arrays]


def alone_kernel(*refs, host):
    n = host.count
    jobs = host.enter(refs[:n], refs[n : 2 * n], refs[2 * n :])
    host.leave(jobs)


def exchange(kind, arrays, ident, name, pieces):
    host = Host(kind, arrays, ident, [0.0], axis=0, pieces=pieces)
    if not host.used:
        return plain(kind, arrays)
    return host.results(pl.pallas_call(
        functools.partial(alone_kernel, host=host), grid=(1,),
        in_specs=host.ins, out_specs=host.outs, out_shape=host.shapes, scratch_shapes=host.scratch,
        compiler_params=host.params(), name=name)(*host.arrays))


def layer_norm(values, gain, shift):
    centre = values - jnp.mean(values, axis=-1, keepdims=True)
    spread = jnp.mean(centre * centre, axis=-1, keepdims=True)
    return centre * lax.rsqrt(spread + EPS) * gain + shift


def inner_rows(left, right):
    return lax.dot_general(left, right, (((0,), (0,)), ((), ())), preferred_element_type=F32)


def times_transposed(left, right):
    return lax.dot_general(left, right, (((1,), (1,)), ((), ())), preferred_element_type=F32)


def column_sums(values):
    return jnp.sum(values.astype(F32), axis=0)


def gelu_pair(z):
    c = 0.7978845608028654
    t = jnp.tanh(c * (z + 0.044715 * z * z * z))
    value = 0.5 * z * (1.0 + t)
    slope = 0.5 * (1.0 + t) + 0.5 * z * (1.0 - t * t) * c * (1.0 + 3 * 0.044715 * z * z)
    return value.astype(BF), slope.astype(BF)


def pack_columns(vectors, wide, count):
    length = vectors[0].shape[0]
    ways = wide.shape[0] // length
    per = length // count
    spread = wide.reshape(count, ways, per).transpose(0, 2, 1).reshape(length, ways)
    block = jnp.concatenate([jnp.stack(vectors, axis=1), spread], axis=1)
    return jnp.pad(block, ((0, 0), (0, LANES - block.shape[1])))


def unpack_columns(block, vector_count, ways, count):
    length = block.shape[0]
    turned = block[:, : vector_count + ways].T
    wide = turned[vector_count:].reshape(ways, count, length // count).transpose(1, 0, 2).reshape(-1)
    return [turned[i] for i in range(vector_count)], wide


def local_shards(local):
    (ga, sa, hw, qb, vb, mw, mb, gf, sf, ew, eb, sw, sb) = local
    small = pack_columns([ga, sa, qb, vb, mb, gf, sf, sb], eb, 1)
    return [jnp.concatenate([hw, small], axis=1), mw, ew, sw]


def use_heads(heads, width, ways):
    vecs, wide = unpack_columns(heads[:, 3 * width :], 8, ways, lax.axis_size(AX))
    vecs = [v.astype(F32) for v in vecs]
    return dict(zip(("ga", "sa", "qb", "vb", "mb", "gf", "sf", "sb"), vecs), eb=wide.astype(F32),
                heads=heads[:, : 3 * width])


def forward_use(hidden, w, first_len, host):
    normed = layer_norm(hidden, w["ga"], w["sa"]).astype(BF)
    bias = jnp.concatenate([w["qb"], jnp.zeros_like(w["qb"]), w["vb"]])
    qkv = (jnp.dot(normed, w["heads"], preferred_element_type=F32) + bias).astype(BF)
    attended, lse, *more = attend_fwd(qkv, first_len, host)
    more = host.results(more)
    w.update(expand=more[0], shrink=more[1], mix=more[-1])
    middle = hidden + jnp.dot(attended, w["mix"], preferred_element_type=F32) + w["mb"]
    normed_two = layer_norm(middle, w["gf"], w["sf"]).astype(BF)
    expanded = jnp.dot(normed_two, w["expand"], preferred_element_type=F32) + w["eb"]
    activated, slope = gelu_pair(expanded)
    result = middle + jnp.dot(activated, w["shrink"], preferred_element_type=F32) + w["sb"]
    return result, (hidden, normed, qkv, attended, lse, middle, normed_two, activated, slope), more[2:-1]


def backward_use(grad_out, kept, w, first_len, carried, ident):
    hidden, normed, qkv, attended, lse, middle, normed_two, activated, slope = kept
    count = lax.axis_size(AX)
    grad_low = grad_out.astype(BF)
    shrink_term = inner_rows(activated, grad_low).astype(BF)
    sb = column_sums(grad_low)
    dz = (times_transposed(grad_low, w["shrink"]) * slope.astype(F32)).astype(BF)
    expand_term = inner_rows(normed_two, dz).astype(BF)
    eb = column_sums(dz)
    dc = times_transposed(dz, w["expand"])
    unused, norm_back = jax.vjp(layer_norm, middle, w["gf"], w["sf"])
    middle_norm, gf, sf = norm_back(dc)
    dm = grad_out + middle_norm
    dmb = dm.astype(BF)
    mix_term = inner_rows(attended, dmb).astype(BF)
    mb = column_sums(dmb)
    do = times_transposed(dmb, w["mix"]).astype(BF)
    host = Host(Scatter, [shrink_term, expand_term] + carried + [mix_term], ident, BACKWARD_SLOTS, per=4)
    dq, dk, dv, *more = attend_bwd(qkv, do, lse, first_len, host)
    more = host.results(more)
    dqkv = jnp.concatenate([dq, dk, dv], axis=1)
    heads_term = inner_rows(normed, dqkv).astype(BF)
    qb = column_sums(dq)
    vb = column_sums(dv)
    da = times_transposed(dqkv, w["heads"])
    unused, first_back = jax.vjp(layer_norm, hidden, w["ga"], w["sa"])
    hidden_norm, ga, sa = first_back(da)
    small = pack_columns([ga, sa, qb, vb, mb, gf, sf, sb], eb, count)
    return dm + hidden_norm, more, heads_term, small


def as_shares(shrink, expand, mix, heads, small):
    vecs, wide = unpack_columns(small, 8, shrink.shape[0] // heads.shape[0], 1)
    ga, sa, qb, vb, mb, gf, sf, sb = vecs
    return ga, sa, heads, qb, vb, mix, mb, gf, sf, expand, wide, shrink, sb


FORWARD_SLOTS = [0.43, 0.86, 1.29, 1.72] * 6
BACKWARD_SLOTS = [1.8, 1.35, 0.9, 0.45] * 6


def pick_shards(stacks, source):
    return tuple(lax.dynamic_index_in_dim(stack, source, 0, keepdims=False) for stack in stacks)


def place_terms(sources, shares):
    ids = lax.iota(jnp.int32, UNIQUE)
    out = []
    for items in zip(*shares):
        total = 0.0
        for source, item in zip(sources, items):
            chosen = (ids == source).reshape((UNIQUE,) + (1,) * item.ndim)
            total = total + jnp.where(chosen, item[None], 0.0)
        out.append(total)
    return out


def body(tokens, cotangent, tie_map, first_length, *stacks):
    hidden = tokens.astype(F32)
    width = hidden.shape[1]
    sources = [tie_map[i] for i in range(LAYERS)]
    shards = [local_shards(pick_shards(stacks, s)) for s in sources]
    ways = shards[0][3].shape[0] // shards[0][0].shape[0]
    (heads,) = exchange(Gather, shards[0][:1], 0, "gather", 4)
    kept, weights = [], []
    loads = [shards[0][2:] + shards[1][:1] + shards[0][1:2], shards[1][2:] + shards[1][1:2]]
    for i in range(LAYERS):
        weights.append(use_heads(heads, width, ways))
        host = Host(Gather, loads[i], 1 + i, FORWARD_SLOTS, per=4)
        hidden, saved, spare = forward_use(hidden, weights[i], first_length, host)
        heads = spare[0] if spare else None
        kept.append(saved)
    grad = cotangent.astype(F32)
    grad, late, heads_late, small_late = backward_use(
        grad, kept[1], weights[1], first_length, [], 3)
    grad, early, heads_early, small_early = backward_use(
        grad, kept[0], weights[0], first_length, [heads_late], 4)
    heads_early, small = exchange(
        Scatter, [heads_early, jnp.concatenate([small_early, small_late], axis=1)], 5, "scatter", 4)
    shares = [as_shares(early[0], early[1], early[3], heads_early, small[:, :LANES]),
              as_shares(*late, early[2], small[:, LANES:])]
    return (hidden.astype(BF), grad.astype(BF), *place_terms(sources, shares))


def solution(mesh):
    rows = P(AX, None)
    flat = P(None, AX)
    deep = P(None, AX, None)
    weights = (flat, flat, deep, flat, flat, deep, flat, flat, flat, deep, flat, deep, flat)
    return jax.shard_map(
        body,
        mesh=mesh,
        in_specs=(rows, rows, P(), P(AX)) + weights,
        out_specs=(rows, rows) + weights,
        check_vma=False,
    )
```

```python
import functools

import jax
import jax.numpy as jnp
from jax import lax
from jax.experimental import pallas as pl
from jax.experimental.pallas import tpu as pltpu
from jax.sharding import PartitionSpec as P

LAYERS = 2
UNIQUE = 4
F32 = jnp.float32
BF = jnp.bfloat16
AX = ("dp", "fsdp")
LANES = 128
EPS = 1e-05

NEG=-1e9
def nt(a,b): return lax.dot_general(a,b,(((1,),(1,)),((),())),preferred_element_type=F32)
def nn(a,b): return lax.dot_general(a,b,(((1,),(0,)),((),())),preferred_element_type=F32)
def halves(x):
    lane=lax.broadcasted_iota(jnp.int32,x.shape,1)
    z=jnp.zeros_like(x)
    return jnp.where(lane<64,x,z), jnp.where(lane<64,z,x)

def fwd_kernel(fl_ref,q_ref,k_ref,v_ref,*rest,bq,host):
    n=host.count
    o_ref,lse_ref=rest[n:n+2]
    jobs=host.enter(rest[:n],rest[n+2:2*n+2],rest[2*n+2:])
    L=q_ref.shape[0]; half=L//2
    second=fl_ref[pl.program_id(0)]<L
    shut=jnp.where(second,F32(1e9),F32(0.))
    q=q_ref[...]*BF(0.125); k=k_ref[...]; vT=v_ref[...].T
    sub=lax.broadcasted_iota(jnp.int32,vT.shape,0)
    zero=jnp.zeros_like(vT)
    vTs=(jnp.where(sub<64,vT,zero),jnp.where(sub<64,zero,vT))
    qs=halves(q)
    tri=lax.broadcasted_iota(jnp.int32,(bq,bq),0)<=lax.broadcasted_iota(jnp.int32,(bq,bq),1)
    for j in range(L//bq):
        host.tick(jobs,j)
        lo=j*bq; hi=lo+bq
        acc=jnp.zeros((128,bq),F32)
        for h in range(2):
            qh=qs[h][lo:hi]
            s=nt(k[:hi],qh)
            parts=[]
            if lo>0 : parts.append((0,min(lo,half),s[:min(lo,half)]))
            if lo>half: parts.append((half,lo,s[half:lo]))
            diag=jnp.where(tri,s[lo:],NEG)
            m=jnp.max(diag,axis=0,keepdims=True)
            for a,b,t in parts:
                mt=jnp.max(t,axis=0,keepdims=True)
                if lo>=half and a==0: mt=mt-shut
                m=jnp.maximum(m,mt)
            ps=[]; l=0.
            for a,b,t in parts+[(lo,hi,diag)]:
                mm=m+shut if (lo>=half and a==0) else m
                p=jnp.exp(t-mm)
                l=l+jnp.sum(p,axis=0,keepdims=True)
                ps.append(p.astype(BF))
            p=jnp.concatenate(ps,axis=0) if len(ps)>1 else ps[0]
            oh=nn(vTs[h][:,:hi],p)
            acc=acc+oh*(1.0/l)
            lse_ref[0,h:h+1,lo:hi]=m+jnp.log(l)
        o_ref[lo:hi,:]=acc.T.astype(BF)
    host.leave(jobs)

def attend_fwd(qkv,fl,host,bq=256):
    N,C=qkv.shape; R=fl.shape[0]; L=N//R; D=C//3; G=D//128
    return pl.pallas_call(functools.partial(fwd_kernel,bq=bq,host=host),
        grid_spec=pltpu.PrefetchScalarGridSpec(num_scalar_prefetch=1,grid=(R,G),
          in_specs=[pl.BlockSpec((L,128),lambda r,g,fl:(r,g)),
                    pl.BlockSpec((L,128),lambda r,g,fl:(r,G+g)),
                    pl.BlockSpec((L,128),lambda r,g,fl:(r,2*G+g))]+host.ins,
          out_specs=[pl.BlockSpec((L,128),lambda r,g,fl:(r,g)),
                     pl.BlockSpec((1,2,L),lambda r,g,fl:(r*G+g,0,0))]+host.outs,
          scratch_shapes=host.scratch),
        out_shape=[jax.ShapeDtypeStruct((N,D),BF),jax.ShapeDtypeStruct((R*G,2,L),F32)]+host.shapes,
        compiler_params=host.params(),
        cost_estimate=pl.CostEstimate(flops=2*2*R*L*L*D*2,bytes_accessed=N*D*8,transcendentals=R*L*L*12//2),
        name="attend_fwd")(fl,qkv,qkv,qkv,*host.arrays)

def bwd_kernel(fl_ref,q_ref,k_ref,v_ref,do_ref,lse_ref,*rest,bq,host):
    n=host.count
    dq_ref,dk_ref,dv_ref=rest[n:n+3]
    dk_acc,dv_acc=rest[2*n+3:2*n+5]
    jobs=host.enter(rest[:n],rest[n+3:2*n+3],rest[2*n+5:])
    L=q_ref.shape[0]; half=L//2
    second=fl_ref[pl.program_id(0)]<L
    shut=jnp.where(second,F32(1e9),F32(0.))
    q=q_ref[...]*BF(0.125); k=k_ref[...]; v=v_ref[...]; do=do_ref[...]
    kT=k.T
    sub=lax.broadcasted_iota(jnp.int32,kT.shape,0); zero=jnp.zeros_like(kT)
    kTs=(jnp.where(sub<64,kT,zero),jnp.where(sub<64,zero,kT))
    qs=halves(q); dos=halves(do)
    tri=lax.broadcasted_iota(jnp.int32,(bq,bq),0)<=lax.broadcasted_iota(jnp.int32,(bq,bq),1)
    nb=L//bq
    for j in reversed(range(nb)):
        host.tick(jobs,nb-1-j)
        lo=j*bq; hi=lo+bq
        dqT=jnp.zeros((128,bq),F32)
        dkp=None; dvp=None
        for h in range(2):
            qh=qs[h][lo:hi]; doh=dos[h][lo:hi]
            lse=lse_ref[0,h:h+1,lo:hi]
            s=nt(k[:hi],qh)
            dp=nt(v[:hi],doh)
            ps=[];
            cuts=[]
            if lo>0: cuts.append((0,min(lo,half)))
            if lo>half: cuts.append((half,lo))
            cuts.append((lo,hi))
            for a,b in cuts:
                ll=lse+shut if (lo>=half and b<=half) else lse
                t=s[a:b]-ll
                if a==lo: t=jnp.where(tri,t,NEG)
                ps.append(jnp.exp(t))
            p=jnp.concatenate(ps,axis=0) if len(ps)>1 else ps[0]
            delta=jnp.sum(p*dp,axis=0,keepdims=True)
            ds=(p*(dp-delta)).astype(BF)
            pb=p.astype(BF)
            dv_=nn(pb,doh); dk_=nn(ds,qh)
            dvp=dv_ if dvp is None else dvp+dv_
            dkp=dk_ if dkp is None else dkp+dk_
            dqT=dqT+nn(kTs[h][:,:hi],ds)
        if j==nb-1:
            dk_acc[...]=dkp; dv_acc[...]=dvp
        else:
            dk_acc[:hi]+=dkp; dv_acc[:hi]+=dvp
        dq_ref[lo:hi,:]=(dqT.T*0.125).astype(BF)
    dk_ref[...]=dk_acc[...].astype(BF); dv_ref[...]=dv_acc[...].astype(BF)
    host.leave(jobs)

def attend_bwd(qkv,do,lse,fl,host,bq=256):
    N,C=qkv.shape; R=fl.shape[0]; L=N//R; D=C//3; G=D//128
    blk=lambda off: pl.BlockSpec((L,128),lambda r,g,fl:(r,off*G+g))
    return pl.pallas_call(functools.partial(bwd_kernel,bq=bq,host=host),
        grid_spec=pltpu.PrefetchScalarGridSpec(num_scalar_prefetch=1,grid=(R,G),
          in_specs=[blk(0),blk(1),blk(2),blk(0),pl.BlockSpec((1,2,L),lambda r,g,fl:(r*G+g,0,0))]+host.ins,
          out_specs=[blk(0),blk(0),blk(0)]+host.outs,
          scratch_shapes=[pltpu.VMEM((L,128),F32),pltpu.VMEM((L,128),F32)]+host.scratch),
        out_shape=[jax.ShapeDtypeStruct((N,D),BF)]*3+host.shapes,
        compiler_params=host.params(),
        cost_estimate=pl.CostEstimate(flops=5*2*R*L*L*D*2,bytes_accessed=N*D*16,transcendentals=R*L*L*12//2),
        name="attend_bwd")(fl,qkv,qkv,qkv,do,lse,*host.arrays)


MESH = pl.DeviceIdType.MESH


def block_mesh():
    return lax.axis_size("dp") == 4 and lax.axis_size("fsdp") == 8


class Place:
    def __init__(self):
        d = lax.axis_index("dp")
        f = lax.axis_index("fsdp")
        self.y, self.x = lax.div(d, 2), lax.rem(d, 2)
        self.z, self.c = lax.div(f, 2), lax.rem(f, 2)
        self.zs = [self.z + 1 - 2 * lax.rem(self.z, 2), lax.rem(self.z + 2, 4), 3 - self.z]
        self.to_core = (d, 2 * self.z + 1 - self.c)
        self.to_x = (2 * self.y + 1 - self.x, f)
        self.to_y = (2 * (1 - self.y) + self.x, f)
        self.to_z = [(d, 2 * zz + self.c) for zz in self.zs]

    def greet(self):
        barrier = pltpu.get_barrier_semaphore()
        peers = [self.to_core, self.to_x, self.to_y] + self.to_z
        for peer in peers:
            pl.semaphore_signal(barrier, inc=1, device_id=peer, device_id_type=MESH)
        pl.semaphore_wait(barrier, len(peers))


ALL = slice(None)


class Gather:
    COPIES = 15
    STEPS = 5
    LINKS = (
        (("z", 8, True), ("first", 2, False), ("second", 2, False)),
        (("first", 6, True), ("second", 6, False), ("core", 4, False)),
        (("second", 8, True), ("core", 4, False)),
        (("core", 8, True),),
    )
    STARTS = ((0, 1, 2, 3, 4), (5, 6, 7, 8, 9, 10, 12), (11, 13), (14,), ())
    WAITS = ((), (0, 1, 2), (3, 5, 6, 7), (4, 8, 9, 10, 11), (12, 13, 14))

    def __init__(self, me, shard, out, scratch, cols, x_first, send, recv, local):
        self.send, self.recv = send, recv
        y, x, z, c = me.y, me.x, me.z, me.c
        cols = pl.ds(*cols)
        o = out.at
        tail = (ALL, c, ALL, cols)
        mine = o[y, x, z, c, :, cols]
        self.shard = shard.at[:, cols]
        self.own = pltpu.make_async_copy(self.shard, mine, local)
        if x_first:
            links, near, rest = (me.to_x, me.to_y), (y, 1 - x), (1 - y, ALL)
        else:
            links, near, rest = (me.to_y, me.to_x), (1 - y, x), (ALL, 1 - x)
        came = [o[y, x, zz, c, :, cols] for zz in me.zs]
        self.plan = [(me.to_z[k], mine) for k in range(3)] + [(links[0], mine), (links[1], mine)]
        self.plan += [(links[0], r) for r in came] + [(links[1], r) for r in came]
        self.plan += [(links[1], o[near + tail]), (me.to_core, o[(y, x) + tail]),
                      (me.to_core, o[near + tail]), (me.to_core, o[rest + tail])]

    def copy(self, k):
        peer, ref = self.plan[k]
        return pltpu.make_async_remote_copy(
            src_ref=self.shard if k < 5 else ref, dst_ref=ref, send_sem=self.send.at[k],
            recv_sem=self.recv.at[k], device_id=peer, device_id_type=MESH)

    def run(self, step):
        if step == 0:
            self.own.start()
        for k in self.WAITS[step]:
            self.copy(k).wait_recv()
        if step == 1:
            self.own.wait()
        for k in self.STARTS[step]:
            self.copy(k).start()
        if step == 4:
            for k in range(self.COPIES):
                self.copy(k).wait_send()


class Scatter:
    COPIES = 7
    STEPS = 5
    LINKS = (
        (("core", 16, True),),
        (("first", 8, True), ("first", 8, False)),
        (("second", 8, True),),
        (("z", 8, True),),
    )

    def __init__(self, me, term, out, scratch, cols, x_first, send, recv, local):
        self.me, self.out = me, out
        self.own, self.r = scratch[0], scratch[1:]
        self.send, self.recv = send, recv
        self.cols, self.x_first = pl.ds(*cols), x_first
        own, (r0, r1, r2, r3) = self.own, self.r
        y, x, z, c = me.y, me.x, me.z, me.c
        self.mine = pltpu.make_async_copy(term.at[ALL, ALL, ALL, c, :, self.cols], own, local)
        if x_first:
            first, second, near, across = me.to_x, me.to_y, own.at[y, 1 - x], own.at[1 - y, x]
        else:
            first, second, near, across = me.to_y, me.to_x, own.at[1 - y, x], own.at[y, 1 - x]
        self.plan = [
            (term.at[ALL, ALL, ALL, 1 - c, :, self.cols], me.to_core, r0),
            (own.at[1 - y, 1 - x], first, r1.at[0]), (near, first, r1.at[1]), (across, second, r2)] + [
            (own.at[y, x, me.zs[k]], me.to_z[k], r3.at[k]) for k in range(3)]

    def copy(self, k):
        src, peer, dst = self.plan[k]
        return pltpu.make_async_remote_copy(
            src_ref=src, dst_ref=dst, send_sem=self.send.at[k], recv_sem=self.recv.at[k],
            device_id=peer, device_id_type=MESH)

    def run(self, step):
        y, x, z = self.me.y, self.me.x, self.me.z
        own, (r0, r1, r2, r3) = self.own, self.r
        if step == 0:
            self.mine.start()
            self.copy(0).start()
        elif step == 1:
            self.mine.wait()
            self.copy(0).wait_recv()

            @pl.loop(0, 4)
            def _(k):
                for a in range(2):
                    for b in range(2):
                        own[a, b, k] = own[a, b, k] + r0[a, b, k]

            self.copy(1).start()
            self.copy(2).start()
        elif step == 2:
            self.copy(1).wait_recv()
            ay, ax = (1 - y, x) if self.x_first else (y, 1 - x)

            @pl.loop(0, 4)
            def _(k):
                own[ay, ax, k] = own[ay, ax, k] + r1[0, k]

            self.copy(3).start()
        elif step == 3:
            self.copy(2).wait_recv()
            self.copy(3).wait_recv()

            @pl.loop(0, 4)
            def _(k):
                total = own[y, x, k].astype(F32) + r1[1, k].astype(F32) + r2[k].astype(F32)
                own[y, x, k] = total.astype(own.dtype)

            for k in (4, 5, 6):
                self.copy(k).start()
        else:
            total = own[y, x, z].astype(F32)
            for k in (4, 5, 6):
                self.copy(k).wait_recv()
                total = total + r3[k - 4].astype(F32)
            self.out[:, self.cols] = total
            for k in range(self.COPIES):
                self.copy(k).wait_send()


def cut_jobs(arrays, kind, pieces):
    jobs = []
    for i, a in enumerate(arrays):
        units = a.shape[-1] // 128
        n = min(pieces, units)
        start = 0
        for k in range(n):
            width = 128 * (units // n + (1 if k < units % n else 0))
            jobs.append((i, (start, width), len(jobs) % 2 == 0))
            start += width
    return jobs


def plan_jobs(kind, jobs, rows, slots, window):
    free = dict.fromkeys("xyzc", 0.0)
    ready = {}

    def start(i, step, now):
        array, (unused, width), x_first = jobs[i]
        done = now
        names = {"z": "z", "core": "c", "first": "x" if x_first else "y", "second": "y" if x_first else "x"}
        if step < len(kind.LINKS):
            for link, blocks, counts in kind.LINKS[step]:
                name = names[link]
                rate = {"c": 500e3, "z": 78e3}.get(name, 83e3)
                free[name] = max(free[name], now) + blocks * rows[array] * width * 2 / rate
                if counts:
                    done = max(done, free[name])
        if step < kind.STEPS - 1:
            ready[i, step + 1] = done + 1.8
        if step == 1 and i + window < len(jobs):
            ready[i + window, 0] = now

    for i in range(min(window, len(jobs))):
        ready[i, 0] = 0.0
    now, plan = 0.0, []
    cost = 0.1 if kind is Gather else 0.5
    for length in slots:
        todo = []
        while True:
            can = sorted((e for e in ready if ready[e] <= now and e[1] < kind.STEPS - 1), key=lambda e: (-e[1], e[0]))
            if not can:
                break
            ready.pop(can[0])
            now += cost
            start(*can[0], now)
            todo.append(can[0])
        plan.append(todo)
        now += length
    todo = []
    while ready:
        e = min(ready, key=lambda e: (max(ready[e], now), -e[1], e[0]))
        now = max(ready.pop(e), now) + cost
        start(*e, now)
        todo.append(e)
    return plan + [todo]


class Host:
    def __init__(self, kind=None, arrays=(), ident=None, slots=(), per=1, axis=1, pieces=None, window=None):
        self.kind, self.ident, self.per, self.axis = kind, ident, per, axis
        self.used = bool(arrays) and block_mesh()
        self.source = list(arrays)
        self.arrays, self.ins, self.outs, self.shapes, self.scratch = [], [], [], [], []
        if self.used:
            self.build(arrays, slots, pieces, window)
        self.count = len(self.arrays)

    def build(self, arrays, slots, pieces, window):
        kind = self.kind
        if kind is Scatter:
            arrays = [a.reshape(2, 2, 4, 2, -1, a.shape[-1]) for a in arrays]
        self.arrays = arrays = list(arrays)
        n = len(arrays)
        pieces = pieces or (2 if kind is Gather else 4)
        self.jobs = jobs = cut_jobs(arrays, kind, pieces)
        rows = [a.shape[-2] * a.dtype.itemsize // 2 for a in arrays]
        self.plan = plan_jobs(kind, jobs, rows, slots, window or (8 if kind is Gather else 4))
        m = len(jobs)
        any_space, vmem = pl.BlockSpec(memory_space=pl.ANY), pl.BlockSpec(memory_space=pltpu.VMEM)
        if kind is Gather:
            self.ins, self.outs = [vmem] * n, [any_space] * n
            self.shapes = [jax.ShapeDtypeStruct((2, 2, 4, 2) + a.shape, a.dtype) for a in arrays]
        else:
            self.ins, self.outs = [any_space] * n, [vmem] * n
            self.shapes = [jax.ShapeDtypeStruct(a.shape[4:], F32) for a in arrays]
            for i, (unused, width), unused in jobs:
                for lead in ((2, 2, 4), (2, 2, 4), (2, 4), (4,), (3,)):
                    self.scratch.append(pltpu.VMEM(lead + (arrays[i].shape[-2], width), arrays[i].dtype))
        self.scratch = self.scratch + [
            pltpu.SemaphoreType.DMA((m, kind.COPIES)), pltpu.SemaphoreType.DMA((m, kind.COPIES)),
            pltpu.SemaphoreType.DMA((m,))]

    def params(self):
        if not self.used:
            return pltpu.CompilerParams(vmem_limit_bytes=48 << 20)
        return pltpu.CompilerParams(
            collective_id=self.ident, has_side_effects=True, vmem_limit_bytes=56 << 20)

    def enter(self, ins, outs, scratch):
        if not self.used:
            return None
        me = Place()
        send, recv, local = scratch[-3:]
        work = []
        for k, (i, cols, x_first) in enumerate(self.jobs):
            own = scratch[5 * k : 5 * k + 5] if self.kind is Scatter else ()
            work.append(self.kind(me, ins[i], outs[i], own, cols, x_first, send.at[k], recv.at[k], local.at[k]))
        self.now = pl.program_id(self.axis)

        @pl.when(self.now == 0)
        def _():
            me.greet()

        return work

    def tick(self, work, at):
        if not self.used:
            return
        for g in range((len(self.plan) - 1) // self.per):
            todo = self.plan[g * self.per + at]
            if todo:
                @pl.when(self.now == g)
                def _():
                    for i, t in todo:
                        work[i].run(t)

    def leave(self, work):
        if not self.used:
            return

        @pl.when(self.now == (len(self.plan) - 1) // self.per - 1)
        def _():
            for i, t in self.plan[-1]:
                work[i].run(t)

    def results(self, values):
        if self.used and self.kind is Gather:
            return [w.reshape(-1, w.shape[-1]) for w in values]
        if self.used:
            return list(values)
        return plain(self.kind, self.source)


def plain(kind, arrays):
    if kind is Gather:
        return [lax.all_gather(a, AX, axis=0, tiled=True) for a in arrays]
    return [lax.psum_scatter(t.astype(F32), AX, scatter_dimension=0, tiled=True) for t in arrays]


def alone_kernel(*refs, host):
    n = host.count
    jobs = host.enter(refs[:n], refs[n : 2 * n], refs[2 * n :])
    host.tick(jobs, 0)
    host.leave(jobs)


def exchange(kind, arrays, ident, name, pieces):
    host = Host(kind, arrays, ident, [0.0], axis=0, pieces=pieces)
    if not host.used:
        return plain(kind, arrays)
    return host.results(pl.pallas_call(
        functools.partial(alone_kernel, host=host), grid=(1,),
        in_specs=host.ins, out_specs=host.outs, out_shape=host.shapes, scratch_shapes=host.scratch,
        compiler_params=host.params(), name=name)(*host.arrays))


def layer_norm(values, gain, shift):
    centre = values - jnp.mean(values, axis=-1, keepdims=True)
    spread = jnp.mean(centre * centre, axis=-1, keepdims=True)
    return centre * lax.rsqrt(spread + EPS) * gain + shift


def inner_rows(left, right):
    return lax.dot_general(left, right, (((0,), (0,)), ((), ())), preferred_element_type=F32)


def times_transposed(left, right):
    return lax.dot_general(left, right, (((1,), (1,)), ((), ())), preferred_element_type=F32)


def column_sums(values):
    return jnp.sum(values.astype(F32), axis=0)


def gelu_pair(z):
    c = 0.7978845608028654
    t = jnp.tanh(c * (z + 0.044715 * z * z * z))
    value = 0.5 * z * (1.0 + t)
    slope = 0.5 * (1.0 + t) + 0.5 * z * (1.0 - t * t) * c * (1.0 + 3 * 0.044715 * z * z)
    return value.astype(BF), slope.astype(BF)


def pack_columns(vectors, wide, count):
    length = vectors[0].shape[0]
    ways = wide.shape[0] // length
    per = length // count
    spread = wide.reshape(count, ways, per).transpose(0, 2, 1).reshape(length, ways)
    block = jnp.concatenate([jnp.stack(vectors, axis=1), spread], axis=1)
    return jnp.pad(block, ((0, 0), (0, LANES - block.shape[1])))


def unpack_columns(block, vector_count, ways, count):
    length = block.shape[0]
    turned = block[:, : vector_count + ways].T
    wide = turned[vector_count:].reshape(ways, count, length // count).transpose(1, 0, 2).reshape(-1)
    return [turned[i] for i in range(vector_count)], wide


def local_shards(local):
    (ga, sa, hw, qb, vb, mw, mb, gf, sf, ew, eb, sw, sb) = local
    small = pack_columns([ga, sa, qb, vb, mb, gf, sf, sb], eb, 1)
    return [jnp.concatenate([hw, small], axis=1), mw, ew, sw]


def use_heads(heads, width, ways):
    vecs, wide = unpack_columns(heads[:, 3 * width :], 8, ways, lax.axis_size(AX))
    vecs = [v.astype(F32) for v in vecs]
    return dict(zip(("ga", "sa", "qb", "vb", "mb", "gf", "sf", "sb"), vecs), eb=wide.astype(F32),
                heads=heads[:, : 3 * width])


def forward_use(hidden, w, first_len, host):
    normed = layer_norm(hidden, w["ga"], w["sa"]).astype(BF)
    bias = jnp.concatenate([w["qb"], jnp.zeros_like(w["qb"]), w["vb"]])
    qkv = (jnp.dot(normed, w["heads"], preferred_element_type=F32) + bias).astype(BF)
    attended, lse, *more = attend_fwd(qkv, first_len, host)
    more = host.results(more)
    w.update(expand=more[0], shrink=more[1], mix=more[-1])
    middle = hidden + jnp.dot(attended, w["mix"], preferred_element_type=F32) + w["mb"]
    normed_two = layer_norm(middle, w["gf"], w["sf"]).astype(BF)
    expanded = jnp.dot(normed_two, w["expand"], preferred_element_type=F32) + w["eb"]
    activated, slope = gelu_pair(expanded)
    result = middle + jnp.dot(activated, w["shrink"], preferred_element_type=F32) + w["sb"]
    return result, (hidden, normed, qkv, attended, lse, middle, normed_two, activated, slope), more[2:-1]


def backward_use(grad_out, kept, w, first_len, carried, ident):
    hidden, normed, qkv, attended, lse, middle, normed_two, activated, slope = kept
    count = lax.axis_size(AX)
    grad_low = grad_out.astype(BF)
    shrink_term = inner_rows(activated, grad_low).astype(BF)
    sb = column_sums(grad_low)
    dz = (times_transposed(grad_low, w["shrink"]) * slope.astype(F32)).astype(BF)
    expand_term = inner_rows(normed_two, dz).astype(BF)
    eb = column_sums(dz)
    dc = times_transposed(dz, w["expand"])
    unused, norm_back = jax.vjp(layer_norm, middle, w["gf"], w["sf"])
    middle_norm, gf, sf = norm_back(dc)
    dm = grad_out + middle_norm
    dmb = dm.astype(BF)
    mix_term = inner_rows(attended, dmb).astype(BF)
    mb = column_sums(dmb)
    do = times_transposed(dmb, w["mix"]).astype(BF)
    host = Host(Scatter, [shrink_term, expand_term] + carried + [mix_term], ident, BACKWARD_SLOTS, per=4)
    dq, dk, dv, *more = attend_bwd(qkv, do, lse, first_len, host)
    more = host.results(more)
    dqkv = jnp.concatenate([dq, dk, dv], axis=1)
    heads_term = inner_rows(normed, dqkv).astype(BF)
    qb = column_sums(dq)
    vb = column_sums(dv)
    da = times_transposed(dqkv, w["heads"])
    unused, first_back = jax.vjp(layer_norm, hidden, w["ga"], w["sa"])
    hidden_norm, ga, sa = first_back(da)
    small = pack_columns([ga, sa, qb, vb, mb, gf, sf, sb], eb, count)
    return dm + hidden_norm, more, heads_term, small


def as_shares(shrink, expand, mix, heads, small):
    vecs, wide = unpack_columns(small, 8, shrink.shape[0] // heads.shape[0], 1)
    ga, sa, qb, vb, mb, gf, sf, sb = vecs
    return ga, sa, heads, qb, vb, mix, mb, gf, sf, expand, wide, shrink, sb


FORWARD_SLOTS = [0.43, 0.86, 1.29, 1.72] * 6
BACKWARD_SLOTS = [1.8, 1.35, 0.9, 0.45] * 6


def pick_shards(stacks, source):
    return tuple(lax.dynamic_index_in_dim(stack, source, 0, keepdims=False) for stack in stacks)


def place_terms(sources, shares):
    ids = lax.iota(jnp.int32, UNIQUE)
    out = []
    for items in zip(*shares):
        total = 0.0
        for source, item in zip(sources, items):
            chosen = (ids == source).reshape((UNIQUE,) + (1,) * item.ndim)
            total = total + jnp.where(chosen, item[None], 0.0)
        out.append(total)
    return out


def body(tokens, cotangent, tie_map, first_length, *stacks):
    hidden = tokens.astype(F32)
    width = hidden.shape[1]
    sources = [tie_map[i] for i in range(LAYERS)]
    shards = [local_shards(pick_shards(stacks, s)) for s in sources]
    ways = shards[0][3].shape[0] // shards[0][0].shape[0]
    (heads,) = exchange(Gather, shards[0][:1], 0, "gather", 4)
    kept, weights = [], []
    loads = [shards[0][2:] + shards[1][:1] + shards[0][1:2], shards[1][2:] + shards[1][1:2]]
    for i in range(LAYERS):
        weights.append(use_heads(heads, width, ways))
        host = Host(Gather, loads[i], 1 + i, FORWARD_SLOTS, per=4)
        hidden, saved, spare = forward_use(hidden, weights[i], first_length, host)
        heads = spare[0] if spare else None
        kept.append(saved)
    grad = cotangent.astype(F32)
    grad, late, heads_late, small_late = backward_use(
        grad, kept[1], weights[1], first_length, [], 3)
    grad, early, heads_early, small_early = backward_use(
        grad, kept[0], weights[0], first_length, [heads_late], 4)
    heads_early, small = exchange(
        Scatter, [heads_early, jnp.concatenate([small_early, small_late], axis=1)], 5, "scatter", 4)
    shares = [as_shares(early[0], early[1], early[3], heads_early, small[:, :LANES]),
              as_shares(*late, early[2], small[:, LANES:])]
    return (hidden.astype(BF), grad.astype(BF), *place_terms(sources, shares))


def solution(mesh):
    rows = P(AX, None)
    flat = P(None, AX)
    deep = P(None, AX, None)
    weights = (flat, flat, deep, flat, flat, deep, flat, flat, flat, deep, flat, deep, flat)
    return jax.shard_map(
        body,
        mesh=mesh,
        in_specs=(rows, rows, P(), P(AX)) + weights,
        out_specs=(rows, rows) + weights,
        check_vma=False,
    )
```

```python
import functools

import jax
import jax.numpy as jnp
from jax import lax
from jax.experimental import pallas as pl
from jax.experimental.pallas import tpu as pltpu
from jax.sharding import PartitionSpec as P

LAYERS = 2
UNIQUE = 4
F32 = jnp.float32
BF = jnp.bfloat16
AX = ("dp", "fsdp")
LANES = 128
EPS = 1e-05

NEG=-1e9
def nt(a,b): return lax.dot_general(a,b,(((1,),(1,)),((),())),preferred_element_type=F32)
def nn(a,b): return lax.dot_general(a,b,(((1,),(0,)),((),())),preferred_element_type=F32)
def halves(x):
    lane=lax.broadcasted_iota(jnp.int32,x.shape,1)
    z=jnp.zeros_like(x)
    return jnp.where(lane<64,x,z), jnp.where(lane<64,z,x)

def fwd_kernel(fl_ref,q_ref,k_ref,v_ref,*rest,bq,host):
    n=host.count
    o_ref,lse_ref=rest[n:n+2]
    jobs=host.enter(rest[:n],rest[n+2:2*n+2],rest[2*n+2:])
    L=q_ref.shape[0]; half=L//2
    second=fl_ref[pl.program_id(0)]<L
    shut=jnp.where(second,F32(1e9),F32(0.))
    q=q_ref[...]*BF(0.125); k=k_ref[...]; vT=v_ref[...].T
    sub=lax.broadcasted_iota(jnp.int32,vT.shape,0)
    zero=jnp.zeros_like(vT)
    vTs=(jnp.where(sub<64,vT,zero),jnp.where(sub<64,zero,vT))
    qs=halves(q)
    tri=lax.broadcasted_iota(jnp.int32,(bq,bq),0)<=lax.broadcasted_iota(jnp.int32,(bq,bq),1)
    for j in range(L//bq):
        host.tick(jobs,j)
        lo=j*bq; hi=lo+bq
        acc=jnp.zeros((128,bq),F32)
        for h in range(2):
            qh=qs[h][lo:hi]
            s=nt(k[:hi],qh)
            parts=[]
            if lo>0 : parts.append((0,min(lo,half),s[:min(lo,half)]))
            if lo>half: parts.append((half,lo,s[half:lo]))
            diag=jnp.where(tri,s[lo:],NEG)
            m=jnp.max(diag,axis=0,keepdims=True)
            for a,b,t in parts:
                mt=jnp.max(t,axis=0,keepdims=True)
                if lo>=half and a==0: mt=mt-shut
                m=jnp.maximum(m,mt)
            ps=[]; l=0.
            for a,b,t in parts+[(lo,hi,diag)]:
                mm=m+shut if (lo>=half and a==0) else m
                p=jnp.exp(t-mm)
                l=l+jnp.sum(p,axis=0,keepdims=True)
                ps.append(p.astype(BF))
            p=jnp.concatenate(ps,axis=0) if len(ps)>1 else ps[0]
            oh=nn(vTs[h][:,:hi],p)
            acc=acc+oh*(1.0/l)
            lse_ref[0,h:h+1,lo:hi]=m+jnp.log(l)
        o_ref[lo:hi,:]=acc.T.astype(BF)
    host.leave(jobs)

def attend_fwd(qkv,fl,host,bq=256):
    N,C=qkv.shape; R=fl.shape[0]; L=N//R; D=C//3; G=D//128
    return pl.pallas_call(functools.partial(fwd_kernel,bq=bq,host=host),
        grid_spec=pltpu.PrefetchScalarGridSpec(num_scalar_prefetch=1,grid=(R,G),
          in_specs=[pl.BlockSpec((L,128),lambda r,g,fl:(r,g)),
                    pl.BlockSpec((L,128),lambda r,g,fl:(r,G+g)),
                    pl.BlockSpec((L,128),lambda r,g,fl:(r,2*G+g))]+host.ins,
          out_specs=[pl.BlockSpec((L,128),lambda r,g,fl:(r,g)),
                     pl.BlockSpec((1,2,L),lambda r,g,fl:(r*G+g,0,0))]+host.outs,
          scratch_shapes=host.scratch),
        out_shape=[jax.ShapeDtypeStruct((N,D),BF),jax.ShapeDtypeStruct((R*G,2,L),F32)]+host.shapes,
        compiler_params=host.params(),
        cost_estimate=pl.CostEstimate(flops=2*2*R*L*L*D*2,bytes_accessed=N*D*8,transcendentals=R*L*L*12//2),
        name="attend_fwd")(fl,qkv,qkv,qkv,*host.arrays)

def bwd_kernel(fl_ref,q_ref,k_ref,v_ref,do_ref,lse_ref,*rest,bq,host):
    n=host.count
    dq_ref,dk_ref,dv_ref=rest[n:n+3]
    dk_acc,dv_acc=rest[2*n+3:2*n+5]
    jobs=host.enter(rest[:n],rest[n+3:2*n+3],rest[2*n+5:])
    L=q_ref.shape[0]; half=L//2
    second=fl_ref[pl.program_id(0)]<L
    shut=jnp.where(second,F32(1e9),F32(0.))
    q=q_ref[...]*BF(0.125); k=k_ref[...]; v=v_ref[...]; do=do_ref[...]
    kT=k.T
    sub=lax.broadcasted_iota(jnp.int32,kT.shape,0); zero=jnp.zeros_like(kT)
    kTs=(jnp.where(sub<64,kT,zero),jnp.where(sub<64,zero,kT))
    qs=halves(q); dos=halves(do)
    tri=lax.broadcasted_iota(jnp.int32,(bq,bq),0)<=lax.broadcasted_iota(jnp.int32,(bq,bq),1)
    nb=L//bq
    for j in reversed(range(nb)):
        host.tick(jobs,nb-1-j)
        lo=j*bq; hi=lo+bq
        dqT=jnp.zeros((128,bq),F32)
        dkp=None; dvp=None
        for h in range(2):
            qh=qs[h][lo:hi]; doh=dos[h][lo:hi]
            lse=lse_ref[0,h:h+1,lo:hi]
            s=nt(k[:hi],qh)
            dp=nt(v[:hi],doh)
            ps=[];
            cuts=[]
            if lo>0: cuts.append((0,min(lo,half)))
            if lo>half: cuts.append((half,lo))
            cuts.append((lo,hi))
            for a,b in cuts:
                ll=lse+shut if (lo>=half and b<=half) else lse
                t=s[a:b]-ll
                if a==lo: t=jnp.where(tri,t,NEG)
                ps.append(jnp.exp(t))
            p=jnp.concatenate(ps,axis=0) if len(ps)>1 else ps[0]
            delta=jnp.sum(p*dp,axis=0,keepdims=True)
            ds=(p*(dp-delta)).astype(BF)
            pb=p.astype(BF)
            dv_=nn(pb,doh); dk_=nn(ds,qh)
            dvp=dv_ if dvp is None else dvp+dv_
            dkp=dk_ if dkp is None else dkp+dk_
            dqT=dqT+nn(kTs[h][:,:hi],ds)
        if j==nb-1:
            dk_acc[...]=dkp; dv_acc[...]=dvp
        else:
            dk_acc[:hi]+=dkp; dv_acc[:hi]+=dvp
        dq_ref[lo:hi,:]=(dqT.T*0.125).astype(BF)
    dk_ref[...]=dk_acc[...].astype(BF); dv_ref[...]=dv_acc[...].astype(BF)
    host.leave(jobs)

def attend_bwd(qkv,do,lse,fl,host,bq=256):
    N,C=qkv.shape; R=fl.shape[0]; L=N//R; D=C//3; G=D//128
    blk=lambda off: pl.BlockSpec((L,128),lambda r,g,fl:(r,off*G+g))
    return pl.pallas_call(functools.partial(bwd_kernel,bq=bq,host=host),
        grid_spec=pltpu.PrefetchScalarGridSpec(num_scalar_prefetch=1,grid=(R,G),
          in_specs=[blk(0),blk(1),blk(2),blk(0),pl.BlockSpec((1,2,L),lambda r,g,fl:(r*G+g,0,0))]+host.ins,
          out_specs=[blk(0),blk(0),blk(0)]+host.outs,
          scratch_shapes=[pltpu.VMEM((L,128),F32),pltpu.VMEM((L,128),F32)]+host.scratch),
        out_shape=[jax.ShapeDtypeStruct((N,D),BF)]*3+host.shapes,
        compiler_params=host.params(),
        cost_estimate=pl.CostEstimate(flops=5*2*R*L*L*D*2,bytes_accessed=N*D*16,transcendentals=R*L*L*12//2),
        name="attend_bwd")(fl,qkv,qkv,qkv,do,lse,*host.arrays)


def tn(a,b): return lax.dot_general(a,b,(((0,),(0,)),((),())),preferred_element_type=F32)

def feed_fwd_kernel(c_ref,e_ref,eb_ref,s_ref,m_ref,sb_ref,*rest,rows,host):
    n=host.count
    h_ref,u_ref,slope_ref=rest[n:n+3]
    jobs=host.enter(rest[:n],rest[n+3:2*n+3],rest[2*n+3:])
    N=c_ref.shape[0]
    e=e_ref[...]; s=s_ref[...]; eb=eb_ref[...]
    @pl.when(pl.program_id(0)==0)
    def _(): h_ref[...]=m_ref[...]+sb_ref[...]
    for j in range(N//rows):
        host.tick(jobs,j)
        at=slice(j*rows,(j+1)*rows)
        u,slope=gelu_pair(nn(c_ref[at,:],e)+eb)
        u_ref[at,:]=u; slope_ref[at,:]=slope
        h_ref[at,:]+=nn(u,s)
    host.leave(jobs)

def feed_fwd(c,w,middle,host,tile=512,rows=256):
    N,D=c.shape; F=w["expand"].shape[1]
    fixed=lambda r: pl.BlockSpec((r,D),lambda t: (0,0))
    return pl.pallas_call(functools.partial(feed_fwd_kernel,rows=rows,host=host),grid=(F//tile,),
        in_specs=[fixed(N),pl.BlockSpec((D,tile),lambda t:(0,t)),pl.BlockSpec((1,tile),lambda t:(0,t)),
                  pl.BlockSpec((tile,D),lambda t:(t,0)),fixed(N),fixed(1)]+host.ins,
        out_specs=[fixed(N)]+[pl.BlockSpec((N,tile),lambda t:(0,t))]*2+host.outs,
        out_shape=[jax.ShapeDtypeStruct((N,D),F32)]+[jax.ShapeDtypeStruct((N,F),BF)]*2+host.shapes,
        scratch_shapes=host.scratch,compiler_params=host.params(),
        cost_estimate=pl.CostEstimate(flops=4*N*D*F,bytes_accessed=4*N*F+4*D*F,transcendentals=N*F),
        name="feed_fwd")(c,w["expand"],w["eb"][None],w["shrink"],middle,w["sb"][None],*host.arrays)

def feed_bwd_kernel(g_ref,u_ref,slope_ref,c_ref,e_ref,s_ref,*rest,rows,host):
    n=host.count
    dc_ref,de_ref,ds_ref,eb_ref=rest[n:n+4]
    dz_ref=rest[2*n+4]
    jobs=host.enter(rest[:n],rest[n+4:2*n+4],rest[2*n+5:])
    N=c_ref.shape[0]
    e=e_ref[...]; s=s_ref[...]
    @pl.when(pl.program_id(0)==0)
    def _(): dc_ref[...]=jnp.zeros_like(dc_ref)
    total=0.
    for j in range(N//rows):
        host.tick(jobs,j)
        at=slice(j*rows,(j+1)*rows)
        dz=(nt(g_ref[at,:],s)*slope_ref[at,:].astype(F32)).astype(BF)
        dz_ref[at,:]=dz
        total=total+jnp.sum(dz.astype(F32),axis=0,keepdims=True)
        dc_ref[at,:]+=nt(dz,e)
    eb_ref[...]=total
    de_ref[...]=tn(c_ref[...],dz_ref[...]).astype(BF)
    ds_ref[...]=tn(u_ref[...],g_ref[...]).astype(BF)
    host.leave(jobs)

def feed_bwd(g,u,slope,c,w,host,tile=512,rows=256):
    N,D=c.shape; F=u.shape[1]
    fixed=pl.BlockSpec((N,D),lambda t:(0,0))
    wide=lambda r: pl.BlockSpec((r,tile),lambda t:(0,t))
    tall=pl.BlockSpec((tile,D),lambda t:(t,0))
    return pl.pallas_call(functools.partial(feed_bwd_kernel,rows=rows,host=host),grid=(F//tile,),
        in_specs=[fixed,wide(N),wide(N),fixed,wide(D),tall]+host.ins,
        out_specs=[fixed,wide(D),tall,wide(1)]+host.outs,
        out_shape=[jax.ShapeDtypeStruct((N,D),F32),jax.ShapeDtypeStruct((D,F),BF),
                   jax.ShapeDtypeStruct((F,D),BF),jax.ShapeDtypeStruct((1,F),F32)]+host.shapes,
        scratch_shapes=[pltpu.VMEM((N,tile),BF)]+host.scratch,compiler_params=host.params(),
        cost_estimate=pl.CostEstimate(flops=8*N*D*F,bytes_accessed=4*N*F+8*D*F,transcendentals=0),
        name="feed_bwd")(g,u,slope,c,w["expand"],w["shrink"],*host.arrays)


MESH = pl.DeviceIdType.MESH


def block_mesh():
    return lax.axis_size("dp") == 4 and lax.axis_size("fsdp") == 8


class Place:
    def __init__(self):
        d = lax.axis_index("dp")
        f = lax.axis_index("fsdp")
        self.y, self.x = lax.div(d, 2), lax.rem(d, 2)
        self.z, self.c = lax.div(f, 2), lax.rem(f, 2)
        self.zs = [self.z + 1 - 2 * lax.rem(self.z, 2), lax.rem(self.z + 2, 4), 3 - self.z]
        self.to_core = (d, 2 * self.z + 1 - self.c)
        self.to_x = (2 * self.y + 1 - self.x, f)
        self.to_y = (2 * (1 - self.y) + self.x, f)
        self.to_z = [(d, 2 * zz + self.c) for zz in self.zs]

    def greet(self):
        barrier = pltpu.get_barrier_semaphore()
        peers = [self.to_core, self.to_x, self.to_y] + self.to_z
        for peer in peers:
            pl.semaphore_signal(barrier, inc=1, device_id=peer, device_id_type=MESH)
        pl.semaphore_wait(barrier, len(peers))


ALL = slice(None)


class Gather:
    COPIES = 15
    STEPS = 5
    LINKS = (
        (("z", 8, True), ("first", 2, False), ("second", 2, False)),
        (("first", 6, True), ("second", 6, False), ("core", 4, False)),
        (("second", 8, True), ("core", 4, False)),
        (("core", 8, True),),
    )
    STARTS = ((0, 1, 2, 3, 4), (5, 6, 7, 8, 9, 10, 12), (11, 13), (14,), ())
    WAITS = ((), (0, 1, 2), (3, 5, 6, 7), (4, 8, 9, 10, 11), (12, 13, 14))

    def __init__(self, me, shard, out, scratch, cols, x_first, send, recv, local):
        self.send, self.recv = send, recv
        y, x, z, c = me.y, me.x, me.z, me.c
        cols = pl.ds(*cols)
        o = out.at
        tail = (ALL, c, ALL, cols)
        mine = o[y, x, z, c, :, cols]
        self.shard = shard.at[:, cols]
        self.own = pltpu.make_async_copy(self.shard, mine, local)
        if x_first:
            links, near, rest = (me.to_x, me.to_y), (y, 1 - x), (1 - y, ALL)
        else:
            links, near, rest = (me.to_y, me.to_x), (1 - y, x), (ALL, 1 - x)
        came = [o[y, x, zz, c, :, cols] for zz in me.zs]
        self.plan = [(me.to_z[k], mine) for k in range(3)] + [(links[0], mine), (links[1], mine)]
        self.plan += [(links[0], r) for r in came] + [(links[1], r) for r in came]
        self.plan += [(links[1], o[near + tail]), (me.to_core, o[(y, x) + tail]),
                      (me.to_core, o[near + tail]), (me.to_core, o[rest + tail])]

    def copy(self, k):
        peer, ref = self.plan[k]
        return pltpu.make_async_remote_copy(
            src_ref=self.shard if k < 5 else ref, dst_ref=ref, send_sem=self.send.at[k],
            recv_sem=self.recv.at[k], device_id=peer, device_id_type=MESH)

    def run(self, step):
        if step == 0:
            self.own.start()
        for k in self.WAITS[step]:
            self.copy(k).wait_recv()
        if step == 1:
            self.own.wait()
        for k in self.STARTS[step]:
            self.copy(k).start()
        if step == 4:
            for k in range(self.COPIES):
                self.copy(k).wait_send()


class Scatter:
    COPIES = 7
    STEPS = 5
    LINKS = (
        (("core", 16, True),),
        (("first", 8, True), ("first", 8, False)),
        (("second", 8, True),),
        (("z", 8, True),),
    )

    def __init__(self, me, term, out, scratch, cols, x_first, send, recv, local):
        self.me, self.out = me, out
        self.own, self.r = scratch[0], scratch[1:]
        self.send, self.recv = send, recv
        self.cols, self.x_first = pl.ds(*cols), x_first
        own, (r0, r1, r2, r3) = self.own, self.r
        y, x, z, c = me.y, me.x, me.z, me.c
        self.mine = pltpu.make_async_copy(term.at[ALL, ALL, ALL, c, :, self.cols], own, local)
        if x_first:
            first, second, near, across = me.to_x, me.to_y, own.at[y, 1 - x], own.at[1 - y, x]
        else:
            first, second, near, across = me.to_y, me.to_x, own.at[1 - y, x], own.at[y, 1 - x]
        self.plan = [
            (term.at[ALL, ALL, ALL, 1 - c, :, self.cols], me.to_core, r0),
            (own.at[1 - y, 1 - x], first, r1.at[0]), (near, first, r1.at[1]), (across, second, r2)] + [
            (own.at[y, x, me.zs[k]], me.to_z[k], r3.at[k]) for k in range(3)]

    def copy(self, k):
        src, peer, dst = self.plan[k]
        return pltpu.make_async_remote_copy(
            src_ref=src, dst_ref=dst, send_sem=self.send.at[k], recv_sem=self.recv.at[k],
            device_id=peer, device_id_type=MESH)

    def run(self, step):
        y, x, z = self.me.y, self.me.x, self.me.z
        own, (r0, r1, r2, r3) = self.own, self.r
        if step == 0:
            self.mine.start()
            self.copy(0).start()
        elif step == 1:
            self.mine.wait()
            self.copy(0).wait_recv()

            @pl.loop(0, 4)
            def _(k):
                for a in range(2):
                    for b in range(2):
                        own[a, b, k] = own[a, b, k] + r0[a, b, k]

            self.copy(1).start()
            self.copy(2).start()
        elif step == 2:
            self.copy(1).wait_recv()
            ay, ax = (1 - y, x) if self.x_first else (y, 1 - x)

            @pl.loop(0, 4)
            def _(k):
                own[ay, ax, k] = own[ay, ax, k] + r1[0, k]

            self.copy(3).start()
        elif step == 3:
            self.copy(2).wait_recv()
            self.copy(3).wait_recv()

            @pl.loop(0, 4)
            def _(k):
                total = own[y, x, k].astype(F32) + r1[1, k].astype(F32) + r2[k].astype(F32)
                own[y, x, k] = total.astype(own.dtype)

            for k in (4, 5, 6):
                self.copy(k).start()
        else:
            total = own[y, x, z].astype(F32)
            for k in (4, 5, 6):
                self.copy(k).wait_recv()
                total = total + r3[k - 4].astype(F32)
            self.out[:, self.cols] = total
            for k in range(self.COPIES):
                self.copy(k).wait_send()


def cut_jobs(arrays, kind, pieces):
    jobs = []
    for i, a in enumerate(arrays):
        units = a.shape[-1] // 128
        n = min(pieces, units)
        start = 0
        for k in range(n):
            width = 128 * (units // n + (1 if k < units % n else 0))
            jobs.append((i, (start, width), len(jobs) % 2 == 0))
            start += width
    return jobs


def plan_jobs(kind, jobs, rows, slots, window):
    free = dict.fromkeys("xyzc", 0.0)
    ready = {}

    def start(i, step, now):
        array, (unused, width), x_first = jobs[i]
        done = now
        names = {"z": "z", "core": "c", "first": "x" if x_first else "y", "second": "y" if x_first else "x"}
        if step < len(kind.LINKS):
            for link, blocks, counts in kind.LINKS[step]:
                name = names[link]
                rate = {"c": 500e3, "z": 78e3}.get(name, 83e3)
                free[name] = max(free[name], now) + blocks * rows[array] * width * 2 / rate
                if counts:
                    done = max(done, free[name])
        if step < kind.STEPS - 1:
            ready[i, step + 1] = done + 1.8
        if step == 1 and i + window < len(jobs):
            ready[i + window, 0] = now

    for i in range(min(window, len(jobs))):
        ready[i, 0] = 0.0
    now, plan = 0.0, []
    cost = 0.1 if kind is Gather else 0.5
    for length in slots:
        todo = []
        while True:
            can = sorted((e for e in ready if ready[e] <= now and e[1] < kind.STEPS - 1), key=lambda e: (-e[1], e[0]))
            if not can:
                break
            ready.pop(can[0])
            now += cost
            start(*can[0], now)
            todo.append(can[0])
        plan.append(todo)
        now += length
    todo = []
    while ready:
        e = min(ready, key=lambda e: (max(ready[e], now), -e[1], e[0]))
        now = max(ready.pop(e), now) + cost
        start(*e, now)
        todo.append(e)
    return plan + [todo]


class Host:
    def __init__(self, kind=None, arrays=(), ident=None, slots=(), per=1, axis=1, pieces=None, window=None):
        self.kind, self.ident, self.per, self.axis = kind, ident, per, axis
        self.used = bool(arrays) and block_mesh()
        self.source = list(arrays)
        self.arrays, self.ins, self.outs, self.shapes, self.scratch = [], [], [], [], []
        if self.used:
            self.build(arrays, slots, pieces, window)
        self.count = len(self.arrays)

    def build(self, arrays, slots, pieces, window):
        kind = self.kind
        if kind is Scatter:
            arrays = [a.reshape(2, 2, 4, 2, -1, a.shape[-1]) for a in arrays]
        self.arrays = arrays = list(arrays)
        n = len(arrays)
        pieces = pieces or (2 if kind is Gather else 4)
        self.jobs = jobs = cut_jobs(arrays, kind, pieces)
        rows = [a.shape[-2] * a.dtype.itemsize // 2 for a in arrays]
        self.plan = plan_jobs(kind, jobs, rows, slots, window or (8 if kind is Gather else 4))
        m = len(jobs)
        any_space, vmem = pl.BlockSpec(memory_space=pl.ANY), pl.BlockSpec(memory_space=pltpu.VMEM)
        if kind is Gather:
            self.ins, self.outs = [vmem] * n, [any_space] * n
            self.shapes = [jax.ShapeDtypeStruct((2, 2, 4, 2) + a.shape, a.dtype) for a in arrays]
        else:
            self.ins, self.outs = [any_space] * n, [vmem] * n
            self.shapes = [jax.ShapeDtypeStruct(a.shape[4:], F32) for a in arrays]
            for i, (unused, width), unused in jobs:
                for lead in ((2, 2, 4), (2, 2, 4), (2, 4), (4,), (3,)):
                    self.scratch.append(pltpu.VMEM(lead + (arrays[i].shape[-2], width), arrays[i].dtype))
        self.scratch = self.scratch + [
            pltpu.SemaphoreType.DMA((m, kind.COPIES)), pltpu.SemaphoreType.DMA((m, kind.COPIES)),
            pltpu.SemaphoreType.DMA((m,))]

    def params(self):
        if not self.used:
            return pltpu.CompilerParams(vmem_limit_bytes=48 << 20)
        return pltpu.CompilerParams(
            collective_id=self.ident, has_side_effects=True, vmem_limit_bytes=56 << 20)

    def enter(self, ins, outs, scratch):
        if not self.used:
            return None
        me = Place()
        send, recv, local = scratch[-3:]
        work = []
        for k, (i, cols, x_first) in enumerate(self.jobs):
            own = scratch[5 * k : 5 * k + 5] if self.kind is Scatter else ()
            work.append(self.kind(me, ins[i], outs[i], own, cols, x_first, send.at[k], recv.at[k], local.at[k]))
        self.now = pl.program_id(self.axis)

        @pl.when(self.now == 0)
        def _():
            me.greet()

        return work

    def tick(self, work, at):
        if not self.used:
            return
        for g in range((len(self.plan) - 1) // self.per):
            todo = self.plan[g * self.per + at]
            if todo:
                @pl.when(self.now == g)
                def _():
                    for i, t in todo:
                        work[i].run(t)

    def leave(self, work):
        if not self.used:
            return

        @pl.when(self.now == (len(self.plan) - 1) // self.per - 1)
        def _():
            for i, t in self.plan[-1]:
                work[i].run(t)

    def results(self, values):
        if self.used and self.kind is Gather:
            return [w.reshape(-1, w.shape[-1]) for w in values]
        if self.used:
            return list(values)
        return plain(self.kind, self.source) if self.source else []


def plain(kind, arrays):
    if kind is Gather:
        return [lax.all_gather(a, AX, axis=0, tiled=True) for a in arrays]
    return [lax.psum_scatter(t.astype(F32), AX, scatter_dimension=0, tiled=True) for t in arrays]


def alone_kernel(*refs, host):
    n = host.count
    jobs = host.enter(refs[:n], refs[n : 2 * n], refs[2 * n :])
    host.tick(jobs, 0)
    host.leave(jobs)


def exchange(kind, arrays, ident, name, pieces):
    host = Host(kind, arrays, ident, [0.0], axis=0, pieces=pieces)
    if not host.used:
        return plain(kind, arrays)
    return host.results(pl.pallas_call(
        functools.partial(alone_kernel, host=host), grid=(1,),
        in_specs=host.ins, out_specs=host.outs, out_shape=host.shapes, scratch_shapes=host.scratch,
        compiler_params=host.params(), name=name)(*host.arrays))


def layer_norm(values, gain, shift):
    centre = values - jnp.mean(values, axis=-1, keepdims=True)
    spread = jnp.mean(centre * centre, axis=-1, keepdims=True)
    return centre * lax.rsqrt(spread + EPS) * gain + shift


def inner_rows(left, right):
    return lax.dot_general(left, right, (((0,), (0,)), ((), ())), preferred_element_type=F32)


def times_transposed(left, right):
    return lax.dot_general(left, right, (((1,), (1,)), ((), ())), preferred_element_type=F32)


def column_sums(values):
    return jnp.sum(values.astype(F32), axis=0)


def gelu_pair(z):
    c = 0.7978845608028654
    t = jnp.tanh(c * (z + 0.044715 * z * z * z))
    value = 0.5 * z * (1.0 + t)
    slope = 0.5 * (1.0 + t) + 0.5 * z * (1.0 - t * t) * c * (1.0 + 3 * 0.044715 * z * z)
    return value.astype(BF), slope.astype(BF)


def pack_columns(vectors, wide, count):
    length = vectors[0].shape[0]
    ways = wide.shape[0] // length
    per = length // count
    spread = wide.reshape(count, ways, per).transpose(0, 2, 1).reshape(length, ways)
    block = jnp.concatenate([jnp.stack(vectors, axis=1), spread], axis=1)
    return jnp.pad(block, ((0, 0), (0, LANES - block.shape[1])))


def unpack_columns(block, vector_count, ways, count):
    length = block.shape[0]
    turned = block[:, : vector_count + ways].T
    wide = turned[vector_count:].reshape(ways, count, length // count).transpose(1, 0, 2).reshape(-1)
    return [turned[i] for i in range(vector_count)], wide


def local_shards(local):
    (ga, sa, hw, qb, vb, mw, mb, gf, sf, ew, eb, sw, sb) = local
    small = pack_columns([ga, sa, qb, vb, mb, gf, sf, sb], eb, 1)
    return [jnp.concatenate([hw, small], axis=1), mw, ew, sw]


def use_heads(heads, width, ways):
    vecs, wide = unpack_columns(heads[:, 3 * width :], 8, ways, lax.axis_size(AX))
    vecs = [v.astype(F32) for v in vecs]
    return dict(zip(("ga", "sa", "qb", "vb", "mb", "gf", "sf", "sb"), vecs), eb=wide.astype(F32),
                heads=heads[:, : 3 * width])


def forward_use(hidden, w, first_len, host, spare_host):
    normed = layer_norm(hidden, w["ga"], w["sa"]).astype(BF)
    bias = jnp.concatenate([w["qb"], jnp.zeros_like(w["qb"]), w["vb"]])
    qkv = (jnp.dot(normed, w["heads"], preferred_element_type=F32) + bias).astype(BF)
    attended, lse, *more = attend_fwd(qkv, first_len, host)
    more = host.results(more)
    w.update(expand=more[0], shrink=more[1], mix=more[-1])
    middle = hidden + jnp.dot(attended, w["mix"], preferred_element_type=F32) + w["mb"]
    normed_two = layer_norm(middle, w["gf"], w["sf"]).astype(BF)
    result, activated, slope, *spare = feed_fwd(normed_two, w, middle, spare_host)
    kept = (hidden, normed, qkv, attended, lse, middle, normed_two, activated, slope)
    return result, kept, spare_host.results(spare)


def backward_use(grad_out, kept, w, first_len, carried, ident, spare_ident):
    hidden, normed, qkv, attended, lse, middle, normed_two, activated, slope = kept
    count = lax.axis_size(AX)
    grad_low = grad_out.astype(BF)
    sb = column_sums(grad_low)
    spare = Host(Scatter, carried, spare_ident, FEED_BACKWARD_SLOTS, per=4, axis=0)
    dc, expand_term, shrink_term, eb, *carried = feed_bwd(grad_low, activated, slope, normed_two, w, spare)
    carried = spare.results(carried)
    eb = eb[0]
    unused, norm_back = jax.vjp(layer_norm, middle, w["gf"], w["sf"])
    middle_norm, gf, sf = norm_back(dc)
    dm = grad_out + middle_norm
    dmb = dm.astype(BF)
    mix_term = inner_rows(attended, dmb).astype(BF)
    mb = column_sums(dmb)
    do = times_transposed(dmb, w["mix"]).astype(BF)
    host = Host(Scatter, [shrink_term, expand_term, mix_term], ident, BACKWARD_SLOTS, per=4)
    dq, dk, dv, *more = attend_bwd(qkv, do, lse, first_len, host)
    more = host.results(more)
    dqkv = jnp.concatenate([dq, dk, dv], axis=1)
    heads_term = inner_rows(normed, dqkv).astype(BF)
    qb = column_sums(dq)
    vb = column_sums(dv)
    da = times_transposed(dqkv, w["heads"])
    unused, first_back = jax.vjp(layer_norm, hidden, w["ga"], w["sa"])
    hidden_norm, ga, sa = first_back(da)
    small = pack_columns([ga, sa, qb, vb, mb, gf, sf, sb], eb, count)
    return dm + hidden_norm, more, heads_term, small, carried


def as_shares(shrink, expand, mix, heads, small):
    vecs, wide = unpack_columns(small, 8, shrink.shape[0] // heads.shape[0], 1)
    ga, sa, qb, vb, mb, gf, sf, sb = vecs
    return ga, sa, heads, qb, vb, mix, mb, gf, sf, expand, wide, shrink, sb


FORWARD_SLOTS = [0.43, 0.86, 1.29, 1.72] * 6
BACKWARD_SLOTS = [1.8, 1.35, 0.9, 0.45] * 6
FEED_FORWARD_SLOTS = [0.6, 0.6, 0.6, 0.6] * 6
FEED_BACKWARD_SLOTS = [0.6, 0.6, 0.6, 2.9] * 6


def pick_shards(stacks, source):
    return tuple(lax.dynamic_index_in_dim(stack, source, 0, keepdims=False) for stack in stacks)


def place_terms(sources, shares):
    ids = lax.iota(jnp.int32, UNIQUE)
    out = []
    for items in zip(*shares):
        total = 0.0
        for source, item in zip(sources, items):
            chosen = (ids == source).reshape((UNIQUE,) + (1,) * item.ndim)
            total = total + jnp.where(chosen, item[None], 0.0)
        out.append(total)
    return out


def body(tokens, cotangent, tie_map, first_length, *stacks):
    hidden = tokens.astype(F32)
    width = hidden.shape[1]
    sources = [tie_map[i] for i in range(LAYERS)]
    shards = [local_shards(pick_shards(stacks, s)) for s in sources]
    ways = shards[0][3].shape[0] // shards[0][0].shape[0]
    (heads,) = exchange(Gather, shards[0][:1], 0, "gather", 4)
    kept, weights = [], []
    for i in range(LAYERS):
        weights.append(use_heads(heads, width, ways))
        host = Host(Gather, shards[i][2:] + shards[i][1:2], 1 + i, FORWARD_SLOTS, per=4)
        later = shards[i + 1][:1] if i + 1 < LAYERS else []
        spare_host = Host(Gather, later, 6, FEED_FORWARD_SLOTS, per=4, axis=0)
        hidden, saved, spare = forward_use(hidden, weights[i], first_length, host, spare_host)
        heads = spare[0] if spare else None
        kept.append(saved)
    grad = cotangent.astype(F32)
    grad, late, heads_late, small_late, unused = backward_use(
        grad, kept[1], weights[1], first_length, [], 3, None)
    grad, early, heads_early, small_early, (heads_late,) = backward_use(
        grad, kept[0], weights[0], first_length, [heads_late], 4, 7)
    heads_early, small = exchange(
        Scatter, [heads_early, jnp.concatenate([small_early, small_late], axis=1)], 5, "scatter", 4)
    shares = [as_shares(*early, heads_early, small[:, :LANES]),
              as_shares(*late, heads_late, small[:, LANES:])]
    return (hidden.astype(BF), grad.astype(BF), *place_terms(sources, shares))


def solution(mesh):
    rows = P(AX, None)
    flat = P(None, AX)
    deep = P(None, AX, None)
    weights = (flat, flat, deep, flat, flat, deep, flat, flat, flat, deep, flat, deep, flat)
    return jax.shard_map(
        body,
        mesh=mesh,
        in_specs=(rows, rows, P(), P(AX)) + weights,
        out_specs=(rows, rows) + weights,
        check_vma=False,
    )
```

```python
import functools

import jax
import jax.numpy as jnp
from jax import lax
from jax.experimental import pallas as pl
from jax.experimental.pallas import tpu as pltpu
from jax.sharding import PartitionSpec as P

LAYERS = 2
UNIQUE = 4
F32 = jnp.float32
BF = jnp.bfloat16
AX = ("dp", "fsdp")
LANES = 128
EPS = 1e-05

NEG=-1e9
def nt(a,b): return lax.dot_general(a,b,(((1,),(1,)),((),())),preferred_element_type=F32)
def nn(a,b): return lax.dot_general(a,b,(((1,),(0,)),((),())),preferred_element_type=F32)
def halves(x):
    lane=lax.broadcasted_iota(jnp.int32,x.shape,1)
    z=jnp.zeros_like(x)
    return jnp.where(lane<64,x,z), jnp.where(lane<64,z,x)

def fwd_kernel(fl_ref,hid_ref,ga_ref,sa_ref,wq_ref,wk_ref,wv_ref,qb_ref,vb_ref,*rest,bq,host):
    n=host.count
    q_ref,k_ref,v_ref,normed_ref,o_ref,lse_ref=rest[n:n+6]
    jobs=host.enter(rest[:n],rest[n+6:2*n+6],rest[2*n+6:])
    L=q_ref.shape[0]; half=L//2
    @pl.when(pl.program_id(1)==0)
    def _():
        for lo in range(0,L,bq):
            normed_ref[lo:lo+bq,:]=layer_norm(hid_ref[lo:lo+bq,:],ga_ref[...],sa_ref[...]).astype(BF)
    w=jnp.concatenate([wq_ref[...],wk_ref[...],wv_ref[...]],axis=1)
    qkv=nn(normed_ref[...],w)
    q_ref[...]=(qkv[:,:128]+qb_ref[...]).astype(BF)
    k_ref[...]=qkv[:,128:256].astype(BF)
    v_ref[...]=(qkv[:,256:]+vb_ref[...]).astype(BF)
    second=fl_ref[pl.program_id(0)]<L
    shut=jnp.where(second,F32(1e9),F32(0.))
    q=q_ref[...]*BF(0.125); k=k_ref[...]; vT=v_ref[...].T
    sub=lax.broadcasted_iota(jnp.int32,vT.shape,0)
    zero=jnp.zeros_like(vT)
    vTs=(jnp.where(sub<64,vT,zero),jnp.where(sub<64,zero,vT))
    qs=halves(q)
    tri=lax.broadcasted_iota(jnp.int32,(bq,bq),0)<=lax.broadcasted_iota(jnp.int32,(bq,bq),1)
    for j in range(L//bq):
        host.tick(jobs,j)
        lo=j*bq; hi=lo+bq
        acc=jnp.zeros((128,bq),F32)
        for h in range(2):
            qh=qs[h][lo:hi]
            s=nt(k[:hi],qh)
            parts=[]
            if lo>0 : parts.append((0,min(lo,half),s[:min(lo,half)]))
            if lo>half: parts.append((half,lo,s[half:lo]))
            diag=jnp.where(tri,s[lo:],NEG)
            m=jnp.max(diag,axis=0,keepdims=True)
            for a,b,t in parts:
                mt=jnp.max(t,axis=0,keepdims=True)
                if lo>=half and a==0: mt=mt-shut
                m=jnp.maximum(m,mt)
            ps=[]; l=0.
            for a,b,t in parts+[(lo,hi,diag)]:
                mm=m+shut if (lo>=half and a==0) else m
                p=jnp.exp(t-mm)
                l=l+jnp.sum(p,axis=0,keepdims=True)
                ps.append(p.astype(BF))
            p=jnp.concatenate(ps,axis=0) if len(ps)>1 else ps[0]
            oh=nn(vTs[h][:,:hi],p)
            acc=acc+oh*(1.0/l)
            lse_ref[0,h:h+1,lo:hi]=m+jnp.log(l)
        o_ref[lo:hi,:]=acc.T.astype(BF)
    host.leave(jobs)

def attend_fwd(hidden,w,fl,host,bq=256):
    N,D=hidden.shape; R=fl.shape[0]; L=N//R; G=D//128
    col=lambda off: pl.BlockSpec((D,128),lambda r,g,fl:(0,off*G+g))
    blk=pl.BlockSpec((L,128),lambda r,g,fl:(r,g))
    row=pl.BlockSpec((L,D),lambda r,g,fl:(r,0))
    vec=pl.BlockSpec((1,D),lambda r,g,fl:(0,0)); part=pl.BlockSpec((1,128),lambda r,g,fl:(0,g))
    narrow=jax.ShapeDtypeStruct((N,D),BF)
    return pl.pallas_call(functools.partial(fwd_kernel,bq=bq,host=host),
        grid_spec=pltpu.PrefetchScalarGridSpec(num_scalar_prefetch=1,grid=(R,G),
          in_specs=[row,vec,vec,col(0),col(1),col(2),part,part]+host.ins,
          out_specs=[blk,blk,blk,row,blk,pl.BlockSpec((1,2,L),lambda r,g,fl:(r*G+g,0,0))]+host.outs,
          scratch_shapes=host.scratch),
        out_shape=[narrow]*5+[jax.ShapeDtypeStruct((R*G,2,L),F32)]+host.shapes,
        compiler_params=host.params(),
        cost_estimate=pl.CostEstimate(flops=2*2*R*L*L*D*2+6*N*D*D,bytes_accessed=N*D*14,transcendentals=R*L*L*12//2),
        name="attend_fwd")(fl,hidden,w["ga"][None],w["sa"][None],w["heads"],w["heads"],w["heads"],
                           w["qb"][None],w["vb"][None],*host.arrays)

def bwd_kernel(fl_ref,q_ref,k_ref,v_ref,do_ref,lse_ref,normed_ref,wq_ref,wk_ref,wv_ref,*rest,bq,host):
    n=host.count
    gq_ref,gk_ref,gv_ref,da_ref,qb_ref,vb_ref=rest[n:n+6]
    dk_acc,dv_acc,dqkv=rest[2*n+6:2*n+9]
    jobs=host.enter(rest[:n],rest[n+6:2*n+6],rest[2*n+9:])
    L=q_ref.shape[0]; half=L//2
    second=fl_ref[pl.program_id(0)]<L
    shut=jnp.where(second,F32(1e9),F32(0.))
    q=q_ref[...]*BF(0.125); k=k_ref[...]; v=v_ref[...]; do=do_ref[...]
    kT=k.T
    sub=lax.broadcasted_iota(jnp.int32,kT.shape,0); zero=jnp.zeros_like(kT)
    kTs=(jnp.where(sub<64,kT,zero),jnp.where(sub<64,zero,kT))
    qs=halves(q); dos=halves(do)
    tri=lax.broadcasted_iota(jnp.int32,(bq,bq),0)<=lax.broadcasted_iota(jnp.int32,(bq,bq),1)
    nb=L//bq
    for j in reversed(range(nb)):
        host.tick(jobs,nb-1-j)
        lo=j*bq; hi=lo+bq
        dqT=jnp.zeros((128,bq),F32)
        dkp=None; dvp=None
        for h in range(2):
            qh=qs[h][lo:hi]; doh=dos[h][lo:hi]
            lse=lse_ref[0,h:h+1,lo:hi]
            s=nt(k[:hi],qh)
            dp=nt(v[:hi],doh)
            ps=[];
            cuts=[]
            if lo>0: cuts.append((0,min(lo,half)))
            if lo>half: cuts.append((half,lo))
            cuts.append((lo,hi))
            for a,b in cuts:
                ll=lse+shut if (lo>=half and b<=half) else lse
                t=s[a:b]-ll
                if a==lo: t=jnp.where(tri,t,NEG)
                ps.append(jnp.exp(t))
            p=jnp.concatenate(ps,axis=0) if len(ps)>1 else ps[0]
            delta=jnp.sum(p*dp,axis=0,keepdims=True)
            ds=(p*(dp-delta)).astype(BF)
            pb=p.astype(BF)
            dv_=nn(pb,doh); dk_=nn(ds,qh)
            dvp=dv_ if dvp is None else dvp+dv_
            dkp=dk_ if dkp is None else dkp+dk_
            dqT=dqT+nn(kTs[h][:,:hi],ds)
        if j==nb-1:
            dk_acc[...]=dkp; dv_acc[...]=dvp
        else:
            dk_acc[:hi]+=dkp; dv_acc[:hi]+=dvp
        dqkv[lo:hi,:128]=(dqT.T*0.125).astype(BF)
    dqkv[:,128:256]=dk_acc[...].astype(BF); dqkv[:,256:]=dv_acc[...].astype(BF)
    d=dqkv[...]
    qb_ref[0]=jnp.sum(d[:,:128].astype(F32),axis=0,keepdims=True)
    vb_ref[0]=jnp.sum(d[:,256:].astype(F32),axis=0,keepdims=True)
    terms=tn(normed_ref[...],d).astype(BF)
    gq_ref[0]=terms[:,:128]; gk_ref[0]=terms[:,128:256]; gv_ref[0]=terms[:,256:]
    da=nt(d,jnp.concatenate([wq_ref[...],wk_ref[...],wv_ref[...]],axis=1))
    @pl.when(pl.program_id(1)==0)
    def _(): da_ref[...]=da
    @pl.when(pl.program_id(1)>0)
    def _(): da_ref[...]+=da
    host.leave(jobs)

def attend_bwd(q,k,v,do,lse,normed,w,fl,host,bq=256):
    N,D=q.shape; R=fl.shape[0]; L=N//R; G=D//128
    blk=pl.BlockSpec((L,128),lambda r,g,fl:(r,g))
    row=pl.BlockSpec((L,D),lambda r,g,fl:(r,0))
    col=lambda off: pl.BlockSpec((D,128),lambda r,g,fl:(0,off*G+g))
    term=pl.BlockSpec((1,D,128),lambda r,g,fl:(r,0,g)); part=pl.BlockSpec((1,1,128),lambda r,g,fl:(r,0,g))
    gq,gk,gv,da,qb,vb,*more=pl.pallas_call(functools.partial(bwd_kernel,bq=bq,host=host),
        grid_spec=pltpu.PrefetchScalarGridSpec(num_scalar_prefetch=1,grid=(R,G),
          in_specs=[blk]*4+[pl.BlockSpec((1,2,L),lambda r,g,fl:(r*G+g,0,0)),row,col(0),col(1),col(2)]+host.ins,
          out_specs=[term]*3+[row,part,part]+host.outs,
          scratch_shapes=[pltpu.VMEM((L,128),F32),pltpu.VMEM((L,128),F32),pltpu.VMEM((L,384),BF)]+host.scratch),
        out_shape=[jax.ShapeDtypeStruct((R,D,D),BF)]*3+[jax.ShapeDtypeStruct((N,D),F32)]
          +[jax.ShapeDtypeStruct((R,1,D),F32)]*2+host.shapes,
        compiler_params=host.params(),
        cost_estimate=pl.CostEstimate(flops=5*2*R*L*L*D*2+12*N*D*D,bytes_accessed=N*D*16,transcendentals=R*L*L*12//2),
        name="attend_bwd")(fl,q,k,v,do,lse,normed,w["heads"],w["heads"],w["heads"],*host.arrays)
    gq,gk,gv=[t[0] if R==1 else jnp.sum(t.astype(F32),axis=0).astype(BF) for t in (gq,gk,gv)]
    return [gq,gk,gv],da,jnp.sum(qb,axis=(0,1)),jnp.sum(vb,axis=(0,1)),more


def tn(a,b): return lax.dot_general(a,b,(((0,),(0,)),((),())),preferred_element_type=F32)

def feed_fwd_kernel(c_ref,e_ref,eb_ref,s_ref,m_ref,sb_ref,*rest,rows,host):
    n=host.count
    h_ref,u_ref,slope_ref=rest[n:n+3]
    jobs=host.enter(rest[:n],rest[n+3:2*n+3],rest[2*n+3:])
    N=c_ref.shape[0]
    e=e_ref[...]; s=s_ref[...]; eb=eb_ref[...]
    @pl.when(pl.program_id(0)==0)
    def _(): h_ref[...]=m_ref[...]+sb_ref[...]
    for j in range(N//rows):
        host.tick(jobs,j)
        at=slice(j*rows,(j+1)*rows)
        u,slope=gelu_pair(nn(c_ref[at,:],e)+eb)
        u_ref[at,:]=u; slope_ref[at,:]=slope
        h_ref[at,:]+=nn(u,s)
    host.leave(jobs)

def feed_fwd(c,w,middle,host,tile=512,rows=256):
    N,D=c.shape; F=w["expand"].shape[1]
    fixed=lambda r: pl.BlockSpec((r,D),lambda t: (0,0))
    return pl.pallas_call(functools.partial(feed_fwd_kernel,rows=rows,host=host),grid=(F//tile,),
        in_specs=[fixed(N),pl.BlockSpec((D,tile),lambda t:(0,t)),pl.BlockSpec((1,tile),lambda t:(0,t)),
                  pl.BlockSpec((tile,D),lambda t:(t,0)),fixed(N),fixed(1)]+host.ins,
        out_specs=[fixed(N)]+[pl.BlockSpec((N,tile),lambda t:(0,t))]*2+host.outs,
        out_shape=[jax.ShapeDtypeStruct((N,D),F32)]+[jax.ShapeDtypeStruct((N,F),BF)]*2+host.shapes,
        scratch_shapes=host.scratch,compiler_params=host.params(),
        cost_estimate=pl.CostEstimate(flops=4*N*D*F,bytes_accessed=4*N*F+4*D*F,transcendentals=N*F),
        name="feed_fwd")(c,w["expand"],w["eb"][None],w["shrink"],middle,w["sb"][None],*host.arrays)

def feed_bwd_kernel(g_ref,u_ref,slope_ref,c_ref,e_ref,s_ref,*rest,rows,host):
    n=host.count
    dc_ref,de_ref,ds_ref,eb_ref=rest[n:n+4]
    dz_ref=rest[2*n+4]
    jobs=host.enter(rest[:n],rest[n+4:2*n+4],rest[2*n+5:])
    N=c_ref.shape[0]
    e=e_ref[...]; s=s_ref[...]
    @pl.when(pl.program_id(0)==0)
    def _(): dc_ref[...]=jnp.zeros_like(dc_ref)
    total=0.
    for j in range(N//rows):
        host.tick(jobs,j)
        at=slice(j*rows,(j+1)*rows)
        dz=(nt(g_ref[at,:],s)*slope_ref[at,:].astype(F32)).astype(BF)
        dz_ref[at,:]=dz
        total=total+jnp.sum(dz.astype(F32),axis=0,keepdims=True)
        dc_ref[at,:]+=nt(dz,e)
    eb_ref[...]=total
    de_ref[...]=tn(c_ref[...],dz_ref[...]).astype(BF)
    ds_ref[...]=tn(u_ref[...],g_ref[...]).astype(BF)
    host.leave(jobs)

def feed_bwd(g,u,slope,c,w,host,tile=512,rows=256):
    N,D=c.shape; F=u.shape[1]
    fixed=pl.BlockSpec((N,D),lambda t:(0,0))
    wide=lambda r: pl.BlockSpec((r,tile),lambda t:(0,t))
    tall=pl.BlockSpec((tile,D),lambda t:(t,0))
    return pl.pallas_call(functools.partial(feed_bwd_kernel,rows=rows,host=host),grid=(F//tile,),
        in_specs=[fixed,wide(N),wide(N),fixed,wide(D),tall]+host.ins,
        out_specs=[fixed,wide(D),tall,wide(1)]+host.outs,
        out_shape=[jax.ShapeDtypeStruct((N,D),F32),jax.ShapeDtypeStruct((D,F),BF),
                   jax.ShapeDtypeStruct((F,D),BF),jax.ShapeDtypeStruct((1,F),F32)]+host.shapes,
        scratch_shapes=[pltpu.VMEM((N,tile),BF)]+host.scratch,compiler_params=host.params(),
        cost_estimate=pl.CostEstimate(flops=8*N*D*F,bytes_accessed=4*N*F+8*D*F,transcendentals=0),
        name="feed_bwd")(g,u,slope,c,w["expand"],w["shrink"],*host.arrays)


MESH = pl.DeviceIdType.MESH


def block_mesh():
    return lax.axis_size("dp") == 4 and lax.axis_size("fsdp") == 8


class Place:
    def __init__(self):
        d = lax.axis_index("dp")
        f = lax.axis_index("fsdp")
        self.y, self.x = lax.div(d, 2), lax.rem(d, 2)
        self.z, self.c = lax.div(f, 2), lax.rem(f, 2)
        self.zs = [self.z + 1 - 2 * lax.rem(self.z, 2), lax.rem(self.z + 2, 4), 3 - self.z]
        self.to_core = (d, 2 * self.z + 1 - self.c)
        self.to_x = (2 * self.y + 1 - self.x, f)
        self.to_y = (2 * (1 - self.y) + self.x, f)
        self.to_z = [(d, 2 * zz + self.c) for zz in self.zs]

    def greet(self):
        barrier = pltpu.get_barrier_semaphore()
        peers = [self.to_core, self.to_x, self.to_y] + self.to_z
        for peer in peers:
            pl.semaphore_signal(barrier, inc=1, device_id=peer, device_id_type=MESH)
        pl.semaphore_wait(barrier, len(peers))


ALL = slice(None)


class Gather:
    COPIES = 15
    STEPS = 5
    LINKS = (
        (("z", 8, True), ("first", 2, False), ("second", 2, False)),
        (("first", 6, True), ("second", 6, False), ("core", 4, False)),
        (("second", 8, True), ("core", 4, False)),
        (("core", 8, True),),
    )
    STARTS = ((0, 1, 2, 3, 4), (5, 6, 7, 8, 9, 10, 12), (11, 13), (14,), ())
    WAITS = ((), (0, 1, 2), (3, 5, 6, 7), (4, 8, 9, 10, 11), (12, 13, 14))

    def __init__(self, me, shard, out, scratch, cols, x_first, send, recv, local):
        self.send, self.recv = send, recv
        y, x, z, c = me.y, me.x, me.z, me.c
        cols = pl.ds(*cols)
        o = out.at
        tail = (ALL, c, ALL, cols)
        mine = o[y, x, z, c, :, cols]
        self.shard = shard.at[:, cols]
        self.own = pltpu.make_async_copy(self.shard, mine, local)
        if x_first:
            links, near, rest = (me.to_x, me.to_y), (y, 1 - x), (1 - y, ALL)
        else:
            links, near, rest = (me.to_y, me.to_x), (1 - y, x), (ALL, 1 - x)
        came = [o[y, x, zz, c, :, cols] for zz in me.zs]
        self.plan = [(me.to_z[k], mine) for k in range(3)] + [(links[0], mine), (links[1], mine)]
        self.plan += [(links[0], r) for r in came] + [(links[1], r) for r in came]
        self.plan += [(links[1], o[near + tail]), (me.to_core, o[(y, x) + tail]),
                      (me.to_core, o[near + tail]), (me.to_core, o[rest + tail])]

    def copy(self, k):
        peer, ref = self.plan[k]
        return pltpu.make_async_remote_copy(
            src_ref=self.shard if k < 5 else ref, dst_ref=ref, send_sem=self.send.at[k],
            recv_sem=self.recv.at[k], device_id=peer, device_id_type=MESH)

    def run(self, step):
        if step == 0:
            self.own.start()
        for k in self.WAITS[step]:
            self.copy(k).wait_recv()
        if step == 1:
            self.own.wait()
        for k in self.STARTS[step]:
            self.copy(k).start()
        if step == 4:
            for k in range(self.COPIES):
                self.copy(k).wait_send()


class Scatter:
    COPIES = 7
    STEPS = 5
    LINKS = (
        (("core", 16, True),),
        (("first", 8, True), ("first", 8, False)),
        (("second", 8, True),),
        (("z", 8, True),),
    )

    def __init__(self, me, term, out, scratch, cols, x_first, send, recv, local):
        self.me, self.out = me, out
        self.own, self.r = scratch[0], scratch[1:]
        self.send, self.recv = send, recv
        self.cols, self.x_first = pl.ds(*cols), x_first
        own, (r0, r1, r2, r3) = self.own, self.r
        y, x, z, c = me.y, me.x, me.z, me.c
        self.mine = pltpu.make_async_copy(term.at[ALL, ALL, ALL, c, :, self.cols], own, local)
        if x_first:
            first, second, near, across = me.to_x, me.to_y, own.at[y, 1 - x], own.at[1 - y, x]
        else:
            first, second, near, across = me.to_y, me.to_x, own.at[1 - y, x], own.at[y, 1 - x]
        self.plan = [
            (term.at[ALL, ALL, ALL, 1 - c, :, self.cols], me.to_core, r0),
            (own.at[1 - y, 1 - x], first, r1.at[0]), (near, first, r1.at[1]), (across, second, r2)] + [
            (own.at[y, x, me.zs[k]], me.to_z[k], r3.at[k]) for k in range(3)]

    def copy(self, k):
        src, peer, dst = self.plan[k]
        return pltpu.make_async_remote_copy(
            src_ref=src, dst_ref=dst, send_sem=self.send.at[k], recv_sem=self.recv.at[k],
            device_id=peer, device_id_type=MESH)

    def run(self, step):
        y, x, z = self.me.y, self.me.x, self.me.z
        own, (r0, r1, r2, r3) = self.own, self.r
        if step == 0:
            self.mine.start()
            self.copy(0).start()
        elif step == 1:
            self.mine.wait()
            self.copy(0).wait_recv()

            @pl.loop(0, 4)
            def _(k):
                for a in range(2):
                    for b in range(2):
                        own[a, b, k] = own[a, b, k] + r0[a, b, k]

            self.copy(1).start()
            self.copy(2).start()
        elif step == 2:
            self.copy(1).wait_recv()
            ay, ax = (1 - y, x) if self.x_first else (y, 1 - x)

            @pl.loop(0, 4)
            def _(k):
                own[ay, ax, k] = own[ay, ax, k] + r1[0, k]

            self.copy(3).start()
        elif step == 3:
            self.copy(2).wait_recv()
            self.copy(3).wait_recv()

            @pl.loop(0, 4)
            def _(k):
                total = own[y, x, k].astype(F32) + r1[1, k].astype(F32) + r2[k].astype(F32)
                own[y, x, k] = total.astype(own.dtype)

            for k in (4, 5, 6):
                self.copy(k).start()
        else:
            total = own[y, x, z].astype(F32)
            for k in (4, 5, 6):
                self.copy(k).wait_recv()
                total = total + r3[k - 4].astype(F32)
            self.out[:, self.cols] = total
            for k in range(self.COPIES):
                self.copy(k).wait_send()


RATES = {"c": 500e3, "z": 78e3, "x": 83e3}
DELAY = 2.0
ENTRY = 0.0
COST = {Gather: 0.1, Scatter: 0.2}


def cut_jobs(arrays, kind, pieces):
    jobs = []
    for i, a in enumerate(arrays):
        units = a.shape[-1] // 128
        n = min(pieces, units)
        start = 0
        for k in range(n):
            width = 128 * (units // n + (1 if k < units % n else 0))
            jobs.append((i, (start, width), len(jobs) % 2 == 0))
            start += width
    return jobs


def plan_jobs(kind, jobs, rows, slots, window):
    free = dict.fromkeys("xyzc", 0.0)
    ready = {}

    def start(i, step, now):
        array, (unused, width), x_first = jobs[i]
        done = now
        names = {"z": "z", "core": "c", "first": "x" if x_first else "y", "second": "y" if x_first else "x"}
        if step < len(kind.LINKS):
            for link, blocks, counts in kind.LINKS[step]:
                name = names[link]
                rate = RATES.get(name, RATES["x"])
                free[name] = max(free[name], now) + blocks * rows[array] * width * 2 / rate
                if counts:
                    done = max(done, free[name])
        if step < kind.STEPS - 1:
            ready[i, step + 1] = done + DELAY
        if step == 1 and i + window < len(jobs):
            ready[i + window, 0] = now

    for i in range(min(window, len(jobs))):
        ready[i, 0] = 0.0
    now, plan = ENTRY, []
    cost = COST[kind]
    for length in slots:
        todo = []
        while True:
            can = sorted((e for e in ready if ready[e] <= now and e[1] < kind.STEPS - 1), key=lambda e: (-e[1], e[0]))
            if not can:
                break
            ready.pop(can[0])
            now += cost
            start(*can[0], now)
            todo.append(can[0])
        plan.append(todo)
        now += length
    todo = []
    while ready:
        e = min(ready, key=lambda e: (max(ready[e], now), -e[1], e[0]))
        now = max(ready.pop(e), now) + cost
        start(*e, now)
        todo.append(e)
    return plan + [todo]


class Host:
    def __init__(self, kind=None, arrays=(), ident=None, slots=(), per=1, axis=1, pieces=None, window=None):
        self.kind, self.ident, self.per, self.axis = kind, ident, per, axis
        self.used = bool(arrays) and block_mesh()
        self.source = list(arrays)
        self.arrays, self.ins, self.outs, self.shapes, self.scratch = [], [], [], [], []
        if self.used:
            self.build(arrays, slots, pieces, window)
        self.count = len(self.arrays)

    def build(self, arrays, slots, pieces, window):
        kind = self.kind
        if kind is Scatter:
            arrays = [a.reshape(2, 2, 4, 2, -1, a.shape[-1]) for a in arrays]
        self.arrays = arrays = list(arrays)
        n = len(arrays)
        pieces = pieces or (2 if kind is Gather else 4)
        self.jobs = jobs = cut_jobs(arrays, kind, pieces)
        rows = [a.shape[-2] * a.dtype.itemsize // 2 for a in arrays]
        self.plan = plan_jobs(kind, jobs, rows, slots, window or (8 if kind is Gather else 4))
        m = len(jobs)
        any_space, vmem = pl.BlockSpec(memory_space=pl.ANY), pl.BlockSpec(memory_space=pltpu.VMEM)
        if kind is Gather:
            self.ins, self.outs = [vmem] * n, [any_space] * n
            self.shapes = [jax.ShapeDtypeStruct((2, 2, 4, 2) + a.shape, a.dtype) for a in arrays]
        else:
            self.ins, self.outs = [any_space] * n, [vmem] * n
            self.shapes = [jax.ShapeDtypeStruct(a.shape[4:], F32) for a in arrays]
            for i, (unused, width), unused in jobs:
                for lead in ((2, 2, 4), (2, 2, 4), (2, 4), (4,), (3,)):
                    self.scratch.append(pltpu.VMEM(lead + (arrays[i].shape[-2], width), arrays[i].dtype))
        self.scratch = self.scratch + [
            pltpu.SemaphoreType.DMA((m, kind.COPIES)), pltpu.SemaphoreType.DMA((m, kind.COPIES)),
            pltpu.SemaphoreType.DMA((m,))]

    def params(self):
        if not self.used:
            return pltpu.CompilerParams(vmem_limit_bytes=48 << 20)
        return pltpu.CompilerParams(
            collective_id=self.ident, has_side_effects=True, vmem_limit_bytes=56 << 20)

    def enter(self, ins, outs, scratch):
        if not self.used:
            return None
        me = Place()
        send, recv, local = scratch[-3:]
        work = []
        for k, (i, cols, x_first) in enumerate(self.jobs):
            own = scratch[5 * k : 5 * k + 5] if self.kind is Scatter else ()
            work.append(self.kind(me, ins[i], outs[i], own, cols, x_first, send.at[k], recv.at[k], local.at[k]))
        self.now = pl.program_id(self.axis)

        @pl.when(self.now == 0)
        def _():
            me.greet()

        return work

    def tick(self, work, at):
        if not self.used:
            return
        for g in range((len(self.plan) - 1) // self.per):
            todo = self.plan[g * self.per + at]
            if todo:
                @pl.when(self.now == g)
                def _():
                    for i, t in todo:
                        work[i].run(t)

    def leave(self, work):
        if not self.used:
            return

        @pl.when(self.now == (len(self.plan) - 1) // self.per - 1)
        def _():
            for i, t in self.plan[-1]:
                work[i].run(t)

    def results(self, values):
        if self.used and self.kind is Gather:
            return [w.reshape(-1, w.shape[-1]) for w in values]
        if self.used:
            return list(values)
        return plain(self.kind, self.source) if self.source else []


def plain(kind, arrays):
    if kind is Gather:
        return [lax.all_gather(a, AX, axis=0, tiled=True) for a in arrays]
    return [lax.psum_scatter(t.astype(F32), AX, scatter_dimension=0, tiled=True) for t in arrays]


def alone_kernel(*refs, host):
    n = host.count
    jobs = host.enter(refs[:n], refs[n : 2 * n], refs[2 * n :])
    host.tick(jobs, 0)
    host.leave(jobs)


def exchange(kind, arrays, ident, name, pieces):
    host = Host(kind, arrays, ident, [0.0], axis=0, pieces=pieces)
    if not host.used:
        return plain(kind, arrays)
    return host.results(pl.pallas_call(
        functools.partial(alone_kernel, host=host), grid=(1,),
        in_specs=host.ins, out_specs=host.outs, out_shape=host.shapes, scratch_shapes=host.scratch,
        compiler_params=host.params(), name=name)(*host.arrays))


def layer_norm(values, gain, shift):
    centre = values - jnp.mean(values, axis=-1, keepdims=True)
    spread = jnp.mean(centre * centre, axis=-1, keepdims=True)
    return centre * lax.rsqrt(spread + EPS) * gain + shift


def inner_rows(left, right):
    return lax.dot_general(left, right, (((0,), (0,)), ((), ())), preferred_element_type=F32)


def times_transposed(left, right):
    return lax.dot_general(left, right, (((1,), (1,)), ((), ())), preferred_element_type=F32)


def column_sums(values):
    return jnp.sum(values.astype(F32), axis=0)


def gelu_pair(z):
    c = 0.7978845608028654
    t = jnp.tanh(c * (z + 0.044715 * z * z * z))
    value = 0.5 * z * (1.0 + t)
    slope = 0.5 * (1.0 + t) + 0.5 * z * (1.0 - t * t) * c * (1.0 + 3 * 0.044715 * z * z)
    return value.astype(BF), slope.astype(BF)


def pack_columns(vectors, wide, count):
    length = vectors[0].shape[0]
    ways = wide.shape[0] // length
    per = length // count
    spread = wide.reshape(count, ways, per).transpose(0, 2, 1).reshape(length, ways)
    block = jnp.concatenate([jnp.stack(vectors, axis=1), spread], axis=1)
    return jnp.pad(block, ((0, 0), (0, LANES - block.shape[1])))


def unpack_columns(block, vector_count, ways, count):
    length = block.shape[0]
    turned = block[:, : vector_count + ways].T
    wide = turned[vector_count:].reshape(ways, count, length // count).transpose(1, 0, 2).reshape(-1)
    return [turned[i] for i in range(vector_count)], wide


def local_shards(local):
    (ga, sa, hw, qb, vb, mw, mb, gf, sf, ew, eb, sw, sb) = local
    small = pack_columns([ga, sa, qb, vb, mb, gf, sf, sb], eb, 1)
    return [jnp.concatenate([hw, small], axis=1), mw, ew, sw]


def use_heads(heads, width, ways):
    vecs, wide = unpack_columns(heads[:, 3 * width :], 8, ways, lax.axis_size(AX))
    vecs = [v.astype(F32) for v in vecs]
    return dict(zip(("ga", "sa", "qb", "vb", "mb", "gf", "sf", "sb"), vecs), eb=wide.astype(F32),
                heads=heads)


def forward_use(hidden, w, first_len, host, spare_host):
    q, k, v, normed, attended, lse, *more = attend_fwd(hidden, w, first_len, host)
    more = host.results(more)
    w.update(expand=more[0], shrink=more[1], mix=more[-1])
    middle = hidden + jnp.dot(attended, w["mix"], preferred_element_type=F32) + w["mb"]
    normed_two = layer_norm(middle, w["gf"], w["sf"]).astype(BF)
    result, activated, slope, *spare = feed_fwd(normed_two, w, middle, spare_host)
    kept = (hidden, normed, (q, k, v), attended, lse, middle, normed_two, activated, slope)
    return result, kept, spare_host.results(spare)


def backward_use(grad_out, kept, w, first_len, carried, ident, spare_ident):
    hidden, normed, qkv, attended, lse, middle, normed_two, activated, slope = kept
    count = lax.axis_size(AX)
    grad_low = grad_out.astype(BF)
    sb = column_sums(grad_low)
    spare = Host(Scatter, carried, spare_ident, FEED_BACKWARD_SLOTS, per=4, axis=0, pieces=2, window=2)
    dc, expand_term, shrink_term, eb, *carried = feed_bwd(grad_low, activated, slope, normed_two, w, spare)
    carried = spare.results(carried)
    eb = eb[0]
    unused, norm_back = jax.vjp(layer_norm, middle, w["gf"], w["sf"])
    middle_norm, gf, sf = norm_back(dc)
    dm = grad_out + middle_norm
    dmb = dm.astype(BF)
    mix_term = inner_rows(attended, dmb).astype(BF)
    mb = column_sums(dmb)
    do = times_transposed(dmb, w["mix"]).astype(BF)
    host = Host(Scatter, [shrink_term, mix_term, expand_term], ident, BACKWARD_SLOTS, per=4,
                pieces=8, window=3)
    heads_terms, da, qb, vb, more = attend_bwd(*qkv, do, lse, normed, w, first_len, host)
    more = host.results(more)
    unused, first_back = jax.vjp(layer_norm, hidden, w["ga"], w["sa"])
    hidden_norm, ga, sa = first_back(da)
    small = pack_columns([ga, sa, qb, vb, mb, gf, sf, sb], eb, count)
    return dm + hidden_norm, more, heads_terms, small, carried


def as_shares(shrink, mix, expand, heads, small):
    heads = jnp.concatenate(heads, axis=1)
    vecs, wide = unpack_columns(small, 8, shrink.shape[0] // mix.shape[0], 1)
    ga, sa, qb, vb, mb, gf, sf, sb = vecs
    return ga, sa, heads, qb, vb, mix, mb, gf, sf, expand, wide, shrink, sb


FORWARD_SLOTS = [1.6, 0.86, 1.29, 1.72] * 6
BACKWARD_SLOTS = [1.8, 1.35, 0.9, 2.9] * 6
FEED_FORWARD_SLOTS = [0.95, 0.95, 0.95, 0.95] * 6
FEED_BACKWARD_SLOTS = [0.7, 0.7, 0.7, 2.3] * 6


def pick_shards(stacks, source):
    return tuple(lax.dynamic_index_in_dim(stack, source, 0, keepdims=False) for stack in stacks)


def place_terms(sources, shares):
    ids = lax.iota(jnp.int32, UNIQUE)
    out = []
    for items in zip(*shares):
        total = 0.0
        for source, item in zip(sources, items):
            chosen = (ids == source).reshape((UNIQUE,) + (1,) * item.ndim)
            total = total + jnp.where(chosen, item[None], 0.0)
        out.append(total)
    return out


def body(tokens, cotangent, tie_map, first_length, *stacks):
    hidden = tokens.astype(F32)
    width = hidden.shape[1]
    sources = [tie_map[i] for i in range(LAYERS)]
    shards = [local_shards(pick_shards(stacks, s)) for s in sources]
    ways = shards[0][3].shape[0] // shards[0][0].shape[0]
    (heads,) = exchange(Gather, shards[0][:1], 0, "gather", 4)
    kept, weights = [], []
    for i in range(LAYERS):
        weights.append(use_heads(heads, width, ways))
        host = Host(Gather, shards[i][2:] + shards[i][1:2], 1 + i, FORWARD_SLOTS, per=4, pieces=4, window=12)
        later = shards[i + 1][:1] if i + 1 < LAYERS else []
        spare_host = Host(Gather, later, 6, FEED_FORWARD_SLOTS, per=4, axis=0, pieces=5, window=4)
        hidden, saved, spare = forward_use(hidden, weights[i], first_length, host, spare_host)
        heads = spare[0] if spare else None
        kept.append(saved)
    grad = cotangent.astype(F32)
    grad, late, heads_late, small_late, unused = backward_use(
        grad, kept[1], weights[1], first_length, [], 3, None)
    grad, early, heads_early, small_early, heads_late = backward_use(
        grad, kept[0], weights[0], first_length, heads_late, 4, 7)
    *heads_early, small = exchange(
        Scatter, heads_early + [jnp.concatenate([small_early, small_late], axis=1)], 5, "scatter", 3)
    shares = [as_shares(*early, heads_early, small[:, :LANES]),
              as_shares(*late, heads_late, small[:, LANES:])]
    return (hidden.astype(BF), grad.astype(BF), *place_terms(sources, shares))


def solution(mesh):
    rows = P(AX, None)
    flat = P(None, AX)
    deep = P(None, AX, None)
    weights = (flat, flat, deep, flat, flat, deep, flat, flat, flat, deep, flat, deep, flat)
    return jax.shard_map(
        body,
        mesh=mesh,
        in_specs=(rows, rows, P(), P(AX)) + weights,
        out_specs=(rows, rows) + weights,
        check_vma=False,
    )
```

```python
import functools

import jax
import jax.numpy as jnp
from jax import lax
from jax.experimental import pallas as pl
from jax.experimental.pallas import tpu as pltpu
from jax.sharding import PartitionSpec as P

LAYERS = 2
UNIQUE = 4
F32 = jnp.float32
BF = jnp.bfloat16
AX = ("dp", "fsdp")
LANES = 128
EPS = 1e-05

NEG=-1e9
def nt(a,b): return lax.dot_general(a,b,(((1,),(1,)),((),())),preferred_element_type=F32)
def nn(a,b): return lax.dot_general(a,b,(((1,),(0,)),((),())),preferred_element_type=F32)
def halves(x):
    lane=lax.broadcasted_iota(jnp.int32,x.shape,1)
    z=jnp.zeros_like(x)
    return jnp.where(lane<64,x,z), jnp.where(lane<64,z,x)

def fwd_kernel(fl_ref,hid_ref,vec_ref,wq_ref,wk_ref,wv_ref,part_ref,*rest,bq,host):
    n=host.count
    q_ref,k_ref,v_ref,normed_ref,o_ref,lse_ref=rest[n:n+6]
    jobs=host.enter(rest[:n],rest[n+6:2*n+6],rest[2*n+6:])
    L=q_ref.shape[0]; half=L//2
    @pl.when(pl.program_id(1)==0)
    def _():
        for lo in range(0,L,bq):
            normed_ref[lo:lo+bq,:]=layer_norm(hid_ref[lo:lo+bq,:].astype(F32),vec_ref[0:1,:],vec_ref[1:2,:]).astype(BF)
    w=jnp.concatenate([wq_ref[...],wk_ref[...],wv_ref[...]],axis=1)
    qkv=nn(normed_ref[...],w)
    q_ref[...]=(qkv[:,:128]+part_ref[2:3,:]).astype(BF)
    k_ref[...]=qkv[:,128:256].astype(BF)
    v_ref[...]=(qkv[:,256:]+part_ref[3:4,:]).astype(BF)
    second=fl_ref[pl.program_id(0)]<L
    shut=jnp.where(second,F32(1e9),F32(0.))
    q=q_ref[...]*BF(0.125); k=k_ref[...]; vT=v_ref[...].T
    sub=lax.broadcasted_iota(jnp.int32,vT.shape,0)
    zero=jnp.zeros_like(vT)
    vTs=(jnp.where(sub<64,vT,zero),jnp.where(sub<64,zero,vT))
    qs=halves(q)
    tri=lax.broadcasted_iota(jnp.int32,(bq,bq),0)<=lax.broadcasted_iota(jnp.int32,(bq,bq),1)
    for j in range(L//bq):
        host.tick(jobs,j)
        lo=j*bq; hi=lo+bq
        acc=jnp.zeros((128,bq),F32)
        for h in range(2):
            qh=qs[h][lo:hi]
            s=nt(k[:hi],qh)
            parts=[]
            if lo>0 : parts.append((0,min(lo,half),s[:min(lo,half)]))
            if lo>half: parts.append((half,lo,s[half:lo]))
            diag=jnp.where(tri,s[lo:],NEG)
            m=jnp.max(diag,axis=0,keepdims=True)
            for a,b,t in parts:
                mt=jnp.max(t,axis=0,keepdims=True)
                if lo>=half and a==0: mt=mt-shut
                m=jnp.maximum(m,mt)
            ps=[]; l=0.
            for a,b,t in parts+[(lo,hi,diag)]:
                mm=m+shut if (lo>=half and a==0) else m
                p=jnp.exp(t-mm)
                l=l+jnp.sum(p,axis=0,keepdims=True)
                ps.append(p.astype(BF))
            p=jnp.concatenate(ps,axis=0) if len(ps)>1 else ps[0]
            oh=nn(vTs[h][:,:hi],p)
            acc=acc+oh*(1.0/l)
            lse_ref[0,h:h+1,lo:hi]=m+jnp.log(l)
        o_ref[lo:hi,:]=acc.T.astype(BF)
    host.leave(jobs)

def attend_fwd(hidden,w,fl,host,bq=256):
    N,D=hidden.shape; R=fl.shape[0]; L=N//R; G=D//128
    col=lambda off: pl.BlockSpec((D,128),lambda r,g,fl:(0,off*G+g))
    blk=pl.BlockSpec((L,128),lambda r,g,fl:(r,g))
    row=pl.BlockSpec((L,D),lambda r,g,fl:(r,0))
    vec=pl.BlockSpec((8,D),lambda r,g,fl:(0,0)); part=pl.BlockSpec((8,128),lambda r,g,fl:(0,g))
    narrow=jax.ShapeDtypeStruct((N,D),BF)
    return pl.pallas_call(functools.partial(fwd_kernel,bq=bq,host=host),
        grid_spec=pltpu.PrefetchScalarGridSpec(num_scalar_prefetch=1,grid=(R,G),
          in_specs=[row,vec,col(0),col(1),col(2),part]+host.ins,
          out_specs=[blk,blk,blk,row,blk,pl.BlockSpec((1,2,L),lambda r,g,fl:(r*G+g,0,0))]+host.outs,
          scratch_shapes=host.scratch),
        out_shape=[narrow]*5+[jax.ShapeDtypeStruct((R*G,2,L),F32)]+host.shapes,
        compiler_params=host.params(),
        cost_estimate=pl.CostEstimate(flops=2*2*R*L*L*D*2+6*N*D*D,bytes_accessed=N*D*14,transcendentals=R*L*L*12//2),
        name="attend_fwd")(fl,hidden,w["vecs"],w["heads"],w["heads"],w["heads"],w["vecs"],*host.arrays)

def bwd_kernel(fl_ref,q_ref,k_ref,v_ref,dm_ref,mix_ref,lse_ref,normed_ref,wq_ref,wk_ref,wv_ref,*rest,bq,host):
    n=host.count
    gq_ref,gk_ref,gv_ref,da_ref,qb_ref,vb_ref=rest[n:n+6]
    dk_acc,dv_acc,dqkv=rest[2*n+6:2*n+9]
    jobs=host.enter(rest[:n],rest[n+6:2*n+6],rest[2*n+9:])
    L=q_ref.shape[0]; half=L//2
    second=fl_ref[pl.program_id(0)]<L
    shut=jnp.where(second,F32(1e9),F32(0.))
    q=q_ref[...]*BF(0.125); k=k_ref[...]; v=v_ref[...]; do=nt(dm_ref[...],mix_ref[...]).astype(BF)
    kT=k.T
    sub=lax.broadcasted_iota(jnp.int32,kT.shape,0); zero=jnp.zeros_like(kT)
    kTs=(jnp.where(sub<64,kT,zero),jnp.where(sub<64,zero,kT))
    qs=halves(q); dos=halves(do)
    tri=lax.broadcasted_iota(jnp.int32,(bq,bq),0)<=lax.broadcasted_iota(jnp.int32,(bq,bq),1)
    nb=L//bq
    for j in reversed(range(nb)):
        host.tick(jobs,nb-1-j)
        lo=j*bq; hi=lo+bq
        dqT=jnp.zeros((128,bq),F32)
        dkp=None; dvp=None
        for h in range(2):
            qh=qs[h][lo:hi]; doh=dos[h][lo:hi]
            lse=lse_ref[0,h:h+1,lo:hi]
            s=nt(k[:hi],qh)
            dp=nt(v[:hi],doh)
            ps=[];
            cuts=[]
            if lo>0: cuts.append((0,min(lo,half)))
            if lo>half: cuts.append((half,lo))
            cuts.append((lo,hi))
            for a,b in cuts:
                ll=lse+shut if (lo>=half and b<=half) else lse
                t=s[a:b]-ll
                if a==lo: t=jnp.where(tri,t,NEG)
                ps.append(jnp.exp(t))
            p=jnp.concatenate(ps,axis=0) if len(ps)>1 else ps[0]
            delta=jnp.sum(p*dp,axis=0,keepdims=True)
            ds=(p*(dp-delta)).astype(BF)
            pb=p.astype(BF)
            dv_=nn(pb,doh); dk_=nn(ds,qh)
            dvp=dv_ if dvp is None else dvp+dv_
            dkp=dk_ if dkp is None else dkp+dk_
            dqT=dqT+nn(kTs[h][:,:hi],ds)
        if j==nb-1:
            dk_acc[...]=dkp; dv_acc[...]=dvp
        else:
            dk_acc[:hi]+=dkp; dv_acc[:hi]+=dvp
        dqkv[lo:hi,:128]=(dqT.T*0.125).astype(BF)
    dqkv[:,128:256]=dk_acc[...].astype(BF); dqkv[:,256:]=dv_acc[...].astype(BF)
    d=dqkv[...]
    qb_ref[0]=jnp.sum(d[:,:128].astype(F32),axis=0,keepdims=True)
    vb_ref[0]=jnp.sum(d[:,256:].astype(F32),axis=0,keepdims=True)
    terms=tn(normed_ref[...],d).astype(BF)
    gq_ref[0]=terms[:,:128]; gk_ref[0]=terms[:,128:256]; gv_ref[0]=terms[:,256:]
    da=nt(d,jnp.concatenate([wq_ref[...],wk_ref[...],wv_ref[...]],axis=1))
    @pl.when(pl.program_id(1)==0)
    def _(): da_ref[...]=da
    @pl.when(pl.program_id(1)>0)
    def _(): da_ref[...]+=da
    host.leave(jobs)

def attend_bwd(q,k,v,dmb,lse,normed,w,fl,host,bq=256):
    N,D=q.shape; R=fl.shape[0]; L=N//R; G=D//128
    blk=pl.BlockSpec((L,128),lambda r,g,fl:(r,g))
    row=pl.BlockSpec((L,D),lambda r,g,fl:(r,0))
    col=lambda off: pl.BlockSpec((D,128),lambda r,g,fl:(0,off*G+g))
    term=pl.BlockSpec((1,D,128),lambda r,g,fl:(r,0,g)); part=pl.BlockSpec((1,1,128),lambda r,g,fl:(r,0,g))
    gq,gk,gv,da,qb,vb,*more=pl.pallas_call(functools.partial(bwd_kernel,bq=bq,host=host),
        grid_spec=pltpu.PrefetchScalarGridSpec(num_scalar_prefetch=1,grid=(R,G),
          in_specs=[blk]*3+[row,pl.BlockSpec((128,D),lambda r,g,fl:(g,0)),pl.BlockSpec((1,2,L),lambda r,g,fl:(r*G+g,0,0)),row,col(0),col(1),col(2)]+host.ins,
          out_specs=[term]*3+[row,part,part]+host.outs,
          scratch_shapes=[pltpu.VMEM((L,128),F32),pltpu.VMEM((L,128),F32),pltpu.VMEM((L,384),BF)]+host.scratch),
        out_shape=[jax.ShapeDtypeStruct((R,D,D),BF)]*3+[jax.ShapeDtypeStruct((N,D),F32)]
          +[jax.ShapeDtypeStruct((R,1,D),F32)]*2+host.shapes,
        compiler_params=host.params(),
        cost_estimate=pl.CostEstimate(flops=5*2*R*L*L*D*2+12*N*D*D,bytes_accessed=N*D*16,transcendentals=R*L*L*12//2),
        name="attend_bwd")(fl,q,k,v,dmb,w["mix"],lse,normed,w["heads"],w["heads"],w["heads"],*host.arrays)
    gq,gk,gv=[t[0] if R==1 else jnp.sum(t.astype(F32),axis=0).astype(BF) for t in (gq,gk,gv)]
    return [gq,gk,gv],da,jnp.sum(qb,axis=(0,1)),jnp.sum(vb,axis=(0,1)),more


def tn(a,b): return lax.dot_general(a,b,(((0,),(0,)),((),())),preferred_element_type=F32)

def feed_fwd_kernel(c_ref,e_ref,eb_ref,s_ref,m_ref,sb_ref,*rest,rows,host):
    n=host.count
    h_ref,u_ref,slope_ref=rest[n:n+3]
    jobs=host.enter(rest[:n],rest[n+3:2*n+3],rest[2*n+3:])
    N=c_ref.shape[0]
    e=e_ref[...]; s=s_ref[...]; eb=eb_ref[...]
    @pl.when(pl.program_id(0)==0)
    def _(): h_ref[...]=m_ref[...]+sb_ref[7:8,:]
    for j in range(N//rows):
        host.tick(jobs,j)
        at=slice(j*rows,(j+1)*rows)
        u,slope=gelu_pair(nn(c_ref[at,:],e)+eb)
        u_ref[at,:]=u; slope_ref[at,:]=slope
        h_ref[at,:]+=nn(u,s)
    host.leave(jobs)

def feed_fwd(c,w,middle,host,tile=512,rows=256):
    N,D=c.shape; F=w["expand"].shape[1]
    fixed=lambda r: pl.BlockSpec((r,D),lambda t: (0,0))
    return pl.pallas_call(functools.partial(feed_fwd_kernel,rows=rows,host=host),grid=(F//tile,),
        in_specs=[fixed(N),pl.BlockSpec((D,tile),lambda t:(0,t)),pl.BlockSpec((1,tile),lambda t:(0,t)),
                  pl.BlockSpec((tile,D),lambda t:(t,0)),fixed(N),fixed(8)]+host.ins,
        out_specs=[fixed(N)]+[pl.BlockSpec((N,tile),lambda t:(0,t))]*2+host.outs,
        out_shape=[jax.ShapeDtypeStruct((N,D),F32)]+[jax.ShapeDtypeStruct((N,F),BF)]*2+host.shapes,
        scratch_shapes=host.scratch,compiler_params=host.params(),
        cost_estimate=pl.CostEstimate(flops=4*N*D*F,bytes_accessed=4*N*F+4*D*F,transcendentals=N*F),
        name="feed_fwd")(c,w["expand"],w["eb"],w["shrink"],middle,w["vecs"],*host.arrays)

def feed_bwd_kernel(g_ref,u_ref,slope_ref,c_ref,e_ref,s_ref,*rest,rows,host):
    n=host.count
    dc_ref,de_ref,ds_ref,eb_ref=rest[n:n+4]
    dz_ref=rest[2*n+4]
    jobs=host.enter(rest[:n],rest[n+4:2*n+4],rest[2*n+5:])
    N=c_ref.shape[0]
    e=e_ref[...]; s=s_ref[...]
    @pl.when(pl.program_id(0)==0)
    def _(): dc_ref[...]=jnp.zeros_like(dc_ref)
    total=0.
    for j in range(N//rows):
        host.tick(jobs,j)
        at=slice(j*rows,(j+1)*rows)
        dz=(nt(g_ref[at,:],s)*slope_ref[at,:].astype(F32)).astype(BF)
        dz_ref[at,:]=dz
        total=total+jnp.sum(dz.astype(F32),axis=0,keepdims=True)
        dc_ref[at,:]+=nt(dz,e)
    eb_ref[...]=total
    de_ref[...]=tn(c_ref[...],dz_ref[...]).astype(BF)
    ds_ref[...]=tn(u_ref[...],g_ref[...]).astype(BF)
    host.leave(jobs)

def feed_bwd(g,u,slope,c,w,host,tile=512,rows=256):
    N,D=c.shape; F=u.shape[1]
    fixed=pl.BlockSpec((N,D),lambda t:(0,0))
    wide=lambda r: pl.BlockSpec((r,tile),lambda t:(0,t))
    tall=pl.BlockSpec((tile,D),lambda t:(t,0))
    return pl.pallas_call(functools.partial(feed_bwd_kernel,rows=rows,host=host),grid=(F//tile,),
        in_specs=[fixed,wide(N),wide(N),fixed,wide(D),tall]+host.ins,
        out_specs=[fixed,wide(D),tall,wide(1)]+host.outs,
        out_shape=[jax.ShapeDtypeStruct((N,D),F32),jax.ShapeDtypeStruct((D,F),BF),
                   jax.ShapeDtypeStruct((F,D),BF),jax.ShapeDtypeStruct((1,F),F32)]+host.shapes,
        scratch_shapes=[pltpu.VMEM((N,tile),BF)]+host.scratch,compiler_params=host.params(),
        cost_estimate=pl.CostEstimate(flops=8*N*D*F,bytes_accessed=4*N*F+8*D*F,transcendentals=0),
        name="feed_bwd")(g,u,slope,c,w["expand"],w["shrink"],*host.arrays)


MESH = pl.DeviceIdType.MESH


def block_mesh():
    return lax.axis_size("dp") == 4 and lax.axis_size("fsdp") == 8


class Place:
    def __init__(self):
        d = lax.axis_index("dp")
        f = lax.axis_index("fsdp")
        self.y, self.x = lax.div(d, 2), lax.rem(d, 2)
        self.z, self.c = lax.div(f, 2), lax.rem(f, 2)
        self.zs = [self.z + 1 - 2 * lax.rem(self.z, 2), lax.rem(self.z + 2, 4), 3 - self.z]
        self.to_core = (d, 2 * self.z + 1 - self.c)
        self.to_x = (2 * self.y + 1 - self.x, f)
        self.to_y = (2 * (1 - self.y) + self.x, f)
        self.to_z = [(d, 2 * zz + self.c) for zz in self.zs]

    def greet(self):
        barrier = pltpu.get_barrier_semaphore()
        peers = [self.to_core, self.to_x, self.to_y] + self.to_z
        for peer in peers:
            pl.semaphore_signal(barrier, inc=1, device_id=peer, device_id_type=MESH)
        pl.semaphore_wait(barrier, len(peers))


ALL = slice(None)


class Gather:
    COPIES = 15
    STEPS = 5
    LINKS = (
        (("z", 8, True), ("first", 2, False), ("second", 2, False)),
        (("first", 6, True), ("second", 6, False), ("core", 4, False)),
        (("second", 8, True), ("core", 4, False)),
        (("core", 8, True),),
    )
    STARTS = ((0, 1, 2, 3, 4), (5, 6, 7, 8, 9, 10, 12), (11, 13), (14,), ())
    WAITS = ((), (0, 1, 2), (3, 5, 6, 7), (4, 8, 9, 10, 11), (12, 13, 14))

    def __init__(self, me, shard, out, scratch, cols, x_first, send, recv, local):
        self.send, self.recv = send, recv
        y, x, z, c = me.y, me.x, me.z, me.c
        cols = pl.ds(*cols)
        o = out.at
        tail = (ALL, c, ALL, cols)
        mine = o[y, x, z, c, :, cols]
        self.shard = shard.at[:, cols]
        self.own = pltpu.make_async_copy(self.shard, mine, local)
        if x_first:
            links, near, rest = (me.to_x, me.to_y), (y, 1 - x), (1 - y, ALL)
        else:
            links, near, rest = (me.to_y, me.to_x), (1 - y, x), (ALL, 1 - x)
        came = [o[y, x, zz, c, :, cols] for zz in me.zs]
        self.plan = [(me.to_z[k], mine) for k in range(3)] + [(links[0], mine), (links[1], mine)]
        self.plan += [(links[0], r) for r in came] + [(links[1], r) for r in came]
        self.plan += [(links[1], o[near + tail]), (me.to_core, o[(y, x) + tail]),
                      (me.to_core, o[near + tail]), (me.to_core, o[rest + tail])]

    def copy(self, k):
        peer, ref = self.plan[k]
        return pltpu.make_async_remote_copy(
            src_ref=self.shard if k < 5 else ref, dst_ref=ref, send_sem=self.send.at[k],
            recv_sem=self.recv.at[k], device_id=peer, device_id_type=MESH)

    def run(self, step):
        if step == 0:
            self.own.start()
        for k in self.WAITS[step]:
            self.copy(k).wait_recv()
        if step == 1:
            self.own.wait()
        for k in self.STARTS[step]:
            self.copy(k).start()
        if step == 4:
            for k in range(self.COPIES):
                self.copy(k).wait_send()


class Scatter:
    COPIES = 7
    STEPS = 5
    LINKS = (
        (("core", 16, True),),
        (("first", 8, True), ("first", 8, False)),
        (("second", 8, True),),
        (("z", 8, True),),
    )

    def __init__(self, me, term, out, scratch, cols, x_first, send, recv, local):
        self.me, self.out = me, out
        self.own, self.r = scratch[0], scratch[1:]
        self.send, self.recv = send, recv
        self.cols, self.x_first = pl.ds(*cols), x_first
        own, (r0, r1, r2, r3) = self.own, self.r
        y, x, z, c = me.y, me.x, me.z, me.c
        self.mine = pltpu.make_async_copy(term.at[ALL, ALL, ALL, c, :, self.cols], own, local)
        if x_first:
            first, second, near, across = me.to_x, me.to_y, own.at[y, 1 - x], own.at[1 - y, x]
        else:
            first, second, near, across = me.to_y, me.to_x, own.at[1 - y, x], own.at[y, 1 - x]
        self.plan = [
            (term.at[ALL, ALL, ALL, 1 - c, :, self.cols], me.to_core, r0),
            (own.at[1 - y, 1 - x], first, r1.at[0]), (near, first, r1.at[1]), (across, second, r2)] + [
            (own.at[y, x, me.zs[k]], me.to_z[k], r3.at[k]) for k in range(3)]

    def copy(self, k):
        src, peer, dst = self.plan[k]
        return pltpu.make_async_remote_copy(
            src_ref=src, dst_ref=dst, send_sem=self.send.at[k], recv_sem=self.recv.at[k],
            device_id=peer, device_id_type=MESH)

    def run(self, step):
        y, x, z = self.me.y, self.me.x, self.me.z
        own, (r0, r1, r2, r3) = self.own, self.r
        if step == 0:
            self.mine.start()
            self.copy(0).start()
        elif step == 1:
            self.mine.wait()
            self.copy(0).wait_recv()

            @pl.loop(0, 4)
            def _(k):
                for a in range(2):
                    for b in range(2):
                        own[a, b, k] = own[a, b, k] + r0[a, b, k]

            self.copy(1).start()
            self.copy(2).start()
        elif step == 2:
            self.copy(1).wait_recv()
            ay, ax = (1 - y, x) if self.x_first else (y, 1 - x)

            @pl.loop(0, 4)
            def _(k):
                own[ay, ax, k] = own[ay, ax, k] + r1[0, k]

            self.copy(3).start()
        elif step == 3:
            self.copy(2).wait_recv()
            self.copy(3).wait_recv()

            @pl.loop(0, 4)
            def _(k):
                total = own[y, x, k].astype(F32) + r1[1, k].astype(F32) + r2[k].astype(F32)
                own[y, x, k] = total.astype(own.dtype)

            for k in (4, 5, 6):
                self.copy(k).start()
        else:
            total = own[y, x, z].astype(F32)
            for k in (4, 5, 6):
                self.copy(k).wait_recv()
                total = total + r3[k - 4].astype(F32)
            self.out[:, self.cols] = total
            for k in range(self.COPIES):
                self.copy(k).wait_send()


RATES = {"c": 500e3, "z": 78e3, "x": 83e3}
DELAY = 2.0
ENTRY = 0.0
COST = {Gather: 0.1, Scatter: 0.2}


def cut_jobs(arrays, kind, pieces):
    jobs = []
    for i, a in enumerate(arrays):
        units = a.shape[-1] // 128
        n = min(pieces, units)
        start = 0
        for k in range(n):
            width = 128 * (units // n + (1 if k < units % n else 0))
            jobs.append((i, (start, width), len(jobs) % 2 == 0))
            start += width
    return jobs


def plan_jobs(kind, jobs, rows, slots, window):
    free = dict.fromkeys("xyzc", 0.0)
    ready = {}

    def start(i, step, now):
        array, (unused, width), x_first = jobs[i]
        done = now
        names = {"z": "z", "core": "c", "first": "x" if x_first else "y", "second": "y" if x_first else "x"}
        if step < len(kind.LINKS):
            for link, blocks, counts in kind.LINKS[step]:
                name = names[link]
                rate = RATES.get(name, RATES["x"])
                free[name] = max(free[name], now) + blocks * rows[array] * width * 2 / rate
                if counts:
                    done = max(done, free[name])
        if step < kind.STEPS - 1:
            ready[i, step + 1] = done + DELAY
        if step == 1 and i + window < len(jobs):
            ready[i + window, 0] = now

    for i in range(min(window, len(jobs))):
        ready[i, 0] = 0.0
    now, plan = ENTRY, []
    cost = COST[kind]
    for length in slots:
        todo = []
        while True:
            can = sorted((e for e in ready if ready[e] <= now and e[1] < kind.STEPS - 1), key=lambda e: (-e[1], e[0]))
            if not can:
                break
            ready.pop(can[0])
            now += cost
            start(*can[0], now)
            todo.append(can[0])
        plan.append(todo)
        now += length
    todo = []
    while ready:
        e = min(ready, key=lambda e: (max(ready[e], now), -e[1], e[0]))
        now = max(ready.pop(e), now) + cost
        start(*e, now)
        todo.append(e)
    return plan + [todo]


class Host:
    def __init__(self, kind=None, arrays=(), ident=None, slots=(), per=1, axis=1, pieces=None, window=None):
        self.kind, self.ident, self.per, self.axis = kind, ident, per, axis
        self.used = bool(arrays) and block_mesh()
        self.source = list(arrays)
        self.arrays, self.ins, self.outs, self.shapes, self.scratch = [], [], [], [], []
        if self.used:
            self.build(arrays, slots, pieces, window)
        self.count = len(self.arrays)

    def build(self, arrays, slots, pieces, window):
        kind = self.kind
        if kind is Scatter:
            arrays = [a.reshape(2, 2, 4, 2, -1, a.shape[-1]) for a in arrays]
        self.arrays = arrays = list(arrays)
        n = len(arrays)
        pieces = pieces or (2 if kind is Gather else 4)
        self.jobs = jobs = cut_jobs(arrays, kind, pieces)
        rows = [a.shape[-2] * a.dtype.itemsize // 2 for a in arrays]
        self.plan = plan_jobs(kind, jobs, rows, slots, window or (8 if kind is Gather else 4))
        m = len(jobs)
        any_space, vmem = pl.BlockSpec(memory_space=pl.ANY), pl.BlockSpec(memory_space=pltpu.VMEM)
        if kind is Gather:
            self.ins, self.outs = [vmem] * n, [any_space] * n
            self.shapes = [jax.ShapeDtypeStruct((2, 2, 4, 2) + a.shape, a.dtype) for a in arrays]
        else:
            self.ins, self.outs = [any_space] * n, [vmem] * n
            self.shapes = [jax.ShapeDtypeStruct(a.shape[4:], F32) for a in arrays]
            for i, (unused, width), unused in jobs:
                for lead in ((2, 2, 4), (2, 2, 4), (2, 4), (4,), (3,)):
                    self.scratch.append(pltpu.VMEM(lead + (arrays[i].shape[-2], width), arrays[i].dtype))
        self.scratch = self.scratch + [
            pltpu.SemaphoreType.DMA((m, kind.COPIES)), pltpu.SemaphoreType.DMA((m, kind.COPIES)),
            pltpu.SemaphoreType.DMA((m,))]

    def params(self):
        if not self.used:
            return pltpu.CompilerParams(vmem_limit_bytes=48 << 20)
        return pltpu.CompilerParams(
            collective_id=self.ident, has_side_effects=True, vmem_limit_bytes=56 << 20)

    def enter(self, ins, outs, scratch):
        if not self.used:
            return None
        me = Place()
        send, recv, local = scratch[-3:]
        work = []
        for k, (i, cols, x_first) in enumerate(self.jobs):
            own = scratch[5 * k : 5 * k + 5] if self.kind is Scatter else ()
            work.append(self.kind(me, ins[i], outs[i], own, cols, x_first, send.at[k], recv.at[k], local.at[k]))
        self.now = pl.program_id(self.axis)

        @pl.when(self.now == 0)
        def _():
            me.greet()

        return work

    def tick(self, work, at):
        if not self.used:
            return
        for g in range((len(self.plan) - 1) // self.per):
            todo = self.plan[g * self.per + at]
            if todo:
                @pl.when(self.now == g)
                def _():
                    for i, t in todo:
                        work[i].run(t)

    def leave(self, work):
        if not self.used:
            return

        @pl.when(self.now == (len(self.plan) - 1) // self.per - 1)
        def _():
            for i, t in self.plan[-1]:
                work[i].run(t)

    def results(self, values):
        if self.used and self.kind is Gather:
            return [w.reshape(-1, w.shape[-1]) for w in values]
        if self.used:
            return list(values)
        return plain(self.kind, self.source) if self.source else []


def plain(kind, arrays):
    if kind is Gather:
        return [lax.all_gather(a, AX, axis=0, tiled=True) for a in arrays]
    return [lax.psum_scatter(t.astype(F32), AX, scatter_dimension=0, tiled=True) for t in arrays]


def alone_kernel(*refs, host):
    n = host.count
    jobs = host.enter(refs[:n], refs[n : 2 * n], refs[2 * n :])
    host.tick(jobs, 0)
    host.leave(jobs)


def exchange(kind, arrays, ident, name, pieces):
    host = Host(kind, arrays, ident, [0.0], axis=0, pieces=pieces)
    if not host.used:
        return plain(kind, arrays)
    return host.results(pl.pallas_call(
        functools.partial(alone_kernel, host=host), grid=(1,),
        in_specs=host.ins, out_specs=host.outs, out_shape=host.shapes, scratch_shapes=host.scratch,
        compiler_params=host.params(), name=name)(*host.arrays))


def layer_norm(values, gain, shift):
    centre = values - jnp.mean(values, axis=-1, keepdims=True)
    spread = jnp.mean(centre * centre, axis=-1, keepdims=True)
    return centre * lax.rsqrt(spread + EPS) * gain + shift


def inner_rows(left, right):
    return lax.dot_general(left, right, (((0,), (0,)), ((), ())), preferred_element_type=F32)


def times_transposed(left, right):
    return lax.dot_general(left, right, (((1,), (1,)), ((), ())), preferred_element_type=F32)


def column_sums(values):
    return jnp.sum(values.astype(F32), axis=0)


def gelu_pair(z):
    c = 0.7978845608028654
    t = jnp.tanh(c * (z + 0.044715 * z * z * z))
    value = 0.5 * z * (1.0 + t)
    slope = 0.5 * (1.0 + t) + 0.5 * z * (1.0 - t * t) * c * (1.0 + 3 * 0.044715 * z * z)
    return value.astype(BF), slope.astype(BF)


def pack_columns(vectors, wide, count):
    length = vectors[0].shape[0]
    ways = wide.shape[0] // length
    per = length // count
    spread = wide.reshape(count, ways, per).transpose(0, 2, 1).reshape(length, ways)
    block = jnp.concatenate([jnp.stack(vectors, axis=1), spread], axis=1)
    return jnp.pad(block, ((0, 0), (0, LANES - block.shape[1])))


def unpack_columns(block, vector_count, ways, count):
    length = block.shape[0]
    turned = block[:, : vector_count + ways].T
    wide = turned[vector_count:].reshape(ways, count, length // count).transpose(1, 0, 2).reshape(-1)
    return [turned[i] for i in range(vector_count)], wide


def pick_kernel(tie_ref, *refs):
    n = 5 * LAYERS
    for i in range(LAYERS):
        heads, small, mix, expand, shrink = refs[5 * i : 5 * i + 5]
        outs = refs[n + 4 * i : n + 4 * i + 4]
        width = heads.shape[-1]
        outs[0][:, :width] = heads[0]
        outs[0][:, width:] = small[0]
        for out, ref in zip(outs[1:], (mix, expand, shrink)):
            out[...] = ref[0]


def pick_shards(tie_map, stacks):
    (ga, sa, hw, qb, vb, mw, mb, gf, sf, ew, eb, sw, sb) = stacks
    per = ga.shape[1]
    small = jnp.stack([ga, sa, qb, vb, mb, gf, sf, sb], axis=1)
    small = jnp.concatenate([small, eb.reshape(UNIQUE, -1, per)], axis=1).transpose(0, 2, 1)
    small = jnp.pad(small, ((0, 0), (0, 0), (0, LANES - small.shape[2])))
    arrays = [hw, small, mw, ew, sw]
    shapes = [(per, hw.shape[2] + LANES), mw.shape[1:], ew.shape[1:], sw.shape[1:]] * LAYERS
    specs = [pl.BlockSpec((1,) + a.shape[1:], lambda g, tie, use=i: (tie[use], 0, 0))
             for i in range(LAYERS) for a in arrays]
    outs = pl.pallas_call(
        pick_kernel,
        grid_spec=pltpu.PrefetchScalarGridSpec(
            num_scalar_prefetch=1, grid=(1,), in_specs=specs,
            out_specs=[pl.BlockSpec(shape, lambda g, tie: (0, 0)) for shape in shapes]),
        out_shape=[jax.ShapeDtypeStruct(shape, BF) for shape in shapes],
        name="pick")(tie_map, *(arrays * LAYERS))
    return [outs[4 * i : 4 * i + 4] for i in range(LAYERS)]


def use_heads(heads, width, ways):
    count = lax.axis_size(AX)
    turned = heads[:, 3 * width : 3 * width + 8 + ways].T.astype(F32)
    wide = turned[8:].reshape(ways, count, width // count).transpose(1, 0, 2).reshape(1, -1)
    vecs = turned[:8]
    return dict(vecs=vecs, ga=vecs[0], sa=vecs[1], mb=vecs[4], gf=vecs[5], sf=vecs[6], eb=wide, heads=heads)


def forward_use(hidden, w, first_len, host, spare_host):
    q, k, v, normed, attended, lse, *more = attend_fwd(hidden, w, first_len, host)
    more = host.results(more)
    w.update(expand=more[0], shrink=more[1], mix=more[-1])
    hidden = hidden.astype(F32)
    middle = hidden + jnp.dot(attended, w["mix"], preferred_element_type=F32) + w["mb"]
    normed_two = layer_norm(middle, w["gf"], w["sf"]).astype(BF)
    result, activated, slope, *spare = feed_fwd(normed_two, w, middle, spare_host)
    kept = (hidden, normed, (q, k, v), attended, lse, middle, normed_two, activated, slope)
    return result, kept, spare_host.results(spare)


def backward_use(grad_out, kept, w, first_len, carried, ident, spare_ident):
    hidden, normed, qkv, attended, lse, middle, normed_two, activated, slope = kept
    count = lax.axis_size(AX)
    grad_low = grad_out.astype(BF)
    sb = column_sums(grad_low)
    spare = Host(Scatter, carried, spare_ident, FEED_BACKWARD_SLOTS, per=4, axis=0, pieces=2, window=2)
    dc, expand_term, shrink_term, eb, *carried = feed_bwd(grad_low, activated, slope, normed_two, w, spare)
    carried = spare.results(carried)
    eb = eb[0]
    unused, norm_back = jax.vjp(layer_norm, middle, w["gf"], w["sf"])
    middle_norm, gf, sf = norm_back(dc)
    dm = grad_out + middle_norm
    dmb = dm.astype(BF)
    mix_term = inner_rows(attended, dmb).astype(BF)
    mb = column_sums(dmb)
    host = Host(Scatter, [shrink_term, mix_term, expand_term], ident, BACKWARD_SLOTS, per=4,
                pieces=8, window=3)
    heads_terms, da, qb, vb, more = attend_bwd(*qkv, dmb, lse, normed, w, first_len, host)
    more = host.results(more)
    unused, first_back = jax.vjp(layer_norm, hidden, w["ga"], w["sa"])
    hidden_norm, ga, sa = first_back(da)
    small = pack_columns([ga, sa, qb, vb, mb, gf, sf, sb], eb, count)
    return dm + hidden_norm, more, heads_terms, small, carried


def as_shares(shrink, mix, expand, heads, small):
    heads = jnp.concatenate(heads, axis=1)
    vecs, wide = unpack_columns(small, 8, shrink.shape[0] // mix.shape[0], 1)
    ga, sa, qb, vb, mb, gf, sf, sb = vecs
    return ga, sa, heads, qb, vb, mix, mb, gf, sf, expand, wide, shrink, sb


FORWARD_SLOTS = [1.6, 0.86, 1.29, 1.72] * 6
BACKWARD_SLOTS = [1.8, 1.35, 0.9, 2.9] * 6
FEED_FORWARD_SLOTS = [0.95, 0.95, 0.95, 0.95] * 6
FEED_BACKWARD_SLOTS = [0.7, 0.7, 0.7, 2.3] * 6


def place_terms(sources, shares):
    ids = lax.iota(jnp.int32, UNIQUE)
    out = []
    for items in zip(*shares):
        total = 0.0
        for source, item in zip(sources, items):
            chosen = (ids == source).reshape((UNIQUE,) + (1,) * item.ndim)
            total = total + jnp.where(chosen, item[None], 0.0)
        out.append(total)
    return out


def body(tokens, cotangent, tie_map, first_length, *stacks):
    hidden = tokens
    width = hidden.shape[1]
    sources = [tie_map[i] for i in range(LAYERS)]
    shards = pick_shards(tie_map, stacks)
    ways = shards[0][3].shape[0] // shards[0][0].shape[0]
    (heads,) = exchange(Gather, shards[0][:1], 0, "gather", 4)
    kept, weights = [], []
    for i in range(LAYERS):
        weights.append(use_heads(heads, width, ways))
        host = Host(Gather, shards[i][2:] + shards[i][1:2], 1 + i, FORWARD_SLOTS, per=4, pieces=4, window=12)
        later = shards[i + 1][:1] if i + 1 < LAYERS else []
        spare_host = Host(Gather, later, 6, FEED_FORWARD_SLOTS, per=4, axis=0, pieces=5, window=4)
        hidden, saved, spare = forward_use(hidden, weights[i], first_length, host, spare_host)
        heads = spare[0] if spare else None
        kept.append(saved)
    grad = cotangent.astype(F32)
    grad, late, heads_late, small_late, unused = backward_use(
        grad, kept[1], weights[1], first_length, [], 3, None)
    grad, early, heads_early, small_early, heads_late = backward_use(
        grad, kept[0], weights[0], first_length, heads_late, 4, 7)
    *heads_early, small = exchange(
        Scatter, heads_early + [jnp.concatenate([small_early, small_late], axis=1)], 5, "scatter", 3)
    shares = [as_shares(*early, heads_early, small[:, :LANES]),
              as_shares(*late, heads_late, small[:, LANES:])]
    return (hidden.astype(BF), grad.astype(BF), *place_terms(sources, shares))


def solution(mesh):
    rows = P(AX, None)
    flat = P(None, AX)
    deep = P(None, AX, None)
    weights = (flat, flat, deep, flat, flat, deep, flat, flat, flat, deep, flat, deep, flat)
    return jax.shard_map(
        body,
        mesh=mesh,
        in_specs=(rows, rows, P(), P(AX)) + weights,
        out_specs=(rows, rows) + weights,
        check_vma=False,
    )
```

```python
import functools

import jax
import jax.numpy as jnp
from jax import lax
from jax.experimental import pallas as pl
from jax.experimental.pallas import tpu as pltpu
from jax.sharding import PartitionSpec as P

LAYERS = 2
UNIQUE = 4
F32 = jnp.float32
BF = jnp.bfloat16
AX = ("dp", "fsdp")
LANES = 128
EPS = 1e-05

NEG=-1e9
def nt(a,b): return lax.dot_general(a,b,(((1,),(1,)),((),())),preferred_element_type=F32)
def nn(a,b): return lax.dot_general(a,b,(((1,),(0,)),((),())),preferred_element_type=F32)
def halves(x):
    lane=lax.broadcasted_iota(jnp.int32,x.shape,1)
    z=jnp.zeros_like(x)
    return jnp.where(lane<64,x,z), jnp.where(lane<64,z,x)

def fwd_kernel(fl_ref,hid_ref,vec_ref,wq_ref,wk_ref,wv_ref,part_ref,*rest,bq,host):
    n=host.count
    q_ref,k_ref,v_ref,normed_ref,o_ref,lse_ref=rest[n:n+6]
    jobs=host.enter(rest[:n],rest[n+6:2*n+6],rest[2*n+6:])
    L=q_ref.shape[0]; half=L//2
    @pl.when(pl.program_id(1)==0)
    def _():
        for lo in range(0,L,bq):
            normed_ref[lo:lo+bq,:]=layer_norm(hid_ref[lo:lo+bq,:].astype(F32),vec_ref[0:1,:],vec_ref[1:2,:]).astype(BF)
    w=jnp.concatenate([wq_ref[...],wk_ref[...],wv_ref[...]],axis=1)
    qkv=nn(normed_ref[...],w)
    q_ref[...]=(qkv[:,:128]+part_ref[2:3,:]).astype(BF)
    k_ref[...]=qkv[:,128:256].astype(BF)
    v_ref[...]=(qkv[:,256:]+part_ref[3:4,:]).astype(BF)
    second=fl_ref[pl.program_id(0)]<L
    shut=jnp.where(second,F32(1e9),F32(0.))
    q=q_ref[...]*BF(0.125); k=k_ref[...]; vT=v_ref[...].T
    sub=lax.broadcasted_iota(jnp.int32,vT.shape,0)
    zero=jnp.zeros_like(vT)
    vTs=(jnp.where(sub<64,vT,zero),jnp.where(sub<64,zero,vT))
    qs=halves(q)
    tri=lax.broadcasted_iota(jnp.int32,(bq,bq),0)<=lax.broadcasted_iota(jnp.int32,(bq,bq),1)
    for j in range(L//bq):
        host.tick(jobs,j)
        lo=j*bq; hi=lo+bq
        acc=jnp.zeros((128,bq),F32)
        for h in range(2):
            qh=qs[h][lo:hi]
            s=nt(k[:hi],qh)
            parts=[]
            if lo>0 : parts.append((0,min(lo,half),s[:min(lo,half)]))
            if lo>half: parts.append((half,lo,s[half:lo]))
            diag=jnp.where(tri,s[lo:],NEG)
            m=jnp.max(diag,axis=0,keepdims=True)
            for a,b,t in parts:
                mt=jnp.max(t,axis=0,keepdims=True)
                if lo>=half and a==0: mt=mt-shut
                m=jnp.maximum(m,mt)
            ps=[]; l=0.
            for a,b,t in parts+[(lo,hi,diag)]:
                mm=m+shut if (lo>=half and a==0) else m
                p=jnp.exp(t-mm)
                l=l+jnp.sum(p,axis=0,keepdims=True)
                ps.append(p.astype(BF))
            p=jnp.concatenate(ps,axis=0) if len(ps)>1 else ps[0]
            oh=nn(vTs[h][:,:hi],p)
            acc=acc+oh*(1.0/l)
            lse_ref[0,h:h+1,lo:hi]=m+jnp.log(l)
        o_ref[lo:hi,:]=acc.T.astype(BF)
    host.leave(jobs)

def attend_fwd(hidden,w,fl,host,bq=256):
    N,D=hidden.shape; R=fl.shape[0]; L=N//R; G=D//128
    col=lambda off: pl.BlockSpec((D,128),lambda r,g,fl:(0,off*G+g))
    blk=pl.BlockSpec((L,128),lambda r,g,fl:(r,g))
    row=pl.BlockSpec((L,D),lambda r,g,fl:(r,0))
    vec=pl.BlockSpec((8,D),lambda r,g,fl:(0,0)); part=pl.BlockSpec((8,128),lambda r,g,fl:(0,g))
    narrow=jax.ShapeDtypeStruct((N,D),BF)
    return pl.pallas_call(functools.partial(fwd_kernel,bq=bq,host=host),
        grid_spec=pltpu.PrefetchScalarGridSpec(num_scalar_prefetch=1,grid=(R,G),
          in_specs=[row,vec,col(0),col(1),col(2),part]+host.ins,
          out_specs=[blk,blk,blk,row,blk,pl.BlockSpec((1,2,L),lambda r,g,fl:(r*G+g,0,0))]+host.outs,
          scratch_shapes=host.scratch),
        out_shape=[narrow]*5+[jax.ShapeDtypeStruct((R*G,2,L),F32)]+host.shapes,
        compiler_params=host.params(),
        cost_estimate=pl.CostEstimate(flops=2*2*R*L*L*D*2+6*N*D*D,bytes_accessed=N*D*14,transcendentals=R*L*L*12//2),
        name="attend_fwd")(fl,hidden,w["vecs"],w["heads"],w["heads"],w["heads"],w["vecs"],*host.arrays)

def bwd_kernel(fl_ref,q_ref,k_ref,v_ref,do_ref,lse_ref,normed_ref,wq_ref,wk_ref,wv_ref,*rest,bq,host):
    n=host.count
    gq_ref,gk_ref,gv_ref,da_ref,qb_ref,vb_ref=rest[n:n+6]
    dk_acc,dv_acc,dqkv=rest[2*n+6:2*n+9]
    jobs=host.enter(rest[:n],rest[n+6:2*n+6],rest[2*n+9:])
    L=q_ref.shape[0]; half=L//2
    second=fl_ref[pl.program_id(0)]<L
    shut=jnp.where(second,F32(1e9),F32(0.))
    q=q_ref[...]*BF(0.125); k=k_ref[...]; v=v_ref[...]; do=do_ref[...]
    kT=k.T
    sub=lax.broadcasted_iota(jnp.int32,kT.shape,0); zero=jnp.zeros_like(kT)
    kTs=(jnp.where(sub<64,kT,zero),jnp.where(sub<64,zero,kT))
    qs=halves(q); dos=halves(do)
    tri=lax.broadcasted_iota(jnp.int32,(bq,bq),0)<=lax.broadcasted_iota(jnp.int32,(bq,bq),1)
    nb=L//bq
    for j in reversed(range(nb)):
        host.tick(jobs,nb-1-j)
        lo=j*bq; hi=lo+bq
        dqT=jnp.zeros((128,bq),F32)
        dkp=None; dvp=None
        for h in range(2):
            qh=qs[h][lo:hi]; doh=dos[h][lo:hi]
            lse=lse_ref[0,h:h+1,lo:hi]
            s=nt(k[:hi],qh)
            dp=nt(v[:hi],doh)
            ps=[];
            cuts=[]
            if lo>0: cuts.append((0,min(lo,half)))
            if lo>half: cuts.append((half,lo))
            cuts.append((lo,hi))
            for a,b in cuts:
                ll=lse+shut if (lo>=half and b<=half) else lse
                t=s[a:b]-ll
                if a==lo: t=jnp.where(tri,t,NEG)
                ps.append(jnp.exp(t))
            p=jnp.concatenate(ps,axis=0) if len(ps)>1 else ps[0]
            delta=jnp.sum(p*dp,axis=0,keepdims=True)
            ds=(p*(dp-delta)).astype(BF)
            pb=p.astype(BF)
            dv_=nn(pb,doh); dk_=nn(ds,qh)
            dvp=dv_ if dvp is None else dvp+dv_
            dkp=dk_ if dkp is None else dkp+dk_
            dqT=dqT+nn(kTs[h][:,:hi],ds)
        if j==nb-1:
            dk_acc[...]=dkp; dv_acc[...]=dvp
        else:
            dk_acc[:hi]+=dkp; dv_acc[:hi]+=dvp
        dqkv[lo:hi,:128]=(dqT.T*0.125).astype(BF)
    dqkv[:,128:256]=dk_acc[...].astype(BF); dqkv[:,256:]=dv_acc[...].astype(BF)
    d=dqkv[...]
    qb_ref[0]=jnp.sum(d[:,:128].astype(F32),axis=0,keepdims=True)
    vb_ref[0]=jnp.sum(d[:,256:].astype(F32),axis=0,keepdims=True)
    terms=tn(normed_ref[...],d).astype(BF)
    gq_ref[0]=terms[:,:128]; gk_ref[0]=terms[:,128:256]; gv_ref[0]=terms[:,256:]
    da=nt(d,jnp.concatenate([wq_ref[...],wk_ref[...],wv_ref[...]],axis=1))
    @pl.when(pl.program_id(1)==0)
    def _(): da_ref[...]=da
    @pl.when(pl.program_id(1)>0)
    def _(): da_ref[...]+=da
    host.leave(jobs)

def attend_bwd(q,k,v,do,lse,normed,w,fl,host,bq=256):
    N,D=q.shape; R=fl.shape[0]; L=N//R; G=D//128
    blk=pl.BlockSpec((L,128),lambda r,g,fl:(r,g))
    row=pl.BlockSpec((L,D),lambda r,g,fl:(r,0))
    col=lambda off: pl.BlockSpec((D,128),lambda r,g,fl:(0,off*G+g))
    term=pl.BlockSpec((1,D,128),lambda r,g,fl:(r,0,g)); part=pl.BlockSpec((1,1,128),lambda r,g,fl:(r,0,g))
    gq,gk,gv,da,qb,vb,*more=pl.pallas_call(functools.partial(bwd_kernel,bq=bq,host=host),
        grid_spec=pltpu.PrefetchScalarGridSpec(num_scalar_prefetch=1,grid=(R,G),
          in_specs=[blk]*4+[pl.BlockSpec((1,2,L),lambda r,g,fl:(r*G+g,0,0)),row,col(0),col(1),col(2)]+host.ins,
          out_specs=[term]*3+[row,part,part]+host.outs,
          scratch_shapes=[pltpu.VMEM((L,128),F32),pltpu.VMEM((L,128),F32),pltpu.VMEM((L,384),BF)]+host.scratch),
        out_shape=[jax.ShapeDtypeStruct((R,D,D),BF)]*3+[jax.ShapeDtypeStruct((N,D),F32)]
          +[jax.ShapeDtypeStruct((R,1,D),F32)]*2+host.shapes,
        compiler_params=host.params(),
        cost_estimate=pl.CostEstimate(flops=5*2*R*L*L*D*2+12*N*D*D,bytes_accessed=N*D*16,transcendentals=R*L*L*12//2),
        name="attend_bwd")(fl,q,k,v,do,lse,normed,w["heads"],w["heads"],w["heads"],*host.arrays)
    gq,gk,gv=[t[0] if R==1 else jnp.sum(t.astype(F32),axis=0).astype(BF) for t in (gq,gk,gv)]
    return [gq,gk,gv],da,jnp.sum(qb,axis=(0,1)),jnp.sum(vb,axis=(0,1)),more


def tn(a,b): return lax.dot_general(a,b,(((0,),(0,)),((),())),preferred_element_type=F32)

def feed_fwd_kernel(c_ref,e_ref,eb_ref,s_ref,m_ref,sb_ref,*rest,rows,host):
    n=host.count
    h_ref,u_ref,slope_ref=rest[n:n+3]
    jobs=host.enter(rest[:n],rest[n+3:2*n+3],rest[2*n+3:])
    N=c_ref.shape[0]
    e=e_ref[...]; s=s_ref[...]; eb=eb_ref[...]
    @pl.when(pl.program_id(0)==0)
    def _(): h_ref[...]=m_ref[...]+sb_ref[7:8,:]
    for j in range(N//rows):
        host.tick(jobs,j)
        at=slice(j*rows,(j+1)*rows)
        u,slope=gelu_pair(nn(c_ref[at,:],e)+eb)
        u_ref[at,:]=u; slope_ref[at,:]=slope
        h_ref[at,:]+=nn(u,s)
    host.leave(jobs)

def feed_fwd(c,w,middle,host,tile=512,rows=256):
    N,D=c.shape; F=w["expand"].shape[1]
    fixed=lambda r: pl.BlockSpec((r,D),lambda t: (0,0))
    return pl.pallas_call(functools.partial(feed_fwd_kernel,rows=rows,host=host),grid=(F//tile,),
        in_specs=[fixed(N),pl.BlockSpec((D,tile),lambda t:(0,t)),pl.BlockSpec((1,tile),lambda t:(0,t)),
                  pl.BlockSpec((tile,D),lambda t:(t,0)),fixed(N),fixed(8)]+host.ins,
        out_specs=[fixed(N)]+[pl.BlockSpec((N,tile),lambda t:(0,t))]*2+host.outs,
        out_shape=[jax.ShapeDtypeStruct((N,D),F32)]+[jax.ShapeDtypeStruct((N,F),BF)]*2+host.shapes,
        scratch_shapes=host.scratch,compiler_params=host.params(),
        cost_estimate=pl.CostEstimate(flops=4*N*D*F,bytes_accessed=4*N*F+4*D*F,transcendentals=N*F),
        name="feed_fwd")(c,w["expand"],w["eb"],w["shrink"],middle,w["vecs"],*host.arrays)

def feed_bwd_kernel(g_ref,u_ref,slope_ref,c_ref,e_ref,s_ref,*rest,rows,host):
    n=host.count
    dc_ref,de_ref,ds_ref,eb_ref=rest[n:n+4]
    dz_ref=rest[2*n+4]
    jobs=host.enter(rest[:n],rest[n+4:2*n+4],rest[2*n+5:])
    N=c_ref.shape[0]
    e=e_ref[...]; s=s_ref[...]
    @pl.when(pl.program_id(0)==0)
    def _(): dc_ref[...]=jnp.zeros_like(dc_ref)
    total=0.
    for j in range(N//rows):
        host.tick(jobs,j)
        at=slice(j*rows,(j+1)*rows)
        dz=(nt(g_ref[at,:],s)*slope_ref[at,:].astype(F32)).astype(BF)
        dz_ref[at,:]=dz
        total=total+jnp.sum(dz.astype(F32),axis=0,keepdims=True)
        dc_ref[at,:]+=nt(dz,e)
    eb_ref[...]=total
    de_ref[...]=tn(c_ref[...],dz_ref[...]).astype(BF)
    ds_ref[...]=tn(u_ref[...],g_ref[...]).astype(BF)
    host.leave(jobs)

def feed_bwd(g,u,slope,c,w,host,tile=512,rows=256):
    N,D=c.shape; F=u.shape[1]
    fixed=pl.BlockSpec((N,D),lambda t:(0,0))
    wide=lambda r: pl.BlockSpec((r,tile),lambda t:(0,t))
    tall=pl.BlockSpec((tile,D),lambda t:(t,0))
    return pl.pallas_call(functools.partial(feed_bwd_kernel,rows=rows,host=host),grid=(F//tile,),
        in_specs=[fixed,wide(N),wide(N),fixed,wide(D),tall]+host.ins,
        out_specs=[fixed,wide(D),tall,wide(1)]+host.outs,
        out_shape=[jax.ShapeDtypeStruct((N,D),F32),jax.ShapeDtypeStruct((D,F),BF),
                   jax.ShapeDtypeStruct((F,D),BF),jax.ShapeDtypeStruct((1,F),F32)]+host.shapes,
        scratch_shapes=[pltpu.VMEM((N,tile),BF)]+host.scratch,compiler_params=host.params(),
        cost_estimate=pl.CostEstimate(flops=8*N*D*F,bytes_accessed=4*N*F+8*D*F,transcendentals=0),
        name="feed_bwd")(g,u,slope,c,w["expand"],w["shrink"],*host.arrays)


MESH = pl.DeviceIdType.MESH


def block_mesh():
    return lax.axis_size("dp") == 4 and lax.axis_size("fsdp") == 8


class Place:
    def __init__(self):
        d = lax.axis_index("dp")
        f = lax.axis_index("fsdp")
        self.y, self.x = lax.div(d, 2), lax.rem(d, 2)
        self.z, self.c = lax.div(f, 2), lax.rem(f, 2)
        self.zs = [self.z + 1 - 2 * lax.rem(self.z, 2), lax.rem(self.z + 2, 4), 3 - self.z]
        self.to_core = (d, 2 * self.z + 1 - self.c)
        self.to_x = (2 * self.y + 1 - self.x, f)
        self.to_y = (2 * (1 - self.y) + self.x, f)
        self.to_z = [(d, 2 * zz + self.c) for zz in self.zs]

    def greet(self):
        barrier = pltpu.get_barrier_semaphore()
        peers = [self.to_core, self.to_x, self.to_y] + self.to_z
        for peer in peers:
            pl.semaphore_signal(barrier, inc=1, device_id=peer, device_id_type=MESH)
        pl.semaphore_wait(barrier, len(peers))


ALL = slice(None)


class Gather:
    COPIES = 15
    STEPS = 5
    LINKS = (
        (("z", 8, True), ("first", 2, False), ("second", 2, False)),
        (("first", 6, True), ("second", 6, False), ("core", 4, False)),
        (("second", 8, True), ("core", 4, False)),
        (("core", 8, True),),
    )
    STARTS = ((0, 1, 2, 3, 4), (5, 6, 7, 8, 9, 10, 12), (11, 13), (14,), ())
    WAITS = ((), (0, 1, 2), (3, 5, 6, 7), (4, 8, 9, 10, 11), (12, 13, 14))

    def __init__(self, me, shard, out, scratch, cols, x_first, send, recv, local):
        self.send, self.recv = send, recv
        y, x, z, c = me.y, me.x, me.z, me.c
        cols = pl.ds(*cols)
        o = out.at
        tail = (ALL, c, ALL, cols)
        mine = o[y, x, z, c, :, cols]
        self.shard = shard.at[:, cols]
        self.own = pltpu.make_async_copy(self.shard, mine, local)
        if x_first:
            links, near, rest = (me.to_x, me.to_y), (y, 1 - x), (1 - y, ALL)
        else:
            links, near, rest = (me.to_y, me.to_x), (1 - y, x), (ALL, 1 - x)
        came = [o[y, x, zz, c, :, cols] for zz in me.zs]
        self.plan = [(me.to_z[k], mine) for k in range(3)] + [(links[0], mine), (links[1], mine)]
        self.plan += [(links[0], r) for r in came] + [(links[1], r) for r in came]
        self.plan += [(links[1], o[near + tail]), (me.to_core, o[(y, x) + tail]),
                      (me.to_core, o[near + tail]), (me.to_core, o[rest + tail])]

    def copy(self, k):
        peer, ref = self.plan[k]
        return pltpu.make_async_remote_copy(
            src_ref=self.shard if k < 5 else ref, dst_ref=ref, send_sem=self.send.at[k],
            recv_sem=self.recv.at[k], device_id=peer, device_id_type=MESH)

    def run(self, step):
        if step == 0:
            self.own.start()
        for k in self.WAITS[step]:
            self.copy(k).wait_recv()
        if step == 1:
            self.own.wait()
        for k in self.STARTS[step]:
            self.copy(k).start()
        if step == 4:
            for k in range(self.COPIES):
                self.copy(k).wait_send()


class Scatter:
    COPIES = 7
    STEPS = 5
    LINKS = (
        (("core", 16, True),),
        (("first", 8, True), ("first", 8, False)),
        (("second", 8, True),),
        (("z", 8, True),),
    )

    def __init__(self, me, term, out, scratch, cols, x_first, send, recv, local):
        self.me, self.out = me, out
        self.own, self.r = scratch[0], scratch[1:]
        self.send, self.recv = send, recv
        self.cols, self.x_first = pl.ds(*cols), x_first
        own, (r0, r1, r2, r3) = self.own, self.r
        y, x, z, c = me.y, me.x, me.z, me.c
        self.mine = pltpu.make_async_copy(term.at[ALL, ALL, ALL, c, :, self.cols], own, local)
        if x_first:
            first, second, near, across = me.to_x, me.to_y, own.at[y, 1 - x], own.at[1 - y, x]
        else:
            first, second, near, across = me.to_y, me.to_x, own.at[1 - y, x], own.at[y, 1 - x]
        self.plan = [
            (term.at[ALL, ALL, ALL, 1 - c, :, self.cols], me.to_core, r0),
            (own.at[1 - y, 1 - x], first, r1.at[0]), (near, first, r1.at[1]), (across, second, r2)] + [
            (own.at[y, x, me.zs[k]], me.to_z[k], r3.at[k]) for k in range(3)]

    def copy(self, k):
        src, peer, dst = self.plan[k]
        return pltpu.make_async_remote_copy(
            src_ref=src, dst_ref=dst, send_sem=self.send.at[k], recv_sem=self.recv.at[k],
            device_id=peer, device_id_type=MESH)

    def run(self, step):
        y, x, z = self.me.y, self.me.x, self.me.z
        own, (r0, r1, r2, r3) = self.own, self.r
        if step == 0:
            self.mine.start()
            self.copy(0).start()
        elif step == 1:
            self.mine.wait()
            self.copy(0).wait_recv()

            @pl.loop(0, 4)
            def _(k):
                for a in range(2):
                    for b in range(2):
                        own[a, b, k] = own[a, b, k] + r0[a, b, k]

            self.copy(1).start()
            self.copy(2).start()
        elif step == 2:
            self.copy(1).wait_recv()
            ay, ax = (1 - y, x) if self.x_first else (y, 1 - x)

            @pl.loop(0, 4)
            def _(k):
                own[ay, ax, k] = own[ay, ax, k] + r1[0, k]

            self.copy(3).start()
        elif step == 3:
            self.copy(2).wait_recv()
            self.copy(3).wait_recv()

            @pl.loop(0, 4)
            def _(k):
                total = own[y, x, k].astype(F32) + r1[1, k].astype(F32) + r2[k].astype(F32)
                own[y, x, k] = total.astype(own.dtype)

            for k in (4, 5, 6):
                self.copy(k).start()
        else:
            total = own[y, x, z].astype(F32)
            for k in (4, 5, 6):
                self.copy(k).wait_recv()
                total = total + r3[k - 4].astype(F32)
            self.out[:, self.cols] = total
            for k in range(self.COPIES):
                self.copy(k).wait_send()


RATES = {"c": 500e3, "z": 78e3, "x": 83e3}
DELAY = 2.0
ENTRY = 0.0
COST = {Gather: 0.1, Scatter: 0.2}


def cut_jobs(arrays, kind, pieces):
    jobs = []
    for i, a in enumerate(arrays):
        units = a.shape[-1] // 128
        n = min(pieces, units)
        start = 0
        for k in range(n):
            width = 128 * (units // n + (1 if k < units % n else 0))
            jobs.append((i, (start, width), len(jobs) % 2 == 0))
            start += width
    return jobs


def plan_jobs(kind, jobs, rows, slots, window):
    free = dict.fromkeys("xyzc", 0.0)
    ready = {}

    def start(i, step, now):
        array, (unused, width), x_first = jobs[i]
        done = now
        names = {"z": "z", "core": "c", "first": "x" if x_first else "y", "second": "y" if x_first else "x"}
        if step < len(kind.LINKS):
            for link, blocks, counts in kind.LINKS[step]:
                name = names[link]
                rate = RATES.get(name, RATES["x"])
                free[name] = max(free[name], now) + blocks * rows[array] * width * 2 / rate
                if counts:
                    done = max(done, free[name])
        if step < kind.STEPS - 1:
            ready[i, step + 1] = done + DELAY
        if step == 1 and i + window < len(jobs):
            ready[i + window, 0] = now

    for i in range(min(window, len(jobs))):
        ready[i, 0] = 0.0
    now, plan = ENTRY, []
    cost = COST[kind]
    for length in slots:
        todo = []
        while True:
            can = sorted((e for e in ready if ready[e] <= now and e[1] < kind.STEPS - 1), key=lambda e: (-e[1], e[0]))
            if not can:
                break
            ready.pop(can[0])
            now += cost
            start(*can[0], now)
            todo.append(can[0])
        plan.append(todo)
        now += length
    todo = []
    while ready:
        e = min(ready, key=lambda e: (max(ready[e], now), -e[1], e[0]))
        now = max(ready.pop(e), now) + cost
        start(*e, now)
        todo.append(e)
    return plan + [todo]


class Host:
    def __init__(self, kind=None, arrays=(), ident=None, slots=(), per=1, axis=1, pieces=None, window=None):
        self.kind, self.ident, self.per, self.axis = kind, ident, per, axis
        self.used = bool(arrays) and block_mesh()
        self.source = list(arrays)
        self.arrays, self.ins, self.outs, self.shapes, self.scratch = [], [], [], [], []
        if self.used:
            self.build(arrays, slots, pieces, window)
        self.count = len(self.arrays)

    def build(self, arrays, slots, pieces, window):
        kind = self.kind
        if kind is Scatter:
            arrays = [a.reshape(2, 2, 4, 2, -1, a.shape[-1]) for a in arrays]
        self.arrays = arrays = list(arrays)
        n = len(arrays)
        pieces = pieces or (2 if kind is Gather else 4)
        self.jobs = jobs = cut_jobs(arrays, kind, pieces)
        rows = [a.shape[-2] * a.dtype.itemsize // 2 for a in arrays]
        self.plan = plan_jobs(kind, jobs, rows, slots, window or (8 if kind is Gather else 4))
        m = len(jobs)
        any_space, vmem = pl.BlockSpec(memory_space=pl.ANY), pl.BlockSpec(memory_space=pltpu.VMEM)
        if kind is Gather:
            self.ins, self.outs = [vmem] * n, [any_space] * n
            self.shapes = [jax.ShapeDtypeStruct((2, 2, 4, 2) + a.shape, a.dtype) for a in arrays]
        else:
            self.ins, self.outs = [any_space] * n, [vmem] * n
            self.shapes = [jax.ShapeDtypeStruct(a.shape[4:], F32) for a in arrays]
            for i, (unused, width), unused in jobs:
                for lead in ((2, 2, 4), (2, 2, 4), (2, 4), (4,), (3,)):
                    self.scratch.append(pltpu.VMEM(lead + (arrays[i].shape[-2], width), arrays[i].dtype))
        self.scratch = self.scratch + [
            pltpu.SemaphoreType.DMA((m, kind.COPIES)), pltpu.SemaphoreType.DMA((m, kind.COPIES)),
            pltpu.SemaphoreType.DMA((m,))]

    def params(self):
        if not self.used:
            return pltpu.CompilerParams(vmem_limit_bytes=48 << 20)
        return pltpu.CompilerParams(
            collective_id=self.ident, has_side_effects=True, vmem_limit_bytes=56 << 20)

    def enter(self, ins, outs, scratch):
        if not self.used:
            return None
        me = Place()
        send, recv, local = scratch[-3:]
        work = []
        for k, (i, cols, x_first) in enumerate(self.jobs):
            own = scratch[5 * k : 5 * k + 5] if self.kind is Scatter else ()
            work.append(self.kind(me, ins[i], outs[i], own, cols, x_first, send.at[k], recv.at[k], local.at[k]))
        self.now = pl.program_id(self.axis)

        @pl.when(self.now == 0)
        def _():
            me.greet()

        return work

    def tick(self, work, at):
        if not self.used:
            return
        for g in range((len(self.plan) - 1) // self.per):
            todo = self.plan[g * self.per + at]
            if todo:
                @pl.when(self.now == g)
                def _():
                    for i, t in todo:
                        work[i].run(t)

    def leave(self, work):
        if not self.used:
            return

        @pl.when(self.now == (len(self.plan) - 1) // self.per - 1)
        def _():
            for i, t in self.plan[-1]:
                work[i].run(t)

    def results(self, values):
        if self.used and self.kind is Gather:
            return [w.reshape(-1, w.shape[-1]) for w in values]
        if self.used:
            return list(values)
        return plain(self.kind, self.source) if self.source else []


def plain(kind, arrays):
    if kind is Gather:
        return [lax.all_gather(a, AX, axis=0, tiled=True) for a in arrays]
    return [lax.psum_scatter(t.astype(F32), AX, scatter_dimension=0, tiled=True) for t in arrays]


def alone_kernel(*refs, host):
    n = host.count
    jobs = host.enter(refs[:n], refs[n : 2 * n], refs[2 * n :])
    host.tick(jobs, 0)
    host.leave(jobs)


def exchange(kind, arrays, ident, name, pieces):
    host = Host(kind, arrays, ident, [0.0], axis=0, pieces=pieces)
    if not host.used:
        return plain(kind, arrays)
    return host.results(pl.pallas_call(
        functools.partial(alone_kernel, host=host), grid=(1,),
        in_specs=host.ins, out_specs=host.outs, out_shape=host.shapes, scratch_shapes=host.scratch,
        compiler_params=host.params(), name=name)(*host.arrays))


def layer_norm(values, gain, shift):
    centre = values - jnp.mean(values, axis=-1, keepdims=True)
    spread = jnp.mean(centre * centre, axis=-1, keepdims=True)
    return centre * lax.rsqrt(spread + EPS) * gain + shift


def inner_rows(left, right):
    return lax.dot_general(left, right, (((0,), (0,)), ((), ())), preferred_element_type=F32)


def times_transposed(left, right):
    return lax.dot_general(left, right, (((1,), (1,)), ((), ())), preferred_element_type=F32)


def column_sums(values):
    return jnp.sum(values.astype(F32), axis=0)


def gelu_pair(z):
    c = 0.7978845608028654
    t = jnp.tanh(c * (z + 0.044715 * z * z * z))
    value = 0.5 * z * (1.0 + t)
    slope = 0.5 * (1.0 + t) + 0.5 * z * (1.0 - t * t) * c * (1.0 + 3 * 0.044715 * z * z)
    return value.astype(BF), slope.astype(BF)


def pack_columns(vectors, wide, count):
    length = vectors[0].shape[0]
    ways = wide.shape[0] // length
    per = length // count
    spread = wide.reshape(count, ways, per).transpose(0, 2, 1).reshape(length, ways)
    block = jnp.concatenate([jnp.stack(vectors, axis=1), spread], axis=1)
    return jnp.pad(block, ((0, 0), (0, LANES - block.shape[1])))


def unpack_columns(block, vector_count, ways, count):
    length = block.shape[0]
    turned = block[:, : vector_count + ways].T
    wide = turned[vector_count:].reshape(ways, count, length // count).transpose(1, 0, 2).reshape(-1)
    return [turned[i] for i in range(vector_count)], wide


def pick_kernel(tie_ref, *refs):
    n = 5 * LAYERS
    vectors, outs = refs[n : n + 8], refs[n + 8 :]
    for i in range(LAYERS):
        heads, wide, mix, expand, shrink = refs[5 * i : 5 * i + 5]
        out = outs[4 * i]
        per, width = heads.shape[1:]
        chosen = lax.broadcasted_iota(jnp.int32, (UNIQUE, per), 0) == tie_ref[i]
        rows = [jnp.sum(jnp.where(chosen, v[...].astype(F32), 0.0), axis=0, keepdims=True) for v in vectors]
        rows.append(wide[0].astype(F32))
        rows.append(jnp.zeros((8 - wide.shape[1], per), F32))
        rows = jnp.concatenate([jnp.concatenate(rows, axis=0), jnp.zeros((16, LANES - per), F32)], axis=1)
        out[:, :width] = heads[0]
        out[:, width:] = jnp.concatenate([rows.T[:per], jnp.zeros((per, LANES - 16), F32)], axis=1).astype(BF)
        for out, ref in zip(outs[4 * i + 1 : 4 * i + 4], (mix, expand, shrink)):
            out[...] = ref[0]


def pick_shards(tie_map, stacks):
    (ga, sa, hw, qb, vb, mw, mb, gf, sf, ew, eb, sw, sb) = stacks
    per = ga.shape[1]
    arrays = [hw, eb.reshape(UNIQUE, -1, per), mw, ew, sw]
    shapes = [(per, hw.shape[2] + LANES), mw.shape[1:], ew.shape[1:], sw.shape[1:]] * LAYERS
    specs = [pl.BlockSpec((1,) + a.shape[1:], lambda g, tie, use=i: (tie[use], 0, 0))
             for i in range(LAYERS) for a in arrays]
    specs += [pl.BlockSpec(ga.shape, lambda g, tie: (0, 0))] * 8
    outs = pl.pallas_call(
        pick_kernel,
        grid_spec=pltpu.PrefetchScalarGridSpec(
            num_scalar_prefetch=1, grid=(1,), in_specs=specs,
            out_specs=[pl.BlockSpec(shape, lambda g, tie: (0, 0)) for shape in shapes]),
        out_shape=[jax.ShapeDtypeStruct(shape, BF) for shape in shapes],
        name="pick")(tie_map, *(arrays * LAYERS), ga, sa, qb, vb, mb, gf, sf, sb)
    return [outs[4 * i : 4 * i + 4] for i in range(LAYERS)]


def use_heads(heads, width, ways):
    count = lax.axis_size(AX)
    turned = heads[:, 3 * width : 3 * width + 8 + ways].T.astype(F32)
    wide = turned[8:].reshape(ways, count, width // count).transpose(1, 0, 2).reshape(1, -1)
    vecs = turned[:8]
    return dict(vecs=vecs, ga=vecs[0], sa=vecs[1], mb=vecs[4], gf=vecs[5], sf=vecs[6], eb=wide, heads=heads)


def forward_use(hidden, w, first_len, host, spare_host):
    q, k, v, normed, attended, lse, *more = attend_fwd(hidden, w, first_len, host)
    more = host.results(more)
    w.update(expand=more[0], shrink=more[1], mix=more[-1])
    hidden = hidden.astype(F32)
    middle = hidden + jnp.dot(attended, w["mix"], preferred_element_type=F32) + w["mb"]
    normed_two = layer_norm(middle, w["gf"], w["sf"]).astype(BF)
    result, activated, slope, *spare = feed_fwd(normed_two, w, middle, spare_host)
    kept = (hidden, normed, (q, k, v), attended, lse, middle, normed_two, activated, slope)
    return result, kept, spare_host.results(spare)


def backward_use(grad_out, kept, w, first_len, carried, ident, spare_ident):
    hidden, normed, qkv, attended, lse, middle, normed_two, activated, slope = kept
    count = lax.axis_size(AX)
    grad_low = grad_out.astype(BF)
    sb = column_sums(grad_low)
    spare = Host(Scatter, carried, spare_ident, FEED_BACKWARD_SLOTS, per=4, axis=0, pieces=2, window=2)
    dc, expand_term, shrink_term, eb, *carried = feed_bwd(grad_low, activated, slope, normed_two, w, spare)
    carried = spare.results(carried)
    eb = eb[0]
    unused, norm_back = jax.vjp(layer_norm, middle, w["gf"], w["sf"])
    middle_norm, gf, sf = norm_back(dc)
    dm = grad_out + middle_norm
    dmb = dm.astype(BF)
    mix_term = inner_rows(attended, dmb).astype(BF)
    mb = column_sums(dmb)
    do = times_transposed(dmb, w["mix"]).astype(BF)
    host = Host(Scatter, [shrink_term, mix_term, expand_term], ident, BACKWARD_SLOTS, per=4,
                pieces=8, window=3)
    heads_terms, da, qb, vb, more = attend_bwd(*qkv, do, lse, normed, w, first_len, host)
    more = host.results(more)
    unused, first_back = jax.vjp(layer_norm, hidden, w["ga"], w["sa"])
    hidden_norm, ga, sa = first_back(da)
    small = pack_columns([ga, sa, qb, vb, mb, gf, sf, sb], eb, count)
    return dm + hidden_norm, more, heads_terms, small, carried


def as_shares(shrink, mix, expand, heads, small):
    heads = jnp.concatenate(heads, axis=1)
    vecs, wide = unpack_columns(small, 8, shrink.shape[0] // mix.shape[0], 1)
    ga, sa, qb, vb, mb, gf, sf, sb = vecs
    return ga, sa, heads, qb, vb, mix, mb, gf, sf, expand, wide, shrink, sb


FORWARD_SLOTS = [1.6, 0.86, 1.29, 1.72] * 6
BACKWARD_SLOTS = [1.8, 1.35, 0.9, 2.9] * 6
FEED_FORWARD_SLOTS = [0.95, 0.95, 0.95, 0.95] * 6
FEED_BACKWARD_SLOTS = [0.7, 0.7, 0.7, 2.3] * 6


def place_terms(sources, shares):
    ids = lax.iota(jnp.int32, UNIQUE)
    out = []
    for items in zip(*shares):
        total = 0.0
        for source, item in zip(sources, items):
            chosen = (ids == source).reshape((UNIQUE,) + (1,) * item.ndim)
            total = total + jnp.where(chosen, item[None], 0.0)
        out.append(total)
    return out


def body(tokens, cotangent, tie_map, first_length, *stacks):
    hidden = tokens
    width = hidden.shape[1]
    sources = [tie_map[i] for i in range(LAYERS)]
    shards = pick_shards(tie_map, stacks)
    ways = shards[0][3].shape[0] // shards[0][0].shape[0]
    (heads,) = exchange(Gather, shards[0][:1], 0, "gather", 4)
    kept, weights = [], []
    for i in range(LAYERS):
        weights.append(use_heads(heads, width, ways))
        host = Host(Gather, shards[i][2:] + shards[i][1:2], 1 + i, FORWARD_SLOTS, per=4, pieces=4, window=12)
        later = shards[i + 1][:1] if i + 1 < LAYERS else []
        spare_host = Host(Gather, later, 6, FEED_FORWARD_SLOTS, per=4, axis=0, pieces=5, window=4)
        hidden, saved, spare = forward_use(hidden, weights[i], first_length, host, spare_host)
        heads = spare[0] if spare else None
        kept.append(saved)
    grad = cotangent.astype(F32)
    grad, late, heads_late, small_late, unused = backward_use(
        grad, kept[1], weights[1], first_length, [], 3, None)
    grad, early, heads_early, small_early, heads_late = backward_use(
        grad, kept[0], weights[0], first_length, heads_late, 4, 7)
    *heads_early, small = exchange(
        Scatter, heads_early + [jnp.concatenate([small_early, small_late], axis=1)], 5, "scatter", 3)
    shares = [as_shares(*early, heads_early, small[:, :LANES]),
              as_shares(*late, heads_late, small[:, LANES:])]
    return (hidden.astype(BF), grad.astype(BF), *place_terms(sources, shares))


def solution(mesh):
    rows = P(AX, None)
    flat = P(None, AX)
    deep = P(None, AX, None)
    weights = (flat, flat, deep, flat, flat, deep, flat, flat, flat, deep, flat, deep, flat)
    return jax.shard_map(
        body,
        mesh=mesh,
        in_specs=(rows, rows, P(), P(AX)) + weights,
        out_specs=(rows, rows) + weights,
        check_vma=False,
    )
```
